32 devices in a mesh: req: 2 (over core), ctx: 16 (over z, y, x).
Axes of the slice: x: 2, y: 2, z: 4, core: 2. Of those that a mesh axis runs over, the one named last changes fastest.
Arguments:
- queries: bfloat16 [32, 8192], P(('req', 'ctx')), parts along dimension 0, may hold values from -256 to 256
- new_kv: bfloat16 [32, 2, 1024], P(('req', 'ctx')), parts along dimension 0, may hold values from -12 to 12
- prefix_kv: bfloat16 [2, 16384, 2, 1024], P('req', 'ctx'), parts along dimension 0, may hold values from -4.5 to 4.5
- pool: bfloat16 [256, 16, 2, 1024], P(('req', 'ctx')), parts along dimension 0, may hold values from -12 to 12
- out_weight: bfloat16 [8192, 8192], P('ctx'), may hold values from -0.0625 to 0.0625
- parents: int32 [32], P('req'), parts along dimension 0, may hold values from 0 to 15, as said below
- tail_table: int32 [32, 4], P('req'), parts along dimension 0, may hold values from 0 to 127, as said below
- fresh_slots: int32 [32], P('req'), parts along dimension 0, may hold values from 0 to 127, as said below
- tail_lengths: int32 [32], P('req'), parts along dimension 0, may hold values from 1 to 63
Outputs:
- attn_out: float32 [32, 8192], P(('req', 'ctx')), parts along dimension 0
- new_pool: bfloat16 [256, 16, 2, 1024], P(('req', 'ctx')), parts along dimension 0
The draws below stay inside these ranges and needn't reach their ends.
There are 2 independent parts, one for each index of `req`. The reference program is written for one: setup_inputs(seed, part) draws one part's arguments, and reference() takes and returns one part's arrays. A program takes and returns all parts, laid end to end along the dimension named above; an argument that names none is the same for every part. Nothing has to cross between parts.
Inputs may be any that keep to these rules, and one draw needn't show every extreme that they name: `parents`: row i's parent is a beam of the same request, from 16 * (i // 16) to that plus 16 - 1. `tail_table`: all entries are distinct pool blocks, none among the last 2 blocks of a device's 8. Distinct pool blocks; fresh_slots[i] is one of the last 2 blocks of the device that holds beam row i, that is of device i.
All inputs are finite; a program needn't handle non-finite values.
Results may differ from the reference program's by a relative error of at most 0.0055.
Values may be sent and summed in bfloat16 or wider, within the bound.
No kernel may reach another device: no remote copies, remote signals or barrier semaphores. Data moves between devices by JAX's collectives and lax.ppermute only.
A program may use at most 384 MiB of HBM per device.

```python
import jax
import jax.numpy as jnp
from jax import lax

D = 8192
HQ = 64
KVH = 8
HD = 128
BEAMS = 16
BLOCK = 16
TB = 4
CAP = 2
POOL_DEV = 8
ROW_DEV = 1
ROWS = 16
REQS = 1
PREFIX = 16384
NBLK = 128
QW = 8192
KVW = 1024


def attention_inputs(key):
    seeded = jax.random.fold_in(key, 7)
    subkeys = jax.random.split(seeded, 2)
    queries = jax.random.truncated_normal(subkeys[0], -4.5, 4.5, (ROWS, QW), jnp.float32)
    prefix = jax.random.truncated_normal(subkeys[1], -4.5, 4.5, (REQS, PREFIX, 2, KVW), jnp.float32)
    return (queries, prefix)


def draw_queries(key, part):
    return attention_inputs(key)[0].astype(jnp.bfloat16)


def draw_prefix_kv(key, part):
    return attention_inputs(key)[1].astype(jnp.bfloat16)


def draw_parents(key, part):
    seeded = jax.random.fold_in(key, 3)
    former_key, latter_key = jax.random.split(seeded)
    first_pick = jax.random.randint(former_key, (ROWS,), 0, BEAMS)
    second_pick = jax.random.randint(latter_key, (ROWS,), 0, BEAMS)
    row_ids = jnp.arange(ROWS, dtype=jnp.int32)
    request_base = row_ids // BEAMS * BEAMS
    within = row_ids % BEAMS
    picked = jnp.minimum(first_pick, second_pick)
    picked = jnp.where(within == 0, BEAMS - 1, jnp.where(within == 1, 0, picked))
    return (request_base + picked).astype(jnp.int32)


def slot_plan(key):
    seeded = jax.random.fold_in(key, 11)
    subkeys = jax.random.split(seeded, 2)
    device_count = NBLK // POOL_DEV
    old_per = POOL_DEV - CAP
    ordering = jax.random.permutation(subkeys[0], device_count * old_per)[:ROWS * TB]
    old_slots = ordering // old_per * POOL_DEV + ordering % old_per
    table = old_slots.reshape(ROWS, TB)
    row_ids = jnp.arange(ROWS, dtype=jnp.int32)
    home = row_ids // ROW_DEV
    rotation = jax.random.randint(subkeys[1], (device_count,), 0, CAP)
    place = (rotation[home] + row_ids % ROW_DEV) % CAP
    fresh = home * POOL_DEV + old_per + place
    return (table.astype(jnp.int32), fresh.astype(jnp.int32))


def draw_tail_table(key, part):
    return slot_plan(key)[0]


def draw_fresh_slots(key, part):
    return slot_plan(key)[1]


def with_ends(drawn, key, low, largest):
    spot = [jax.random.randint(jax.random.fold_in(key, axis), (), 0, length) for axis, length in enumerate(drawn.shape)]
    widest = drawn.shape.index(max(drawn.shape))
    neighbour = spot[:widest] + [(spot[widest] + 1) % drawn.shape[widest]] + spot[widest + 1:]
    return drawn.at[tuple(spot)].set(low).at[tuple(neighbour)].set(largest)


def steps_of(rng, dims, pieces, smallest, largest):
    gain = 1.0
    for axis_at, shards_of in pieces:
        steps = jax.random.uniform(jax.random.fold_in(jax.random.fold_in(rng, 6), axis_at), (shards_of,), jnp.float32, smallest / len(pieces), largest / len(pieces))
        gain = gain * jnp.repeat(jnp.exp(steps), dims[axis_at] // shards_of).reshape((-1,) + (1,) * (len(dims) - 1 - axis_at))
    return gain


def normal_values(stream_key, shape, width, most, shards=(), held_as=jnp.bfloat16):
    result = jax.random.normal(stream_key, shape, jnp.float32) * width
    if len(shards) > 0:
        result = steps_of(stream_key, shape, shards, -0.22, 0.18) * result
    return jnp.clip(result, min=-most, max=most).astype(held_as)


def setup_inputs(seed: int = 0, part: int = 0) -> dict:
    key_list = jax.random.split(jax.random.key(seed), 10)
    own_keys = jax.random.split(jax.random.fold_in(key_list[9], part), 10)
    return {
        "queries": draw_queries(jax.random.fold_in(jax.random.fold_in(key_list[9], part), 71), part),
        "new_kv": normal_values(own_keys[1], (ROWS, 2, KVW), 3.0, 12.0, ((0, 16),)),
        "prefix_kv": draw_prefix_kv(jax.random.fold_in(jax.random.fold_in(key_list[9], part), 71), part),
        "pool": normal_values(own_keys[3], (NBLK, BLOCK, 2, KVW), 3.0, 12.0, ((0, 16),)),
        "out_weight": normal_values(key_list[4], (QW, D), QW ** -0.5, 0.0625, ((0, 16),)),
        "parents": draw_parents(jax.random.fold_in(jax.random.fold_in(key_list[9], part), 71), part),
        "tail_table": draw_tail_table(jax.random.fold_in(jax.random.fold_in(key_list[9], part), 71), part),
        "fresh_slots": draw_fresh_slots(jax.random.fold_in(jax.random.fold_in(key_list[9], part), 71), part),
        "tail_lengths": with_ends(jax.random.randint(own_keys[8], (ROWS,), 1, TB * BLOCK), jax.random.fold_in(own_keys[8], 1), 1, (TB * BLOCK) - 1).astype(jnp.int32),
    }


masked_score = -1.0e30


def narrow(values):
    return lax.optimization_barrier(values.astype(jnp.bfloat16)).astype(jnp.float32)


def reference(queries, new_kv, prefix_kv, pool, out_weight, parents, tail_table, fresh_slots, tail_lengths):
    groups = HQ // KVH
    scaling = HD ** -0.5
    tail_len = TB * BLOCK
    highest_mode = lax.Precision.HIGHEST
    parent_len = tail_lengths[parents]
    parent_table = tail_table[parents]
    tail_blocks = pool[parent_table.reshape(-1)].reshape(ROWS, tail_len, 2, KVW)
    position = jnp.arange(tail_len, dtype=jnp.int32)
    live_mask = position[None, :] < parent_len[:, None]
    query_grid = queries.astype(jnp.float32).reshape(ROWS, KVH, groups, HD)
    tail_keys = tail_blocks[:, :, 0].astype(jnp.float32).reshape(ROWS, tail_len, KVH, HD)
    tail_vals = tail_blocks[:, :, 1].astype(jnp.float32).reshape(ROWS, tail_len, KVH, HD)
    tail_score = jnp.einsum("ikgd,itkd->ikgt", query_grid, tail_keys, precision=highest_mode) * scaling
    tail_score = jnp.where(live_mask[:, None, None, :], tail_score, masked_score)
    new_keys = new_kv[:, 0].astype(jnp.float32).reshape(ROWS, KVH, HD)
    new_vals = new_kv[:, 1].astype(jnp.float32).reshape(ROWS, KVH, HD)
    new_score = jnp.einsum("ikgd,ikd->ikg", query_grid, new_keys, precision=highest_mode) * scaling

    def one_request(inputs):
        req_query, req_prefix, req_tail_score, req_tail_vals, req_new_score, req_new_vals = inputs
        pre_keys = req_prefix[:, 0].astype(jnp.float32).reshape(PREFIX, KVH, HD)
        pre_vals = req_prefix[:, 1].astype(jnp.float32).reshape(PREFIX, KVH, HD)
        pre_score = jnp.einsum("bkgd,pkd->bkgp", req_query, pre_keys, precision=highest_mode) * scaling
        highest = jnp.maximum(jnp.maximum(pre_score.max(-1), req_tail_score.max(-1)), req_new_score)
        pre_exp = jnp.exp(pre_score - highest[..., None])
        tail_exp = jnp.exp(req_tail_score - highest[..., None])
        new_exp = jnp.exp(req_new_score - highest)
        totals = pre_exp.sum(-1) + tail_exp.sum(-1) + new_exp
        output = jnp.einsum("bkgp,pkd->bkgd", narrow(pre_exp), pre_vals, precision=highest_mode)
        output = output + jnp.einsum("bkgt,btkd->bkgd", narrow(tail_exp), req_tail_vals, precision=highest_mode)
        output = output + narrow(new_exp)[..., None] * req_new_vals[:, :, None, :]
        return (output / totals[..., None]).astype(jnp.bfloat16).reshape(BEAMS, QW)

    attended = lax.map(one_request, (
        query_grid.reshape(REQS, BEAMS, KVH, groups, HD),
        prefix_kv,
        tail_score.reshape(REQS, BEAMS, KVH, groups, tail_len),
        tail_vals.reshape(REQS, BEAMS, tail_len, KVH, HD),
        new_score.reshape(REQS, BEAMS, KVH, groups),
        new_vals.reshape(REQS, BEAMS, KVH, HD)))
    attended = attended.reshape(ROWS, QW)
    attn_out = jnp.dot(attended, out_weight, preferred_element_type=jnp.float32)
    offset = parent_len % BLOCK
    source = jnp.take_along_axis(parent_table, (parent_len // BLOCK)[:, None], axis=1)[:, 0]
    slot_pos = jnp.arange(BLOCK, dtype=jnp.int32)
    keep_old = (slot_pos[None, :] < offset[:, None])[:, :, None, None]
    copied = jnp.where(keep_old, pool[source], jnp.zeros((), jnp.bfloat16))
    write_new = (slot_pos[None, :] == offset[:, None])[:, :, None, None]
    copied = jnp.where(write_new, new_kv[:, None], copied)
    new_pool = pool.at[fresh_slots].set(copied)
    return attn_out, new_pool
```

```python
import functools
import math

import jax
import jax.numpy as jnp
from jax import lax
from jax.experimental import pallas as pl
from jax.experimental.pallas import tpu as pltpu
from jax.sharding import PartitionSpec as P

HQ = 64
KVH = 8
HD = 128
CAP = 2

STAT_ROWS = 16
VMEM_LIMIT = 48 << 20
masked_score = -1e30
bf16 = jnp.bfloat16
f32 = jnp.float32


def split_kv(source, head, scratch, keys, values):
    tokens = source.shape[0]
    pairs = source[:, :, head * HD : (head + 1) * HD].astype(f32)
    scratch[: 2 * tokens, :] = pairs.reshape(2 * tokens, HD)
    keys[...] = scratch[pl.ds(0, tokens, stride=2), :].astype(bf16)
    values[...] = scratch[pl.ds(1, tokens, stride=2), :].astype(bf16)


def unpack_kernel(prefix, pool, new_kv, keys, values, tail_keys, tail_values, scratch):
    for head in range(KVH):
        split_kv(prefix.at[0], head, scratch.at[head], keys.at[0, head], values.at[0, head])

    @pl.when((pl.program_id(0) == 0) & (pl.program_id(1) == 0))
    def _():
        blocks, block_len = pool.shape[:2]
        tokens = blocks * block_len
        for head in range(KVH):
            for block in range(blocks):
                at = pl.ds(block * block_len, block_len)
                split_kv(
                    pool.at[block],
                    head,
                    scratch.at[head],
                    tail_keys.at[head, at],
                    tail_values.at[head, at],
                )
            rows = new_kv.shape[0]
            first = tokens - CAP * block_len
            at = pl.ds(first, CAP * block_len)
            lanes = slice(head * HD, (head + 1) * HD)
            slot = lax.broadcasted_iota(jnp.int32, (CAP * block_len, HD), 0)
            key = tail_keys[head, at, :]
            value = tail_values[head, at, :]
            for row in range(rows):
                key = jnp.where(slot == row, new_kv[row, 0:1, lanes], key)
                value = jnp.where(slot == row, new_kv[row, 1:2, lanes], value)
            tail_keys[head, at, :] = key
            tail_values[head, at, :] = value


def unpack(prefix_kv, pool, new_kv):
    requests, length, _, width = prefix_kv.shape
    blocks, block_len = pool.shape[:2]
    tokens = blocks * block_len
    step = min(256, length)
    whole = lambda shape: pl.BlockSpec(shape, lambda r, i: (0,) * len(shape))
    return pl.pallas_call(
        unpack_kernel,
        name="unpack",
        grid=(requests, length // step),
        in_specs=[
            pl.BlockSpec((1, step, 2, width), lambda r, i: (r, i, 0, 0)),
            whole(pool.shape),
            whole(new_kv.shape),
        ],
        out_specs=[pl.BlockSpec((1, KVH, step, HD), lambda r, i: (r, 0, i, 0))] * 2
        + [whole((KVH, tokens, HD))] * 2,
        out_shape=[jax.ShapeDtypeStruct((requests, KVH, length, HD), bf16)] * 2
        + [jax.ShapeDtypeStruct((KVH, tokens, HD), bf16)] * 2,
        scratch_shapes=[pltpu.VMEM((KVH, 2 * step, HD), f32)],
        compiler_params=pltpu.CompilerParams(vmem_limit_bytes=VMEM_LIMIT),
        cost_estimate=pl.CostEstimate(
            flops=0, bytes_accessed=4 * prefix_kv.size, transcendentals=0
        ),
    )(prefix_kv, pool, new_kv)


def pieces(value):
    high = value.astype(bf16)
    rest = value - high.astype(f32)
    middle = rest.astype(bf16)
    low = (rest - middle.astype(f32)).astype(bf16)
    return high.astype(f32), middle.astype(f32), low.astype(f32)


def attend_kernel(query, keys, values, tail_keys, tail_values, bias, out):
    groups = HQ // KVH
    targets = out.shape[0]
    beams = query.shape[0]
    count = groups * beams
    share = count // targets
    factor = HD ** (-0.5) * math.log2(math.e)
    stacked = jnp.concatenate([query[:, j * HD : (j + 1) * HD] for j in range(groups)], axis=0)
    contract = (((1,), (1,)), ((), ()))
    score = lax.dot_general(stacked, keys[0, 0], contract, preferred_element_type=f32)
    tail = lax.dot_general(stacked, tail_keys[0], contract, preferred_element_type=f32)
    tail = tail + jnp.concatenate([bias[0]] * groups, axis=0)
    top = jnp.maximum(
        jnp.max(score, axis=1, keepdims=True), jnp.max(tail, axis=1, keepdims=True)
    )
    weight = jnp.exp2((score - top) * factor)
    tail_weight = jnp.exp2((tail - top) * factor)
    total = jnp.sum(weight, axis=1, keepdims=True) + jnp.sum(tail_weight, axis=1, keepdims=True)
    result = jnp.dot(weight.astype(bf16), values[0, 0], preferred_element_type=f32)
    result = result + jnp.dot(
        tail_weight.astype(bf16), tail_values[0], preferred_element_type=f32
    )
    lane = lax.broadcasted_iota(jnp.int32, (count, HD), 1)
    packed = jnp.zeros((count, HD), f32)
    for at, term in enumerate(pieces(top) + pieces(total)):
        packed = jnp.where(lane == at, term, packed)
    stats = jnp.concatenate(
        [packed[t * share : (t + 1) * share] for t in range(targets)]
        + [jnp.zeros((HD - count, HD), f32)] * (count < HD),
        axis=0,
    )
    stats = stats.T
    for t in range(targets):
        out[t, 0, :share, :] = result[t * share : (t + 1) * share].astype(bf16)
        mine = stats if t == 0 else pltpu.roll(stats, HD - t * share, 1)
        out[t, 0, share : share + STAT_ROWS, :] = mine[:STAT_ROWS].astype(bf16)


def attend(everyone, keys, values, tail_keys, tail_values, bias, devices):
    requests, _, length, _ = keys.shape
    tokens = tail_keys.shape[1]
    beams = everyone.shape[0] // requests
    groups = HQ // KVH
    targets = devices // KVH
    rows = groups // targets * beams + STAT_ROWS
    return pl.pallas_call(
        attend_kernel,
        name="attend",
        grid=(requests, KVH),
        in_specs=[
            pl.BlockSpec((beams, groups * HD), lambda r, g: (r, g)),
            pl.BlockSpec((1, 1, length, HD), lambda r, g: (r, g, 0, 0)),
            pl.BlockSpec((1, 1, length, HD), lambda r, g: (r, g, 0, 0)),
            pl.BlockSpec((1, tokens, HD), lambda r, g: (g, 0, 0)),
            pl.BlockSpec((1, tokens, HD), lambda r, g: (g, 0, 0)),
            pl.BlockSpec((1, beams, tokens), lambda r, g: (r, 0, 0)),
        ],
        out_specs=pl.BlockSpec((targets, 1, rows, HD), lambda r, g: (g, r, 0, 0)),
        out_shape=jax.ShapeDtypeStruct((devices, requests, rows, HD), bf16),
        compiler_params=pltpu.CompilerParams(vmem_limit_bytes=VMEM_LIMIT),
        cost_estimate=pl.CostEstimate(
            flops=4 * everyone.size * length,
            bytes_accessed=4 * keys.size,
            transcendentals=everyone.size * length // HD,
        ),
    )(everyone, keys, values, tail_keys, tail_values, bias)


def project_kernel(partial, weight, out, attended, scratch):
    devices, requests, rows, _ = partial.shape
    share = rows - STAT_ROWS
    beams = out.shape[0] // requests
    own = share // beams
    factor = HD ** (-0.5) * math.log2(math.e)

    @pl.when(pl.program_id(0) == 0)
    def _():
        for r in range(requests):
            stats = [partial[p, r, share:rows, :].astype(f32) for p in range(devices)]
            tops = jnp.concatenate([s[0:1] + s[1:2] + s[2:3] for s in stats], axis=0)
            sums = jnp.concatenate([s[3:4] + s[4:5] + s[5:6] for s in stats], axis=0)
            scale = jnp.exp2((tops - jnp.max(tops, axis=0, keepdims=True)) * factor)
            scale = scale / jnp.sum(scale * sums, axis=0, keepdims=True)
            if devices < HD:
                scale = jnp.concatenate([scale, jnp.zeros((HD - devices, HD), f32)], axis=0)
            scale = scale.T
            total = jnp.zeros((share, HD), f32)
            for p in range(devices):
                total = total + partial[p, r, :share, :].astype(f32) * scale[:share, p : p + 1]
            for h in range(own):
                attended[r * beams : (r + 1) * beams, h * HD : (h + 1) * HD] = total[
                    h * beams : (h + 1) * beams
                ].astype(bf16)

    product = jnp.dot(attended[...], weight[...], preferred_element_type=f32)
    row_total = out.shape[0]
    chunks = weight.shape[1] // HD
    for c in range(chunks):
        scratch[pl.ds(c, row_total, stride=chunks), :] = product[:, c * HD : (c + 1) * HD]
    for row in range(row_total):
        out[row] = scratch[row * chunks : (row + 1) * chunks, :].astype(bf16)


def project(partial, weight, row_total):
    devices, requests, rows, _ = partial.shape
    depth, width = weight.shape
    step = min(2048, width)
    chunks = step // HD
    return pl.pallas_call(
        project_kernel,
        name="project",
        grid=(width // step,),
        in_specs=[
            pl.BlockSpec(partial.shape, lambda n: (0, 0, 0, 0)),
            pl.BlockSpec((depth, step), lambda n: (0, n)),
        ],
        out_specs=pl.BlockSpec((row_total, chunks, HD), lambda n: (0, n, 0)),
        out_shape=jax.ShapeDtypeStruct((row_total, width // HD, HD), bf16),
        scratch_shapes=[
            pltpu.VMEM((row_total, depth), bf16),
            pltpu.VMEM((row_total * chunks, HD), f32),
        ],
        compiler_params=pltpu.CompilerParams(vmem_limit_bytes=VMEM_LIMIT),
        cost_estimate=pl.CostEstimate(
            flops=2 * row_total * depth * width, bytes_accessed=2 * weight.size, transcendentals=0
        ),
    )(partial, weight)


def exchange(array):
    return lax.all_to_all(array, "ctx", split_axis=0, concat_axis=0, tiled=True)


def local(
    queries, new_kv, prefix_kv, pool, out_weight, parents, tail_table, fresh_slots, tail_lengths
):
    devices = lax.axis_size("ctx")
    my_index = lax.axis_index("ctx")
    local_rows = queries.shape[0]
    row_total = local_rows * devices
    pool_dev, block_len, _, kv_width = pool.shape
    requests = prefix_kv.shape[0]
    table_depth = tail_table.shape[1]
    beams = row_total // requests
    old_dev = pool_dev - CAP
    tokens = pool_dev * block_len

    width = queries.shape[1]
    outgoing = jnp.broadcast_to(queries[None], (devices, local_rows, width))
    everyone = exchange(outgoing).reshape(row_total, width)

    token_parts = min(devices, block_len)
    width_parts = devices // token_parts
    piece = (block_len // token_parts, 2, kv_width // width_parts)
    spread = pool[:old_dev].reshape(
        old_dev, token_parts, piece[0], 2, width_parts, piece[2]
    ).transpose(1, 4, 0, 2, 3, 5)
    spread = exchange(spread.reshape((devices, old_dev) + piece))

    keys, values, tail_keys, tail_values = unpack(prefix_kv, pool, new_kv)

    parent_len = tail_lengths[parents]
    parent_table = tail_table[parents]
    offset = parent_len % block_len
    source = jnp.take_along_axis(parent_table, (parent_len // block_len)[:, None], axis=1)[:, 0]
    slot = lax.broadcasted_iota(jnp.int32, (1, 1, pool_dev), 2) + my_index * pool_dev
    depth = lax.broadcasted_iota(jnp.int32, (1, table_depth, 1), 1)
    matches = parent_table[:, :, None] == slot
    reach = jnp.sum(
        jnp.where(matches, parent_len[:, None, None] - depth * block_len, 0), axis=1
    )
    position = jnp.arange(tokens, dtype=jnp.int32)
    live = position[None, :] % block_len < jnp.repeat(reach, block_len, axis=1)
    row_ids = jnp.arange(row_total, dtype=jnp.int32)
    own_slot = row_ids - my_index * local_rows
    own = (own_slot >= 0) & (own_slot < local_rows)
    live = live | (own[:, None] & (position[None, :] == old_dev * block_len + own_slot[:, None]))
    bias = jnp.where(live, 0.0, masked_score).astype(f32).reshape(requests, beams, tokens)

    partial = attend(everyone, keys, values, tail_keys, tail_values, bias, devices)
    partial = exchange(partial)

    picked = spread.reshape((devices * old_dev,) + piece)[
        source // pool_dev * old_dev + source % pool_dev
    ]
    block = exchange(picked.reshape((devices, local_rows) + piece))

    products = exchange(project(partial, out_weight, row_total).reshape(
        devices, local_rows * (out_weight.shape[1] // HD), HD
    ))
    result = jnp.sum(products.astype(f32), axis=0).reshape(local_rows, out_weight.shape[1])

    block = block.reshape((token_parts, width_parts, local_rows) + piece)
    block = block.transpose(2, 0, 3, 4, 1, 5).reshape(local_rows, block_len, 2, kv_width)
    own_offset = lax.dynamic_slice_in_dim(offset, my_index * local_rows, local_rows)
    own_fresh = lax.dynamic_slice_in_dim(fresh_slots, my_index * local_rows, local_rows)
    at = jnp.arange(block_len, dtype=jnp.int32)[None, :, None, None]
    limit = own_offset[:, None, None, None]
    copied = jnp.where(
        at < limit, block, jnp.where(at == limit, new_kv[:, None], jnp.zeros((), bf16))
    )
    new_pool = pool
    for row in range(local_rows):
        new_pool = lax.dynamic_update_slice_in_dim(
            new_pool, copied[row : row + 1], own_fresh[row] - my_index * pool_dev, 0
        )
    return (result, new_pool)


def solution(mesh):
    in_specs = (
        P(("req", "ctx"), None),
        P(("req", "ctx"), None, None),
        P("req", "ctx", None, None),
        P(("req", "ctx"), None, None, None),
        P("ctx", None),
        P("req"),
        P("req", None),
        P("req"),
        P("req"),
    )
    out_specs = (P(("req", "ctx"), None), P(("req", "ctx"), None, None, None))
    return jax.shard_map(local, mesh=mesh, in_specs=in_specs, out_specs=out_specs, check_vma=False)
```

```python
import functools
import math

import jax
import jax.numpy as jnp
from jax import lax
from jax.experimental import pallas as pl
from jax.experimental.pallas import tpu as pltpu
from jax.sharding import PartitionSpec as P

HQ = 64
KVH = 8
HD = 128
CAP = 2

STAT_ROWS = 16
VMEM_LIMIT = 20 << 20
masked_score = -1e30
bf16 = jnp.bfloat16
f32 = jnp.float32


def broadcast_kernel(query, out, scratch):
    devices, rows = out.shape[:2]
    heads = query.shape[1] // HD
    for row in range(rows):
        for head in range(heads):
            scratch[head : head + 1, :] = query[row : row + 1, head * HD : (head + 1) * HD].astype(
                f32
            )
        value = scratch[...].astype(bf16)
        for device in range(devices):
            out[device, row] = value


def broadcast(queries, devices):
    rows, width = queries.shape
    return pl.pallas_call(
        broadcast_kernel,
        name="broadcast",
        in_specs=[pl.BlockSpec(memory_space=pltpu.VMEM)],
        out_specs=pl.BlockSpec(memory_space=pltpu.VMEM),
        out_shape=jax.ShapeDtypeStruct((devices, rows, width // HD, HD), bf16),
        scratch_shapes=[pltpu.VMEM((width // HD, HD), f32)],
    )(queries)


def source_of(row, parents, table, lengths, block_len):
    parent = parents[row]
    length = lengths[parent]
    return length, table[parent, length // block_len]


def place_of(stage, source, mine, pool_dev):
    return (source // pool_dev ^ mine) & ((1 << stage) - 1)


def fetch_block(stage, me, source, dest, part, rows, pool, arrived, target, sem):
    pool_dev = pool.shape[0]
    place = place_of(stage, source, me, pool_dev)

    @pl.when(place == 0)
    def _():
        pltpu.make_async_copy(pool.at[source % pool_dev], target, sem).start()

    for bit in range(stage):

        @pl.when((place >> bit) == 1)
        def _():
            at = (dest >> (bit + 1)) * rows + part
            pltpu.make_async_copy(arrived[bit].at[at], target, sem).start()


def pick_kernel(stage, rows, me_ref, parents, table, lengths, pool, *refs):
    arrived, (out, sem) = refs[:stage], refs[stage:]
    me = me_ref[0]
    count = out.shape[0]
    flipped = me & ((1 << (stage + 1)) - 1) ^ (1 << stage)

    def begin(at, carry):
        dest = (at // rows << (stage + 1)) | flipped
        part = at % rows
        _, source = source_of(dest * rows + part, parents, table, lengths, pool.shape[1])
        fetch_block(stage, me, source, dest, part, rows, pool, arrived, out.at[at], sem.at[at])
        return carry

    def finish(at, carry):
        pltpu.make_async_copy(pool.at[0], out.at[at], sem.at[at]).wait()
        return carry

    lax.fori_loop(0, count, begin, 0)
    lax.fori_loop(0, count, finish, 0)


def pick(stage, devices, rows, meta, pool, arrived):
    count = (devices >> (stage + 1)) * rows
    block = pool.shape[1:]
    smem = pl.BlockSpec(memory_space=pltpu.SMEM)
    return pl.pallas_call(
        functools.partial(pick_kernel, stage, rows),
        name=f"pick{stage}",
        in_specs=[smem] * 4 + [pl.BlockSpec(memory_space=pl.ANY)] * (1 + stage),
        out_specs=pl.BlockSpec(memory_space=pltpu.VMEM),
        out_shape=jax.ShapeDtypeStruct((count,) + block, bf16),
        scratch_shapes=[pltpu.SemaphoreType.DMA((count,))],
        compiler_params=pltpu.CompilerParams(vmem_limit_bytes=VMEM_LIMIT),
        cost_estimate=pl.CostEstimate(
            flops=0, bytes_accessed=4 * count * math.prod(block), transcendentals=0
        ),
    )(*meta, pool, *arrived)


def place_kernel(stages, rows, me_ref, parents, table, lengths, fresh, new_kv, pool, *refs):
    arrived, (out, sem) = refs[:stages], refs[stages:]
    me = me_ref[0]
    pool_dev, block_len = pool.shape[:2]
    whole = pltpu.make_async_copy(pool, out, sem)
    whole.start()
    whole.wait()
    for part in range(rows):
        row = me * rows + part
        length, source = source_of(row, parents, table, lengths, block_len)
        slot = fresh[row] - me * pool_dev
        fetch_block(stages, me, source, me, part, rows, pool, arrived, out.at[slot], sem)
        pltpu.make_async_copy(pool.at[0], out.at[slot], sem).wait()
        offset = length % block_len

        def token(at, carry):
            @pl.when(at == offset)
            def _():
                out[slot, at] = new_kv[part]

            @pl.when(at > offset)
            def _():
                out[slot, at] = jnp.zeros(out.shape[2:], bf16)

            return carry

        lax.fori_loop(0, block_len, token, 0)


def place(stages, rows, meta, fresh, new_kv, pool, arrived):
    smem = pl.BlockSpec(memory_space=pltpu.SMEM)
    return pl.pallas_call(
        functools.partial(place_kernel, stages, rows),
        name="place",
        in_specs=[smem] * 5
        + [pl.BlockSpec(memory_space=pltpu.VMEM)]
        + [pl.BlockSpec(memory_space=pl.ANY)] * (1 + stages),
        out_specs=pl.BlockSpec(memory_space=pltpu.VMEM),
        out_shape=jax.ShapeDtypeStruct(pool.shape, bf16),
        scratch_shapes=[pltpu.SemaphoreType.DMA],
        compiler_params=pltpu.CompilerParams(vmem_limit_bytes=VMEM_LIMIT),
        cost_estimate=pl.CostEstimate(flops=0, bytes_accessed=4 * pool.size, transcendentals=0),
    )(*meta, fresh, new_kv, pool, *arrived)


def split_kv(source, head, scratch, keys, values):
    tokens = source.shape[0]
    pairs = source[:, :, head * HD : (head + 1) * HD].astype(f32)
    scratch[: 2 * tokens, :] = pairs.reshape(2 * tokens, HD)
    keys[...] = scratch[pl.ds(0, tokens, stride=2), :].astype(bf16)
    values[...] = scratch[pl.ds(1, tokens, stride=2), :].astype(bf16)


def unpack_kernel(
    me_ref,
    parents,
    table,
    lengths,
    prefix,
    pool,
    new_kv,
    keys,
    values,
    tail_keys,
    tail_values,
    bias,
    scratch,
):
    for head in range(KVH):
        split_kv(prefix.at[0], head, scratch.at[head], keys.at[0, head], values.at[0, head])

    @pl.when((pl.program_id(0) == 0) & (pl.program_id(1) == 0))
    def _():
        me = me_ref[0]
        blocks, block_len = pool.shape[:2]
        tokens = blocks * block_len
        rows = new_kv.shape[0]
        first = tokens - CAP * block_len
        for head in range(KVH):
            for block in range(blocks):
                at = pl.ds(block * block_len, block_len)
                split_kv(
                    pool.at[block],
                    head,
                    scratch.at[head],
                    tail_keys.at[head, at],
                    tail_values.at[head, at],
                )
            at = pl.ds(first, CAP * block_len)
            lanes = slice(head * HD, (head + 1) * HD)
            slot = lax.broadcasted_iota(jnp.int32, (CAP * block_len, HD), 0)
            key = tail_keys[head, at, :]
            value = tail_values[head, at, :]
            for row in range(rows):
                key = jnp.where(slot == row, new_kv[row, 0:1, lanes], key)
                value = jnp.where(slot == row, new_kv[row, 1:2, lanes], value)
            tail_keys[head, at, :] = key
            tail_values[head, at, :] = value

        lane = lax.broadcasted_iota(jnp.int32, (1, tokens), 1)

        def mask(row, carry):
            parent = parents[row]
            length = lengths[parent]
            reach = jnp.zeros((1, tokens), jnp.int32)
            for depth in range(table.shape[1]):
                block = table[parent, depth] - me * blocks
                reach = jnp.where(lane // block_len == block, length - depth * block_len, reach)
            own = row - me * rows
            own = jnp.where((own >= 0) & (own < rows), own + first, -1)
            live = (lane % block_len < reach) | (lane == own)
            bias[pl.ds(row, 1), :] = jnp.where(live, 0.0, masked_score)
            return carry

        lax.fori_loop(0, bias.shape[0], mask, 0)


def unpack(meta, prefix_kv, pool, new_kv, row_total):
    requests, length, _, width = prefix_kv.shape
    blocks, block_len = pool.shape[:2]
    tokens = blocks * block_len
    step = min(256, length)
    smem = pl.BlockSpec(memory_space=pltpu.SMEM)
    whole = lambda shape: pl.BlockSpec(shape, lambda r, i: (0,) * len(shape))
    return pl.pallas_call(
        unpack_kernel,
        name="unpack",
        grid=(requests, length // step),
        in_specs=[smem] * 4
        + [
            pl.BlockSpec((1, step, 2, width), lambda r, i: (r, i, 0, 0)),
            whole(pool.shape),
            whole(new_kv.shape),
        ],
        out_specs=[pl.BlockSpec((1, KVH, step, HD), lambda r, i: (r, 0, i, 0))] * 2
        + [whole((KVH, tokens, HD))] * 2
        + [whole((row_total, tokens))],
        out_shape=[jax.ShapeDtypeStruct((requests, KVH, length, HD), bf16)] * 2
        + [jax.ShapeDtypeStruct((KVH, tokens, HD), bf16)] * 2
        + [jax.ShapeDtypeStruct((row_total, tokens), f32)],
        scratch_shapes=[pltpu.VMEM((KVH, 2 * step, HD), f32)],
        compiler_params=pltpu.CompilerParams(vmem_limit_bytes=VMEM_LIMIT),
        cost_estimate=pl.CostEstimate(
            flops=0, bytes_accessed=4 * prefix_kv.size, transcendentals=0
        ),
    )(*meta, prefix_kv, pool, new_kv)


def pieces(value):
    high = value.astype(bf16)
    rest = value - high.astype(f32)
    middle = rest.astype(bf16)
    low = (rest - middle.astype(f32)).astype(bf16)
    return high.astype(f32), middle.astype(f32), low.astype(f32)


def attend_kernel(query, keys, values, tail_keys, tail_values, bias, out, wide, stacks):
    groups = HQ // KVH
    targets = out.shape[0]
    beams = query.shape[0]
    count = groups * beams

    @pl.when(pl.program_id(1) == 0)
    def _():
        wide[...] = query[...].astype(f32).reshape(beams * HQ, HD)
        for head in range(HQ):
            stacks[head * beams : (head + 1) * beams, :] = wide[
                pl.ds(head, beams, stride=HQ), :
            ].astype(bf16)

    share = count // targets
    factor = HD ** (-0.5) * math.log2(math.e)
    stacked = stacks[pl.ds(pl.multiple_of(pl.program_id(1) * count, count), count), :]
    contract = (((1,), (1,)), ((), ()))
    score = lax.dot_general(stacked, keys[0, 0], contract, preferred_element_type=f32)
    tail = lax.dot_general(stacked, tail_keys[0], contract, preferred_element_type=f32)
    tail = tail + jnp.concatenate([bias[...]] * groups, axis=0)
    top = jnp.maximum(
        jnp.max(score, axis=1, keepdims=True), jnp.max(tail, axis=1, keepdims=True)
    )
    weight = jnp.exp2((score - top) * factor)
    tail_weight = jnp.exp2((tail - top) * factor)
    total = jnp.sum(weight, axis=1, keepdims=True) + jnp.sum(tail_weight, axis=1, keepdims=True)
    result = jnp.dot(weight.astype(bf16), values[0, 0], preferred_element_type=f32)
    result = result + jnp.dot(
        tail_weight.astype(bf16), tail_values[0], preferred_element_type=f32
    )
    lane = lax.broadcasted_iota(jnp.int32, (count, HD), 1)
    packed = jnp.zeros((count, HD), f32)
    for at, term in enumerate(pieces(top) + pieces(total)):
        packed = jnp.where(lane == at, term, packed)
    stats = jnp.concatenate(
        [packed[t * share : (t + 1) * share] for t in range(targets)]
        + [jnp.zeros((HD - count, HD), f32)] * (count < HD),
        axis=0,
    )
    stats = stats.T
    for t in range(targets):
        out[t, 0, :share, :] = result[t * share : (t + 1) * share].astype(bf16)
        mine = stats if t == 0 else pltpu.roll(stats, HD - t * share, 1)
        out[t, 0, share : share + STAT_ROWS, :] = mine[:STAT_ROWS].astype(bf16)


def attend(everyone, keys, values, tail_keys, tail_values, bias, devices):
    requests, _, length, _ = keys.shape
    tokens = tail_keys.shape[1]
    beams = everyone.shape[0] // requests
    groups = HQ // KVH
    targets = devices // KVH
    rows = groups // targets * beams + STAT_ROWS
    return pl.pallas_call(
        attend_kernel,
        name="attend",
        grid=(requests, KVH),
        in_specs=[
            pl.BlockSpec((beams, HQ, HD), lambda r, g: (r, 0, 0)),
            pl.BlockSpec((1, 1, length, HD), lambda r, g: (r, g, 0, 0)),
            pl.BlockSpec((1, 1, length, HD), lambda r, g: (r, g, 0, 0)),
            pl.BlockSpec((1, tokens, HD), lambda r, g: (g, 0, 0)),
            pl.BlockSpec((1, tokens, HD), lambda r, g: (g, 0, 0)),
            pl.BlockSpec((beams, tokens), lambda r, g: (r, 0)),
        ],
        out_specs=pl.BlockSpec((targets, 1, rows, HD), lambda r, g: (g, r, 0, 0)),
        out_shape=jax.ShapeDtypeStruct((devices, requests, rows, HD), bf16),
        scratch_shapes=[pltpu.VMEM((beams * HQ, HD), f32), pltpu.VMEM((beams * HQ, HD), bf16)],
        compiler_params=pltpu.CompilerParams(vmem_limit_bytes=VMEM_LIMIT),
        cost_estimate=pl.CostEstimate(
            flops=4 * everyone.size * length,
            bytes_accessed=4 * keys.size,
            transcendentals=everyone.size * length // HD,
        ),
    )(everyone, keys, values, tail_keys, tail_values, bias)


def project_kernel(partial, weight, out, attended, scratch):
    devices, requests, rows, _ = partial.shape
    share = rows - STAT_ROWS
    beams = out.shape[0] // requests
    own = share // beams
    factor = HD ** (-0.5) * math.log2(math.e)

    @pl.when(pl.program_id(0) == 0)
    def _():
        for r in range(requests):
            stats = [partial[p, r, share:rows, :].astype(f32) for p in range(devices)]
            tops = jnp.concatenate([s[0:1] + s[1:2] + s[2:3] for s in stats], axis=0)
            sums = jnp.concatenate([s[3:4] + s[4:5] + s[5:6] for s in stats], axis=0)
            scale = jnp.exp2((tops - jnp.max(tops, axis=0, keepdims=True)) * factor)
            scale = scale / jnp.sum(scale * sums, axis=0, keepdims=True)
            if devices < HD:
                scale = jnp.concatenate([scale, jnp.zeros((HD - devices, HD), f32)], axis=0)
            scale = scale.T
            total = jnp.zeros((share, HD), f32)
            for p in range(devices):
                total = total + partial[p, r, :share, :].astype(f32) * scale[:share, p : p + 1]
            for h in range(own):
                attended[r * beams : (r + 1) * beams, h * HD : (h + 1) * HD] = total[
                    h * beams : (h + 1) * beams
                ].astype(bf16)

    product = jnp.dot(attended[...], weight[...], preferred_element_type=f32)
    row_total = out.shape[0]
    chunks = weight.shape[1] // HD
    for c in range(chunks):
        scratch[pl.ds(c, row_total, stride=chunks), :] = product[:, c * HD : (c + 1) * HD]
    for row in range(row_total):
        out[row] = scratch[row * chunks : (row + 1) * chunks, :].astype(bf16)


def project(partial, weight, row_total):
    devices, requests, rows, _ = partial.shape
    depth, width = weight.shape
    step = min(2048, width)
    chunks = step // HD
    return pl.pallas_call(
        project_kernel,
        name="project",
        grid=(width // step,),
        in_specs=[
            pl.BlockSpec(partial.shape, lambda n: (0, 0, 0, 0)),
            pl.BlockSpec((depth, step), lambda n: (0, n)),
        ],
        out_specs=pl.BlockSpec((row_total, chunks, HD), lambda n: (0, n, 0)),
        out_shape=jax.ShapeDtypeStruct((row_total, width // HD, HD), bf16),
        scratch_shapes=[
            pltpu.VMEM((row_total, depth), bf16),
            pltpu.VMEM((row_total * chunks, HD), f32),
        ],
        compiler_params=pltpu.CompilerParams(vmem_limit_bytes=VMEM_LIMIT),
        cost_estimate=pl.CostEstimate(
            flops=2 * row_total * depth * width, bytes_accessed=2 * weight.size, transcendentals=0
        ),
    )(partial, weight)


def exchange(array):
    return lax.all_to_all(array, "ctx", split_axis=0, concat_axis=0, tiled=True)


def local(
    queries, new_kv, prefix_kv, pool, out_weight, parents, tail_table, fresh_slots, tail_lengths
):
    devices = lax.axis_size("ctx")
    rows = queries.shape[0]
    row_total = rows * devices
    width = out_weight.shape[1]
    stages = devices.bit_length() - 1
    meta = (lax.axis_index("ctx").reshape(1), parents, tail_table, tail_lengths)

    everyone = exchange(broadcast(queries, devices)).reshape(row_total, HQ, HD)
    keys, values, tail_keys, tail_values, bias = unpack(meta, prefix_kv, pool, new_kv, row_total)

    arrived = []
    for stage in range(stages):
        chosen = pick(stage, devices, rows, meta, pool, arrived)
        pairs = [(i, i ^ (1 << stage)) for i in range(devices)]
        arrived.append(lax.ppermute(chosen, "ctx", pairs))

    partial = exchange(attend(everyone, keys, values, tail_keys, tail_values, bias, devices))
    products = project(partial, out_weight, row_total)
    products = exchange(products.reshape(devices, rows * (width // HD), HD))
    result = jnp.sum(products.astype(f32), axis=0).reshape(rows, width)
    new_pool = place(stages, rows, meta, fresh_slots, new_kv, pool, arrived)
    return (result, new_pool)


def solution(mesh):
    in_specs = (
        P(("req", "ctx"), None),
        P(("req", "ctx"), None, None),
        P("req", "ctx", None, None),
        P(("req", "ctx"), None, None, None),
        P("ctx", None),
        P("req"),
        P("req", None),
        P("req"),
        P("req"),
    )
    out_specs = (P(("req", "ctx"), None), P(("req", "ctx"), None, None, None))
    return jax.shard_map(local, mesh=mesh, in_specs=in_specs, out_specs=out_specs, check_vma=False)
```

```python
import functools
import math

import jax
import jax.numpy as jnp
from jax import lax
from jax.experimental import pallas as pl
from jax.experimental.pallas import tpu as pltpu
from jax.sharding import PartitionSpec as P


HQ = 64
KVH = 8
HD = 128
CAP = 2

STAT_ROWS = 16
AT_ONCE = 2
VMEM_LIMIT = 20 << 20
masked_score = -1e30
bf16 = jnp.bfloat16
f32 = jnp.float32


def in_hbm(array):
    return pltpu.with_memory_space_constraint(array, pltpu.HBM)


def rounds_of(devices):
    total = devices.bit_length() - 1
    return [(bit, min(2, total - bit)) for bit in range(0, total, 2)]


def channels_of(rounds):
    return [(first, mask) for first, bits in rounds for mask in range(1, 1 << bits)]


def load_meta(sources, targets, sem):
    copies = [pltpu.make_async_copy(s, t, sem.at[i]) for i, (s, t) in enumerate(zip(sources, targets))]
    for copy in copies:
        copy.start()
    return copies


def meta_scratch(meta):
    return [pltpu.SMEM(m.shape, jnp.int32) for m in meta] + [pltpu.SemaphoreType.DMA((len(meta),))]


def source_of(row, parents, table, lengths, block_len):
    parent = parents[row]
    length = lengths[parent]
    return length, table[length // block_len, parent]


def fetch_block(rounds, me, source, dest, part, rows, pool, arrived, target, sem):
    pool_dev = pool.shape[0]
    done = sum(bits for _, bits in rounds)
    moved = (source // pool_dev ^ me) & ((1 << done) - 1)

    @pl.when(moved == 0)
    def _():
        pltpu.make_async_copy(pool.at[source % pool_dev], target, sem).start()

    for (first, mask), ref in zip(channels_of(rounds), arrived):
        bits = dict(rounds)[first]

        @pl.when((moved >> first) == mask)
        def _():
            at = (dest >> (first + bits)) * rows + part
            pltpu.make_async_copy(ref.at[at], target, sem).start()


def begin_picks(rounds, now, rows, me, meta, pool, arrived, outs, sem):
    first, bits = now
    for mask in range(1, 1 << bits):
        out = outs[mask - 1]
        low = (me & ((1 << (first + bits)) - 1)) ^ (mask << first)

        def begin(at, carry):
            dest = (at // rows << (first + bits)) | low
            part = at % rows
            _, source = source_of(dest * rows + part, *meta, pool.shape[1])
            fetch_block(
                rounds, me, source, dest, part, rows, pool, arrived, out.at[at], sem.at[mask - 1, at]
            )
            return carry

        lax.fori_loop(0, out.shape[0], begin, 0)


def end_picks(pool, outs, sem):
    for index, out in enumerate(outs):

        def finish(at, carry):
            pltpu.make_async_copy(pool.at[0], out.at[at], sem.at[index, at]).wait()
            return carry

        lax.fori_loop(0, out.shape[0], finish, 0)


def ask_kernel(now, query, parents_in, table_in, lengths_in, pool, out, *refs):
    devices, rows = out.shape[:2]
    partners = (1 << now[1]) - 1
    outs, (wide, parents, table, lengths, meta_sem, sem) = refs[:partners], refs[partners:]
    me = lax.axis_index("ctx")
    meta = (parents, table, lengths)
    copies = load_meta((parents_in, table_in, lengths_in), meta, meta_sem)
    heads = query.shape[1] // HD
    for row in range(rows):
        for head in range(heads):
            wide[row, head : head + 1, :] = query[
                row : row + 1, head * HD : (head + 1) * HD
            ].astype(f32)
    for copy in copies:
        copy.wait()
    begin_picks([], now, rows, me, meta, pool, [], outs, sem)
    for row in range(rows):
        value = wide[row].astype(bf16)
        for device in range(devices):
            out[device, row] = value
    end_picks(pool, outs, sem)


def pick_shapes(now, devices, rows, pool):
    first, bits = now
    count = (devices >> (first + bits)) * rows
    partners = (1 << bits) - 1
    return [jax.ShapeDtypeStruct((count,) + pool.shape[1:], bf16)] * partners, (partners, count)


def ask(now, devices, queries, meta, pool):
    rows, width = queries.shape
    heads = width // HD
    shapes, semaphores = pick_shapes(now, devices, rows, pool)
    vmem, hbm = pl.BlockSpec(memory_space=pltpu.VMEM), pl.BlockSpec(memory_space=pltpu.HBM)
    return pl.pallas_call(
        functools.partial(ask_kernel, now),
        name="ask",
        in_specs=[vmem] + [hbm] * 4,
        out_specs=[vmem] * (1 + len(shapes)),
        out_shape=[jax.ShapeDtypeStruct((devices, rows, heads, HD), bf16)] + shapes,
        scratch_shapes=[pltpu.VMEM((rows, heads, HD), f32)]
        + meta_scratch(meta)
        + [pltpu.SemaphoreType.DMA(semaphores)],
        compiler_params=pltpu.CompilerParams(vmem_limit_bytes=VMEM_LIMIT),
    )(queries, *map(in_hbm, meta), in_hbm(pool))


def pick_kernel(rounds, now, rows, channels, parents_in, table_in, lengths_in, pool, *refs):
    partners = (1 << now[1]) - 1
    arrived, refs = refs[:channels], refs[channels:]
    outs, (parents, table, lengths, meta_sem, sem) = refs[:partners], refs[partners:]
    meta = (parents, table, lengths)
    for copy in load_meta((parents_in, table_in, lengths_in), meta, meta_sem):
        copy.wait()
    begin_picks(rounds, now, rows, lax.axis_index("ctx"), meta, pool, arrived, outs, sem)
    end_picks(pool, outs, sem)


def pick(rounds, now, devices, rows, meta, pool, arrived):
    shapes, semaphores = pick_shapes(now, devices, rows, pool)
    vmem, hbm = pl.BlockSpec(memory_space=pltpu.VMEM), pl.BlockSpec(memory_space=pltpu.HBM)
    return pl.pallas_call(
        functools.partial(pick_kernel, rounds, now, rows, len(arrived)),
        name="pick",
        in_specs=[hbm] * 4 + [pl.BlockSpec(memory_space=pl.ANY)] * len(arrived),
        out_specs=[vmem] * len(shapes),
        out_shape=shapes,
        scratch_shapes=meta_scratch(meta) + [pltpu.SemaphoreType.DMA(semaphores)],
        compiler_params=pltpu.CompilerParams(vmem_limit_bytes=VMEM_LIMIT),
        cost_estimate=pl.CostEstimate(flops=0, bytes_accessed=1 << 22, transcendentals=0),
    )(*map(in_hbm, meta), in_hbm(pool), *arrived)


def place_kernel(rounds, rows, parents_in, table_in, lengths_in, fresh_in, new_kv, pool, *refs):
    channels = len(channels_of(rounds))
    arrived, (out, parents, table, lengths, fresh, meta_sem, sem) = refs[:channels], refs[channels:]
    me = lax.axis_index("ctx")
    pool_dev, block_len = pool.shape[:2]
    whole = pltpu.make_async_copy(pool, out, sem)
    whole.start()
    sources = (parents_in, table_in, lengths_in, fresh_in)
    for copy in load_meta(sources, (parents, table, lengths, fresh), meta_sem):
        copy.wait()
    whole.wait()
    for part in range(rows):
        row = me * rows + part
        length, source = source_of(row, parents, table, lengths, block_len)
        slot = fresh[row] - me * pool_dev
        fetch_block(rounds, me, source, me, part, rows, pool, arrived, out.at[slot], sem)
        pltpu.make_async_copy(pool.at[0], out.at[slot], sem).wait()
        offset = length % block_len

        def token(at, carry):
            @pl.when(at == offset)
            def _():
                out[slot, at] = new_kv[part]

            @pl.when(at > offset)
            def _():
                out[slot, at] = jnp.zeros(out.shape[2:], bf16)

            return carry

        lax.fori_loop(0, block_len, token, 0)


def place(rounds, rows, meta, new_kv, pool, arrived):
    vmem, hbm = pl.BlockSpec(memory_space=pltpu.VMEM), pl.BlockSpec(memory_space=pltpu.HBM)
    return pl.pallas_call(
        functools.partial(place_kernel, rounds, rows),
        name="place",
        in_specs=[hbm] * 4 + [vmem, hbm] + [pl.BlockSpec(memory_space=pl.ANY)] * len(arrived),
        out_specs=vmem,
        out_shape=jax.ShapeDtypeStruct(pool.shape, bf16),
        scratch_shapes=meta_scratch(meta) + [pltpu.SemaphoreType.DMA],
        compiler_params=pltpu.CompilerParams(vmem_limit_bytes=VMEM_LIMIT),
        cost_estimate=pl.CostEstimate(flops=0, bytes_accessed=4 * pool.size, transcendentals=0),
    )(*map(in_hbm, meta), new_kv, in_hbm(pool), *arrived)


def split_kv(source, head, scratch, keys, values):
    tokens = source.shape[0]
    pairs = source[:, :, head * HD : (head + 1) * HD].astype(f32)
    scratch[: 2 * tokens, :] = pairs.reshape(2 * tokens, HD)
    keys[...] = scratch[pl.ds(0, tokens, stride=2), :].astype(bf16)
    values[...] = scratch[pl.ds(1, tokens, stride=2), :].astype(bf16)


def unpack_kernel(
    parents_in,
    table_in,
    lengths_in,
    prefix,
    pool,
    new_kv,
    keys,
    values,
    tail_keys,
    tail_values,
    bias,
    scratch,
    parents,
    table,
    lengths,
    meta_sem,
):
    sources, meta = (parents_in, table_in, lengths_in), (parents, table, lengths)
    first_step = (pl.program_id(0) == 0) & (pl.program_id(1) == 0)

    @pl.when(first_step)
    def _():
        load_meta(sources, meta, meta_sem)

    for head in range(KVH):
        split_kv(prefix.at[0], head, scratch.at[head], keys.at[0, head], values.at[0, head])

    @pl.when(first_step)
    def _():
        for index, (from_ref, to_ref) in enumerate(zip(sources, meta)):
            pltpu.make_async_copy(from_ref, to_ref, meta_sem.at[index]).wait()
        me = lax.axis_index("ctx")
        blocks, block_len = pool.shape[:2]
        tokens = blocks * block_len
        rows = new_kv.shape[0]
        first = tokens - CAP * block_len
        for head in range(KVH):
            for block in range(blocks):
                at = pl.ds(block * block_len, block_len)
                split_kv(
                    pool.at[block],
                    head,
                    scratch.at[head],
                    tail_keys.at[head, at],
                    tail_values.at[head, at],
                )
            at = pl.ds(first, CAP * block_len)
            lanes = slice(head * HD, (head + 1) * HD)
            slot = lax.broadcasted_iota(jnp.int32, (CAP * block_len, HD), 0)
            key = tail_keys[head, at, :]
            value = tail_values[head, at, :]
            for row in range(rows):
                key = jnp.where(slot == row, new_kv[row, 0:1, lanes], key)
                value = jnp.where(slot == row, new_kv[row, 1:2, lanes], value)
            tail_keys[head, at, :] = key
            tail_values[head, at, :] = value

        lane = lax.broadcasted_iota(jnp.int32, (1, tokens), 1)

        def mask(row, carry):
            parent = parents[row]
            length = lengths[parent]
            reach = jnp.zeros((1, tokens), jnp.int32)
            for depth in range(table.shape[0]):
                block = table[depth, parent] - me * blocks
                reach = jnp.where(lane // block_len == block, length - depth * block_len, reach)
            own = row - me * rows
            own = jnp.where((own >= 0) & (own < rows), own + first, -1)
            live = (lane % block_len < reach) | (lane == own)
            bias[pl.ds(row, 1), :] = jnp.where(live, 0.0, masked_score)
            return carry

        lax.fori_loop(0, bias.shape[0], mask, 0)


def unpack(meta, prefix_kv, pool, new_kv, row_total):
    requests, length, _, width = prefix_kv.shape
    blocks, block_len = pool.shape[:2]
    tokens = blocks * block_len
    step = min(256, length)
    hbm = pl.BlockSpec(memory_space=pltpu.HBM)
    whole = lambda shape: pl.BlockSpec(shape, lambda r, i: (0,) * len(shape))
    return pl.pallas_call(
        unpack_kernel,
        name="unpack",
        grid=(requests, length // step),
        in_specs=[hbm] * 3
        + [
            pl.BlockSpec((1, step, 2, width), lambda r, i: (r, i, 0, 0)),
            whole(pool.shape),
            whole(new_kv.shape),
        ],
        out_specs=[pl.BlockSpec((1, KVH, step, HD), lambda r, i: (r, 0, i, 0))] * 2
        + [whole((KVH, tokens, HD))] * 2
        + [whole((row_total, tokens))],
        out_shape=[pltpu.HBM((requests, KVH, length, HD), bf16)] * 2
        + [jax.ShapeDtypeStruct((KVH, tokens, HD), bf16)] * 2
        + [jax.ShapeDtypeStruct((row_total, tokens), f32)],
        scratch_shapes=[pltpu.VMEM((KVH, 2 * step, HD), f32)] + meta_scratch(meta),
        compiler_params=pltpu.CompilerParams(vmem_limit_bytes=VMEM_LIMIT),
        cost_estimate=pl.CostEstimate(
            flops=0, bytes_accessed=4 * prefix_kv.size, transcendentals=0
        ),
    )(*map(in_hbm, meta), in_hbm(prefix_kv), pool, new_kv)


def pieces(value):
    high = value.astype(bf16)
    rest = value - high.astype(f32)
    middle = rest.astype(bf16)
    low = (rest - middle.astype(f32)).astype(bf16)
    return high.astype(f32), middle.astype(f32), low.astype(f32)


def attend_kernel(
    query, keys, values, tail_keys, tail_values, bias, out, wide, stacks, key_buffer, value_buffer, sem
):
    groups = HQ // KVH
    targets = out.shape[0] // KVH
    beams = query.shape[0]
    count = groups * beams
    share = count // targets
    factor = HD ** (-0.5) * math.log2(math.e)
    contract = (((1,), (1,)), ((), ()))
    request = pl.program_id(0)

    def loads(head):
        return (
            pltpu.make_async_copy(keys.at[request, head], key_buffer.at[head], sem.at[0, head]),
            pltpu.make_async_copy(values.at[request, head], value_buffer.at[head], sem.at[1, head]),
        )

    for head in range(KVH):
        for copy in loads(head):
            copy.start()

    wide[...] = query[...].astype(f32).reshape(beams * HQ, HD)
    for head in range(HQ):
        stacks[head * beams : (head + 1) * beams, :] = wide[pl.ds(head, beams, stride=HQ), :].astype(
            bf16
        )
    mask = jnp.concatenate([bias[...]] * groups, axis=0)
    lane = lax.broadcasted_iota(jnp.int32, (count, HD), 1)

    def one(head):
        stacked = stacks[pl.ds(pl.multiple_of(head * count, count), count), :]
        score = lax.dot_general(stacked, key_buffer[head], contract, preferred_element_type=f32)
        tail = lax.dot_general(stacked, tail_keys[head], contract, preferred_element_type=f32)
        tail = tail + mask
        top = jnp.maximum(
            jnp.max(score, axis=1, keepdims=True), jnp.max(tail, axis=1, keepdims=True)
        )
        weight = jnp.exp2((score - top) * factor)
        tail_weight = jnp.exp2((tail - top) * factor)
        total = jnp.sum(weight, axis=1, keepdims=True) + jnp.sum(
            tail_weight, axis=1, keepdims=True
        )
        result = jnp.dot(weight.astype(bf16), value_buffer[head], preferred_element_type=f32)
        result = result + jnp.dot(
            tail_weight.astype(bf16), tail_values[head], preferred_element_type=f32
        )
        packed = jnp.zeros((count, HD), f32)
        for at, term in enumerate(pieces(top) + pieces(total)):
            packed = jnp.where(lane == at, term, packed)
        if count < HD:
            packed = jnp.concatenate([packed, jnp.zeros((HD - count, HD), f32)], axis=0)
        stats = packed.T
        for t in range(targets):
            at = head * targets + t
            out[at, 0, :share, :] = result[t * share : (t + 1) * share].astype(bf16)
            mine = stats if t == 0 else pltpu.roll(stats, HD - t * share, 1)
            out[at, 0, share : share + STAT_ROWS, :] = mine[:STAT_ROWS].astype(bf16)

    def some(step, carry):
        heads = [step * AT_ONCE + i for i in range(AT_ONCE)]
        for head in heads:
            for copy in loads(head):
                copy.wait()
        for head in heads:
            one(head)
        return carry

    lax.fori_loop(0, KVH // AT_ONCE, some, 0)


def attend(everyone, keys, values, tail_keys, tail_values, bias, devices):
    requests, _, length, _ = keys.shape
    tokens = tail_keys.shape[1]
    beams = everyone.shape[0] // requests
    groups = HQ // KVH
    targets = devices // KVH
    rows = groups // targets * beams + STAT_ROWS
    hbm = pl.BlockSpec(memory_space=pltpu.HBM)
    return pl.pallas_call(
        attend_kernel,
        name="attend",
        grid=(requests,),
        in_specs=[
            pl.BlockSpec((beams, HQ, HD), lambda r: (r, 0, 0)),
            hbm,
            hbm,
            pl.BlockSpec((KVH, tokens, HD), lambda r: (0, 0, 0)),
            pl.BlockSpec((KVH, tokens, HD), lambda r: (0, 0, 0)),
            pl.BlockSpec((beams, tokens), lambda r: (r, 0)),
        ],
        out_specs=pl.BlockSpec((devices, 1, rows, HD), lambda r: (0, r, 0, 0)),
        out_shape=jax.ShapeDtypeStruct((devices, requests, rows, HD), bf16),
        scratch_shapes=[
            pltpu.VMEM((beams * HQ, HD), f32),
            pltpu.VMEM((beams * HQ, HD), bf16),
            pltpu.VMEM((KVH, length, HD), bf16),
            pltpu.VMEM((KVH, length, HD), bf16),
            pltpu.SemaphoreType.DMA((2, KVH)),
        ],
        compiler_params=pltpu.CompilerParams(vmem_limit_bytes=VMEM_LIMIT),
        cost_estimate=pl.CostEstimate(
            flops=4 * everyone.size * length,
            bytes_accessed=4 * keys.size,
            transcendentals=everyone.size * length // HD,
        ),
    )(everyone, in_hbm(keys), in_hbm(values), tail_keys, tail_values, bias)


def project_kernel(partial, weight, out, attended, scratch, buffer, sem):
    devices, requests, rows, _ = partial.shape
    share = rows - STAT_ROWS
    row_total = out.shape[0]
    beams = row_total // requests
    own = share // beams
    chunks = out.shape[1]
    parts = sem.shape[0]
    step = weight.shape[1] // parts
    factor = HD ** (-0.5) * math.log2(math.e)

    def load(part):
        lanes = pl.ds(part * step, step)
        return pltpu.make_async_copy(weight.at[:, lanes], buffer.at[part], sem.at[part])

    for part in range(parts):
        load(part).start()

    for r in range(requests):
        stats = [partial[p, r, share:rows, :].astype(f32) for p in range(devices)]
        tops = jnp.concatenate([s[0:1] + s[1:2] + s[2:3] for s in stats], axis=0)
        sums = jnp.concatenate([s[3:4] + s[4:5] + s[5:6] for s in stats], axis=0)
        scale = jnp.exp2((tops - jnp.max(tops, axis=0, keepdims=True)) * factor)
        scale = scale / jnp.sum(scale * sums, axis=0, keepdims=True)
        if devices < HD:
            scale = jnp.concatenate([scale, jnp.zeros((HD - devices, HD), f32)], axis=0)
        scale = scale.T
        total = jnp.zeros((share, HD), f32)
        for p in range(devices):
            total = total + partial[p, r, :share, :].astype(f32) * scale[:share, p : p + 1]
        for h in range(own):
            attended[r * beams : (r + 1) * beams, h * HD : (h + 1) * HD] = total[
                h * beams : (h + 1) * beams
            ].astype(bf16)

    for part in range(parts):
        load(part).wait()
        product = jnp.dot(attended[...], buffer[part], preferred_element_type=f32)
        for c in range(step // HD):
            scratch[pl.ds(part * (step // HD) + c, row_total, stride=chunks), :] = product[
                :, c * HD : (c + 1) * HD
            ]
    for row in range(row_total):
        out[row] = scratch[row * chunks : (row + 1) * chunks, :].astype(bf16)


def project(partial, weight, row_total):
    depth, width = weight.shape
    parts = max(1, width // 1024)
    return pl.pallas_call(
        project_kernel,
        name="project",
        in_specs=[
            pl.BlockSpec(memory_space=pltpu.VMEM),
            pl.BlockSpec(memory_space=pltpu.HBM),
        ],
        out_specs=pl.BlockSpec(memory_space=pltpu.VMEM),
        out_shape=jax.ShapeDtypeStruct((row_total, width // HD, HD), bf16),
        scratch_shapes=[
            pltpu.VMEM((row_total, depth), bf16),
            pltpu.VMEM((row_total * (width // HD), HD), f32),
            pltpu.VMEM((parts, depth, width // parts), bf16),
            pltpu.SemaphoreType.DMA((parts,)),
        ],
        compiler_params=pltpu.CompilerParams(vmem_limit_bytes=VMEM_LIMIT),
        cost_estimate=pl.CostEstimate(
            flops=2 * row_total * depth * width, bytes_accessed=2 * weight.size, transcendentals=0
        ),
    )(partial, in_hbm(weight))


def exchange(array):
    return lax.all_to_all(array, "ctx", split_axis=0, concat_axis=0, tiled=True)


def local(
    queries, new_kv, prefix_kv, pool, out_weight, parents, tail_table, fresh_slots, tail_lengths
):
    devices = lax.axis_size("ctx")
    rows = queries.shape[0]
    row_total = rows * devices
    width = out_weight.shape[1]
    rounds = rounds_of(devices)
    meta = (parents, tail_table.T, tail_lengths)

    def move(index, blocks):
        first, _ = rounds[index]
        return [
            lax.ppermute(block, "ctx", [(i, i ^ ((at + 1) << first)) for i in range(devices)])
            for at, block in enumerate(blocks)
        ]

    wide, *blocks = ask(rounds[0], devices, queries, meta, pool)
    everyone = exchange(wide).reshape(row_total, HQ, HD)
    arrived = move(0, blocks)
    tokens = unpack(meta, prefix_kv, pool, new_kv, row_total)
    for index in range(1, len(rounds)):
        blocks = pick(rounds[:index], rounds[index], devices, rows, meta, pool, arrived)
        arrived = arrived + move(index, blocks)
    partial = attend(everyone, *tokens, devices)
    partial = exchange(partial)
    products = project(partial, out_weight, row_total)
    products = exchange(products.reshape(devices, rows * (width // HD), HD))
    result = jnp.sum(products.astype(f32), axis=0).reshape(rows, width)
    new_pool = place(rounds, rows, meta + (fresh_slots,), new_kv, pool, arrived)
    return (result, new_pool)


def solution(mesh):
    in_specs = (
        P(("req", "ctx"), None),
        P(("req", "ctx"), None, None),
        P("req", "ctx", None, None),
        P(("req", "ctx"), None, None, None),
        P("ctx", None),
        P("req"),
        P("req", None),
        P("req"),
        P("req"),
    )
    out_specs = (P(("req", "ctx"), None), P(("req", "ctx"), None, None, None))
    return jax.shard_map(local, mesh=mesh, in_specs=in_specs, out_specs=out_specs, check_vma=False)
```

```python
import functools
import math

import jax
import jax.numpy as jnp
from jax import lax
from jax.experimental import pallas as pl
from jax.experimental.pallas import tpu as pltpu
from jax.sharding import PartitionSpec as P


HQ = 64
KVH = 8
HD = 128
CAP = 2

STAT_ROWS = 8
AT_ONCE = 2
VMEM_LIMIT = 20 << 20
masked_score = -1e30
bf16 = jnp.bfloat16
f32 = jnp.float32


def in_hbm(array):
    return pltpu.with_memory_space_constraint(array, pltpu.HBM)


def rounds_of(devices):
    total = devices.bit_length() - 1
    return [(0, 2)] + [(bit, 1) for bit in range(2, total)]


def channels_of(rounds):
    return [(first, mask) for first, bits in rounds for mask in range(1, 1 << bits)]


def load_meta(sources, targets, sem):
    copies = [pltpu.make_async_copy(s, t, sem.at[i]) for i, (s, t) in enumerate(zip(sources, targets))]
    for copy in copies:
        copy.start()
    return copies


def meta_scratch(meta):
    return [pltpu.SMEM(m.shape, jnp.int32) for m in meta] + [pltpu.SemaphoreType.DMA((len(meta),))]


def source_of(row, parents, table, lengths, block_len):
    parent = parents[row]
    length = lengths[parent]
    return length, table[length // block_len, parent]


def fetch_block(rounds, me, source, dest, part, rows, pool, arrived, target, sem):
    pool_dev = pool.shape[0]
    done = sum(bits for _, bits in rounds)
    moved = (source // pool_dev ^ me) & ((1 << done) - 1)

    @pl.when(moved == 0)
    def _():
        pltpu.make_async_copy(pool.at[source % pool_dev], target, sem).start()

    for (first, mask), ref in zip(channels_of(rounds), arrived):
        bits = dict(rounds)[first]

        @pl.when((moved >> first) == mask)
        def _():
            at = (dest >> (first + bits)) * rows + part
            pltpu.make_async_copy(ref.at[at], target, sem).start()


def begin_picks(rounds, now, rows, me, meta, pool, arrived, outs, sem):
    first, bits = now
    for mask in range(1, 1 << bits):
        out = outs[mask - 1]
        low = (me & ((1 << (first + bits)) - 1)) ^ (mask << first)

        def begin(at, carry):
            dest = (at // rows << (first + bits)) | low
            part = at % rows
            _, source = source_of(dest * rows + part, *meta, pool.shape[1])
            fetch_block(
                rounds, me, source, dest, part, rows, pool, arrived, out.at[at], sem.at[mask - 1, at]
            )
            return carry

        lax.fori_loop(0, out.shape[0], begin, 0)


def end_picks(pool, outs, sem):
    for index, out in enumerate(outs):

        def finish(at, carry):
            pltpu.make_async_copy(pool.at[0], out.at[at], sem.at[index, at]).wait()
            return carry

        lax.fori_loop(0, out.shape[0], finish, 0)


def ask_kernel(query, out, wide):
    devices, rows = out.shape[:2]
    heads = query.shape[1] // HD
    for row in range(rows):
        for head in range(heads):
            wide[head : head + 1, :] = query[row : row + 1, head * HD : (head + 1) * HD].astype(f32)
        value = wide[...].astype(bf16)
        for device in range(devices):
            out[device, row] = value


def ask(queries, devices):
    rows, width = queries.shape
    heads = width // HD
    vmem = pl.BlockSpec(memory_space=pltpu.VMEM)
    return pl.pallas_call(
        ask_kernel,
        name="ask",
        in_specs=[vmem],
        out_specs=vmem,
        out_shape=jax.ShapeDtypeStruct((devices, rows, heads, HD), bf16),
        scratch_shapes=[pltpu.VMEM((heads, HD), f32)],
        compiler_params=pltpu.CompilerParams(vmem_limit_bytes=VMEM_LIMIT),
    )(queries)


def pick_shapes(now, devices, rows, pool):
    first, bits = now
    count = (devices >> (first + bits)) * rows
    partners = (1 << bits) - 1
    return [jax.ShapeDtypeStruct((count,) + pool.shape[1:], bf16)] * partners, (partners, count)


def pick_kernel(rounds, now, rows, channels, parents_in, table_in, lengths_in, pool, *refs):
    partners = (1 << now[1]) - 1
    arrived, refs = refs[:channels], refs[channels:]
    outs, (parents, table, lengths, meta_sem, sem) = refs[:partners], refs[partners:]
    meta = (parents, table, lengths)
    for copy in load_meta((parents_in, table_in, lengths_in), meta, meta_sem):
        copy.wait()
    begin_picks(rounds, now, rows, lax.axis_index("ctx"), meta, pool, arrived, outs, sem)
    end_picks(pool, outs, sem)


def pick(rounds, now, devices, rows, meta, pool, arrived):
    shapes, semaphores = pick_shapes(now, devices, rows, pool)
    vmem, hbm = pl.BlockSpec(memory_space=pltpu.VMEM), pl.BlockSpec(memory_space=pltpu.HBM)
    return pl.pallas_call(
        functools.partial(pick_kernel, rounds, now, rows, len(arrived)),
        name="pick",
        in_specs=[hbm] * 4 + [pl.BlockSpec(memory_space=pl.ANY)] * len(arrived),
        out_specs=[vmem] * len(shapes),
        out_shape=shapes,
        scratch_shapes=meta_scratch(meta) + [pltpu.SemaphoreType.DMA(semaphores)],
        compiler_params=pltpu.CompilerParams(vmem_limit_bytes=VMEM_LIMIT),
        cost_estimate=pl.CostEstimate(flops=0, bytes_accessed=1 << 22, transcendentals=0),
    )(*map(in_hbm, meta), in_hbm(pool), *arrived)


def place_kernel(rounds, rows, parents_in, table_in, lengths_in, fresh_in, new_kv, pool, *refs):
    channels = len(channels_of(rounds))
    arrived, (out, parents, table, lengths, fresh, meta_sem, sem) = refs[:channels], refs[channels:]
    me = lax.axis_index("ctx")
    pool_dev, block_len = pool.shape[:2]
    whole = pltpu.make_async_copy(pool, out, sem)
    whole.start()
    sources = (parents_in, table_in, lengths_in, fresh_in)
    for copy in load_meta(sources, (parents, table, lengths, fresh), meta_sem):
        copy.wait()
    whole.wait()
    for part in range(rows):
        row = me * rows + part
        length, source = source_of(row, parents, table, lengths, block_len)
        slot = fresh[row] - me * pool_dev
        fetch_block(rounds, me, source, me, part, rows, pool, arrived, out.at[slot], sem)
        pltpu.make_async_copy(pool.at[0], out.at[slot], sem).wait()
        offset = length % block_len

        def token(at, carry):
            @pl.when(at == offset)
            def _():
                out[slot, at] = new_kv[part]

            @pl.when(at > offset)
            def _():
                out[slot, at] = jnp.zeros(out.shape[2:], bf16)

            return carry

        lax.fori_loop(0, block_len, token, 0)


def place(rounds, rows, meta, new_kv, pool, arrived):
    vmem, hbm = pl.BlockSpec(memory_space=pltpu.VMEM), pl.BlockSpec(memory_space=pltpu.HBM)
    return pl.pallas_call(
        functools.partial(place_kernel, rounds, rows),
        name="place",
        in_specs=[hbm] * 4 + [vmem, hbm] + [pl.BlockSpec(memory_space=pl.ANY)] * len(arrived),
        out_specs=vmem,
        out_shape=jax.ShapeDtypeStruct(pool.shape, bf16),
        scratch_shapes=meta_scratch(meta) + [pltpu.SemaphoreType.DMA],
        compiler_params=pltpu.CompilerParams(vmem_limit_bytes=VMEM_LIMIT),
        cost_estimate=pl.CostEstimate(flops=0, bytes_accessed=4 * pool.size, transcendentals=0),
    )(*map(in_hbm, meta), new_kv, in_hbm(pool), *arrived)


def pieces(value):
    high = value.astype(bf16)
    rest = value - high.astype(f32)
    middle = rest.astype(bf16)
    low = (rest - middle.astype(f32)).astype(bf16)
    return high.astype(f32), middle.astype(f32), low.astype(f32)


def attend_kernel(
    rows,
    query,
    parents_in,
    table_in,
    lengths_in,
    prefix,
    pool,
    new_kv,
    out,
    wide,
    stacks,
    bias,
    raw,
    pairs,
    sem,
    parents,
    table,
    lengths,
    meta_sem,
):
    groups = HQ // KVH
    targets = out.shape[0] // KVH
    beams = query.shape[0]
    count = groups * beams
    share = count // targets
    factor = HD ** (-0.5) * math.log2(math.e)
    contract = (((1,), (1,)), ((), ()))
    request = pl.program_id(0)
    length = prefix.shape[1]
    blocks, block_len = pool.shape[:2]
    tokens = blocks * block_len
    old = tokens - CAP * block_len
    me = lax.axis_index("ctx")

    def loads(head):
        lanes = pl.ds(pl.multiple_of(head * HD, HD), HD)
        flat = pool.reshape(tokens, 2, pool.shape[3])
        spans = [
            (prefix.at[request, :, :, lanes], 0, length),
            (flat.at[pl.ds(0, old), :, lanes], length, old),
            (new_kv.at[:, :, lanes], length + old, rows),
            (flat.at[pl.ds(old + rows, tokens - old - rows), :, lanes], length + old + rows, 0),
        ]
        return [
            pltpu.make_async_copy(
                source, raw.at[head, pl.ds(first, source.shape[0])], sem.at[index, head]
            )
            for index, (source, first, _) in enumerate(spans)
        ]

    sources = (parents_in, table_in, lengths_in)
    copies = load_meta(sources, (parents, table, lengths), meta_sem)
    for head in range(KVH):
        for copy in loads(head):
            copy.start()

    wide[...] = query[...].astype(f32).reshape(beams * HQ, HD)
    for head in range(HQ):
        stacks[head * beams : (head + 1) * beams, :] = wide[pl.ds(head, beams, stride=HQ), :].astype(
            bf16
        )
    for copy in copies:
        copy.wait()
    position = lax.broadcasted_iota(jnp.int32, (1, tokens), 1)
    in_block, at_block = position % block_len, position // block_len

    for beam in range(beams):
        row = request * beams + beam
        parent = parents[row]
        tail = lengths[parent]
        reach = jnp.zeros((1, tokens), jnp.int32)
        for depth in range(table.shape[0]):
            block = table[depth, parent] - me * blocks
            reach = jnp.where(at_block == block, tail - depth * block_len, reach)
        own = row - me * rows
        own = jnp.where((own >= 0) & (own < rows), own + old, -1)
        live = (in_block < reach) | (position == own)
        bias[beam : beam + 1, :] = jnp.where(live, 0.0, masked_score)

    lane = lax.broadcasted_iota(jnp.int32, (count, HD), 1)

    def one(head, slot):
        stacked = stacks[pl.ds(pl.multiple_of(head * count, count), count), :]
        total_len = length + tokens
        pairs[slot] = raw.at[head].reshape(2 * total_len, HD)[...].astype(f32)
        keys = pairs[slot, pl.ds(0, total_len, stride=2), :].astype(bf16)
        values = pairs[slot, pl.ds(1, total_len, stride=2), :].astype(bf16)
        score = lax.dot_general(stacked, keys, contract, preferred_element_type=f32)
        tail = score[:, length:] + jnp.concatenate([bias[...]] * groups, axis=0)
        score = score[:, :length]
        top = jnp.maximum(
            jnp.max(score, axis=1, keepdims=True), jnp.max(tail, axis=1, keepdims=True)
        )
        weight = jnp.exp2((score - top) * factor)
        tail_weight = jnp.exp2((tail - top) * factor)
        total = jnp.sum(weight, axis=1, keepdims=True) + jnp.sum(
            tail_weight, axis=1, keepdims=True
        )
        weight = jnp.concatenate([weight.astype(bf16), tail_weight.astype(bf16)], axis=1)
        result = jnp.dot(weight, values, preferred_element_type=f32)
        packed = jnp.zeros((count, HD), f32)
        for at, term in enumerate(pieces(top) + pieces(total)):
            packed = jnp.where(lane == at, term, packed)
        if count < HD:
            packed = jnp.concatenate([packed, jnp.zeros((HD - count, HD), f32)], axis=0)
        stats = packed.T
        for t in range(targets):
            at = head * targets + t
            out[at, 0, :share, :] = result[t * share : (t + 1) * share].astype(bf16)
            mine = stats if t == 0 else pltpu.roll(stats, HD - t * share, 1)
            out[at, 0, share : share + STAT_ROWS, :] = mine[:STAT_ROWS].astype(bf16)

    def some(step, carry):
        heads = [step * AT_ONCE + i for i in range(AT_ONCE)]
        for head in heads:
            for copy in loads(head):
                copy.wait()
        for slot, head in enumerate(heads):
            one(head, slot)
        return carry

    lax.fori_loop(0, KVH // AT_ONCE, some, 0)


def attend(everyone, meta, prefix_kv, pool, new_kv, devices):
    requests, length = prefix_kv.shape[:2]
    tokens = pool.shape[0] * pool.shape[1]
    beams = everyone.shape[0] // requests
    groups = HQ // KVH
    targets = devices // KVH
    rows = groups // targets * beams + STAT_ROWS
    hbm = pl.BlockSpec(memory_space=pltpu.HBM)
    return pl.pallas_call(
        functools.partial(attend_kernel, new_kv.shape[0]),
        name="attend",
        grid=(requests,),
        in_specs=[pl.BlockSpec((beams, HQ, HD), lambda r: (r, 0, 0))] + [hbm] * 6,
        out_specs=pl.BlockSpec((devices, 1, rows, HD), lambda r: (0, r, 0, 0)),
        out_shape=jax.ShapeDtypeStruct((devices, requests, rows, HD), bf16),
        scratch_shapes=[
            pltpu.VMEM((beams * HQ, HD), f32),
            pltpu.VMEM((beams * HQ, HD), bf16),
            pltpu.VMEM((beams, tokens), f32),
            pltpu.VMEM((KVH, length + tokens, 2, HD), bf16),
            pltpu.VMEM((AT_ONCE, 2 * (length + tokens), HD), f32),
            pltpu.SemaphoreType.DMA((4, KVH)),
        ]
        + meta_scratch(meta),
        compiler_params=pltpu.CompilerParams(vmem_limit_bytes=VMEM_LIMIT),
        cost_estimate=pl.CostEstimate(
            flops=4 * everyone.size * length,
            bytes_accessed=2 * prefix_kv.size,
            transcendentals=everyone.size * length // HD,
        ),
    )(everyone, *map(in_hbm, meta), in_hbm(prefix_kv), in_hbm(pool), in_hbm(new_kv))


def project_kernel(partial, weight, out, attended, scratch, buffer, sem):
    devices, requests, rows, _ = partial.shape
    share = rows - STAT_ROWS
    row_total = out.shape[0]
    beams = row_total // requests
    own = share // beams
    chunks = out.shape[1]
    parts = sem.shape[0]
    step = weight.shape[1] // parts
    factor = HD ** (-0.5) * math.log2(math.e)

    def load(part):
        lanes = pl.ds(part * step, step)
        return pltpu.make_async_copy(weight.at[:, lanes], buffer.at[part], sem.at[part])

    for part in range(parts):
        load(part).start()

    for r in range(requests):
        stats = [partial[p, r, share:rows, :].astype(f32) for p in range(devices)]
        tops = jnp.concatenate([s[0:1] + s[1:2] + s[2:3] for s in stats], axis=0)
        sums = jnp.concatenate([s[3:4] + s[4:5] + s[5:6] for s in stats], axis=0)
        scale = jnp.exp2((tops - jnp.max(tops, axis=0, keepdims=True)) * factor)
        scale = scale / jnp.sum(scale * sums, axis=0, keepdims=True)
        if devices < HD:
            scale = jnp.concatenate([scale, jnp.zeros((HD - devices, HD), f32)], axis=0)
        scale = scale.T
        total = jnp.zeros((share, HD), f32)
        for p in range(devices):
            total = total + partial[p, r, :share, :].astype(f32) * scale[:share, p : p + 1]
        for h in range(own):
            attended[r * beams : (r + 1) * beams, h * HD : (h + 1) * HD] = total[
                h * beams : (h + 1) * beams
            ].astype(bf16)

    for part in range(parts):
        load(part).wait()
        product = jnp.dot(attended[...], buffer[part], preferred_element_type=f32)
        for c in range(step // HD):
            scratch[pl.ds(part * (step // HD) + c, row_total, stride=chunks), :] = product[
                :, c * HD : (c + 1) * HD
            ]
    for row in range(row_total):
        out[row] = scratch[row * chunks : (row + 1) * chunks, :].astype(bf16)


def project(partial, weight, row_total):
    depth, width = weight.shape
    parts = max(1, width // 1024)
    return pl.pallas_call(
        project_kernel,
        name="project",
        in_specs=[
            pl.BlockSpec(memory_space=pltpu.VMEM),
            pl.BlockSpec(memory_space=pltpu.HBM),
        ],
        out_specs=pl.BlockSpec(memory_space=pltpu.VMEM),
        out_shape=jax.ShapeDtypeStruct((row_total, width // HD, HD), bf16),
        scratch_shapes=[
            pltpu.VMEM((row_total, depth), bf16),
            pltpu.VMEM((row_total * (width // HD), HD), f32),
            pltpu.VMEM((parts, depth, width // parts), bf16),
            pltpu.SemaphoreType.DMA((parts,)),
        ],
        compiler_params=pltpu.CompilerParams(vmem_limit_bytes=VMEM_LIMIT),
        cost_estimate=pl.CostEstimate(
            flops=2 * row_total * depth * width, bytes_accessed=2 * weight.size, transcendentals=0
        ),
    )(partial, in_hbm(weight))


def exchange(array):
    return lax.all_to_all(array, "ctx", split_axis=0, concat_axis=0, tiled=True)


def local(
    queries, new_kv, prefix_kv, pool, out_weight, parents, tail_table, fresh_slots, tail_lengths
):
    devices = lax.axis_size("ctx")
    rows = queries.shape[0]
    row_total = rows * devices
    width = out_weight.shape[1]
    rounds = rounds_of(devices)
    meta = (parents, tail_table.T, tail_lengths)

    def move(index, blocks):
        first, _ = rounds[index]
        return [
            lax.ppermute(block, "ctx", [(i, i ^ ((at + 1) << first)) for i in range(devices)])
            for at, block in enumerate(blocks)
        ]

    wide = ask(queries, devices)
    everyone = exchange(wide).reshape(row_total, HQ, HD)
    arrived = []
    for index in range(len(rounds)):
        blocks = pick(rounds[:index], rounds[index], devices, rows, meta, pool, arrived)
        arrived = arrived + move(index, blocks)
    partial = attend(everyone, meta, prefix_kv, pool, new_kv, devices)
    partial = exchange(partial)
    products = project(partial, out_weight, row_total)
    products = exchange(products.reshape(devices, rows * (width // HD), HD))
    result = jnp.sum(products.astype(f32), axis=0).reshape(rows, width)
    new_pool = place(rounds, rows, meta + (fresh_slots,), new_kv, pool, arrived)
    return (result, new_pool)


def solution(mesh):
    in_specs = (
        P(("req", "ctx"), None),
        P(("req", "ctx"), None, None),
        P("req", "ctx", None, None),
        P(("req", "ctx"), None, None, None),
        P("ctx", None),
        P("req"),
        P("req", None),
        P("req"),
        P("req"),
    )
    out_specs = (P(("req", "ctx"), None), P(("req", "ctx"), None, None, None))
    return jax.shard_map(local, mesh=mesh, in_specs=in_specs, out_specs=out_specs, check_vma=False)
```

```python
import functools
import math

import jax
import jax.numpy as jnp
from jax import lax
from jax.experimental import pallas as pl
from jax.experimental.pallas import tpu as pltpu
from jax.sharding import PartitionSpec as P


HQ = 64
KVH = 8
HD = 128
CAP = 2

STAT_ROWS = 8
AT_ONCE = 2
VMEM_LIMIT = 20 << 20
masked_score = -1e30
bf16 = jnp.bfloat16
f32 = jnp.float32


def in_hbm(array):
    return pltpu.with_memory_space_constraint(array, pltpu.HBM)


def rounds_of(devices):
    total = devices.bit_length() - 1
    return [(0, 2)] + [(bit, 1) for bit in range(2, total)]


def channels_of(rounds):
    return [(first, mask) for first, bits in rounds for mask in range(1, 1 << bits)]


def load_meta(sources, targets, sem):
    copies = [pltpu.make_async_copy(s, t, sem.at[i]) for i, (s, t) in enumerate(zip(sources, targets))]
    for copy in copies:
        copy.start()
    return copies


def meta_scratch(meta):
    return [pltpu.SMEM(m.shape, jnp.int32) for m in meta] + [pltpu.SemaphoreType.DMA((len(meta),))]


def source_of(row, parents, table, lengths, block_len):
    parent = parents[row]
    length = lengths[parent]
    return length, table[length // block_len, parent]


def fetch_block(rounds, me, source, dest, part, rows, pool, arrived, target, sem):
    pool_dev = pool.shape[0]
    done = sum(bits for _, bits in rounds)
    moved = (source // pool_dev ^ me) & ((1 << done) - 1)

    @pl.when(moved == 0)
    def _():
        pltpu.make_async_copy(pool.at[source % pool_dev], target, sem).start()

    for (first, mask), ref in zip(channels_of(rounds), arrived):
        bits = dict(rounds)[first]

        @pl.when((moved >> first) == mask)
        def _():
            at = (dest >> (first + bits)) * rows + part
            pltpu.make_async_copy(ref.at[at], target, sem).start()


def begin_picks(rounds, now, rows, me, meta, pool, arrived, outs, sem):
    first, bits = now
    for mask in range(1, 1 << bits):
        out = outs[mask - 1]
        low = (me & ((1 << (first + bits)) - 1)) ^ (mask << first)

        def begin(at, carry):
            dest = (at // rows << (first + bits)) | low
            part = at % rows
            _, source = source_of(dest * rows + part, *meta, pool.shape[1])
            fetch_block(
                rounds, me, source, dest, part, rows, pool, arrived, out.at[at], sem.at[mask - 1, at]
            )
            return carry

        lax.fori_loop(0, out.shape[0], begin, 0)


def end_picks(pool, outs, sem):
    for index, out in enumerate(outs):

        def finish(at, carry):
            pltpu.make_async_copy(pool.at[0], out.at[at], sem.at[index, at]).wait()
            return carry

        lax.fori_loop(0, out.shape[0], finish, 0)


def ask_kernel(query, out, wide):
    devices, rows = out.shape[:2]
    heads = query.shape[1] // HD
    for row in range(rows):
        for head in range(heads):
            wide[head : head + 1, :] = query[row : row + 1, head * HD : (head + 1) * HD].astype(f32)
        value = wide[...].astype(bf16)
        for device in range(devices):
            out[device, row] = value


def ask(queries, devices):
    rows, width = queries.shape
    heads = width // HD
    vmem = pl.BlockSpec(memory_space=pltpu.VMEM)
    return pl.pallas_call(
        ask_kernel,
        name="ask",
        in_specs=[vmem],
        out_specs=vmem,
        out_shape=jax.ShapeDtypeStruct((devices, rows, heads, HD), bf16),
        scratch_shapes=[pltpu.VMEM((heads, HD), f32)],
        compiler_params=pltpu.CompilerParams(vmem_limit_bytes=VMEM_LIMIT),
    )(queries)


def pick_shapes(now, devices, rows, pool):
    first, bits = now
    count = (devices >> (first + bits)) * rows
    partners = (1 << bits) - 1
    return [jax.ShapeDtypeStruct((count,) + pool.shape[1:], bf16)] * partners, (partners, count)


def pick_kernel(rounds, now, rows, channels, parents_in, table_in, lengths_in, pool, *refs):
    partners = (1 << now[1]) - 1
    arrived, refs = refs[:channels], refs[channels:]
    outs, (parents, table, lengths, meta_sem, sem) = refs[:partners], refs[partners:]
    meta = (parents, table, lengths)
    for copy in load_meta((parents_in, table_in, lengths_in), meta, meta_sem):
        copy.wait()
    begin_picks(rounds, now, rows, lax.axis_index("ctx"), meta, pool, arrived, outs, sem)
    end_picks(pool, outs, sem)


def pick(rounds, now, devices, rows, meta, pool, arrived):
    shapes, semaphores = pick_shapes(now, devices, rows, pool)
    vmem, hbm = pl.BlockSpec(memory_space=pltpu.VMEM), pl.BlockSpec(memory_space=pltpu.HBM)
    return pl.pallas_call(
        functools.partial(pick_kernel, rounds, now, rows, len(arrived)),
        name="pick",
        in_specs=[hbm] * 4 + [pl.BlockSpec(memory_space=pl.ANY)] * len(arrived),
        out_specs=[vmem] * len(shapes),
        out_shape=shapes,
        scratch_shapes=meta_scratch(meta) + [pltpu.SemaphoreType.DMA(semaphores)],
        compiler_params=pltpu.CompilerParams(vmem_limit_bytes=VMEM_LIMIT),
        cost_estimate=pl.CostEstimate(flops=0, bytes_accessed=1 << 22, transcendentals=0),
    )(*map(in_hbm, meta), in_hbm(pool), *arrived)


def place_kernel(rounds, rows, parents_in, table_in, lengths_in, fresh_in, new_kv, pool, *refs):
    channels = len(channels_of(rounds))
    arrived, (out, parents, table, lengths, fresh, meta_sem, sem) = refs[:channels], refs[channels:]
    me = lax.axis_index("ctx")
    pool_dev, block_len = pool.shape[:2]
    whole = pltpu.make_async_copy(pool, out, sem)
    whole.start()
    sources = (parents_in, table_in, lengths_in, fresh_in)
    for copy in load_meta(sources, (parents, table, lengths, fresh), meta_sem):
        copy.wait()
    whole.wait()
    for part in range(rows):
        row = me * rows + part
        length, source = source_of(row, parents, table, lengths, block_len)
        slot = fresh[row] - me * pool_dev
        fetch_block(rounds, me, source, me, part, rows, pool, arrived, out.at[slot], sem)
        pltpu.make_async_copy(pool.at[0], out.at[slot], sem).wait()
        offset = length % block_len

        def token(at, carry):
            @pl.when(at == offset)
            def _():
                out[slot, at] = new_kv[part]

            @pl.when(at > offset)
            def _():
                out[slot, at] = jnp.zeros(out.shape[2:], bf16)

            return carry

        lax.fori_loop(0, block_len, token, 0)


def place(rounds, rows, meta, new_kv, pool, arrived):
    vmem, hbm = pl.BlockSpec(memory_space=pltpu.VMEM), pl.BlockSpec(memory_space=pltpu.HBM)
    return pl.pallas_call(
        functools.partial(place_kernel, rounds, rows),
        name="place",
        in_specs=[hbm] * 4 + [vmem, hbm] + [pl.BlockSpec(memory_space=pl.ANY)] * len(arrived),
        out_specs=vmem,
        out_shape=jax.ShapeDtypeStruct(pool.shape, bf16),
        scratch_shapes=meta_scratch(meta) + [pltpu.SemaphoreType.DMA],
        compiler_params=pltpu.CompilerParams(vmem_limit_bytes=VMEM_LIMIT),
        cost_estimate=pl.CostEstimate(flops=0, bytes_accessed=4 * pool.size, transcendentals=0),
    )(*map(in_hbm, meta), new_kv, in_hbm(pool), *arrived)


def pieces(value):
    high = value.astype(bf16)
    rest = value - high.astype(f32)
    middle = rest.astype(bf16)
    low = (rest - middle.astype(f32)).astype(bf16)
    return high.astype(f32), middle.astype(f32), low.astype(f32)


def tiles(array):
    width = array.shape[-1]
    split = array.reshape(-1, 2, width // HD, HD).transpose(0, 2, 1, 3)
    return split.reshape(-1, HD)


def unpack_kernel(
    rows,
    block_len,
    parents_in,
    table_in,
    lengths_in,
    prefix,
    pool,
    new_kv,
    keys,
    values,
    bias,
    raw,
    wide,
    value_buffer,
    in_sem,
    tail_sem,
    out_sem,
    parents,
    table,
    lengths,
    meta_sem,
):
    requests = keys.shape[0]
    per = 2 * KVH
    size = raw.shape[1]
    tokens = size // per
    chunks = raw.shape[0] - 1
    old = tokens - CAP * block_len
    blocks = tokens // block_len
    me = lax.axis_index("ctx")
    metas = load_meta((parents_in, table_in, lengths_in), (parents, table, lengths), meta_sem)

    first, last = old * per, (old + rows) * per
    spans = [
        (pool.at[pl.ds(0, first)], 0, first),
        (new_kv, first, last - first),
        (pool.at[pl.ds(last, size - last)], last, size - last),
    ]
    tails = [
        pltpu.make_async_copy(source, raw.at[chunks, pl.ds(at, count)], tail_sem.at[index])
        for index, (source, at, count) in enumerate(spans)
    ]

    def load(request, chunk):
        at = pl.multiple_of((request * chunks + chunk) * size, size)
        return pltpu.make_async_copy(prefix.at[pl.ds(at, size)], raw.at[chunk], in_sem.at[chunk])

    def store(request, chunk):
        span = pl.ds(pl.multiple_of(chunk * tokens, tokens), tokens)
        return pltpu.make_async_copy(
            value_buffer.at[:, span], values.at[request, :, span], out_sem.at[chunk]
        )

    def split(request, chunk):
        slot = chunk % 2
        wide[slot] = raw[chunk].astype(f32)
        span = pl.ds(pl.multiple_of(chunk * tokens, tokens), tokens)
        for head in range(KVH):
            keys[request, head, span, :] = wide[
                slot, pl.ds(2 * head, tokens, stride=per), :
            ].astype(bf16)
            value_buffer[head, span, :] = wide[
                slot, pl.ds(2 * head + 1, tokens, stride=per), :
            ].astype(bf16)
        store(request, chunk).start()

    for copy in tails:
        copy.start()
    for request in range(requests):
        for chunk in range(chunks):
            load(request, chunk).start()
        if request == 0:
            for copy in metas:
                copy.wait()
            position = lax.broadcasted_iota(jnp.int32, (1, tokens), 1)
            in_block, at_block = position % block_len, position // block_len

            def mask(row, carry):
                parent = parents[row]
                tail = lengths[parent]
                reach = jnp.zeros((1, tokens), jnp.int32)
                for depth in range(table.shape[0]):
                    block = table[depth, parent] - me * blocks
                    reach = jnp.where(at_block == block, tail - depth * block_len, reach)
                own = row - me * rows
                own = jnp.where((own >= 0) & (own < rows), own + old, -1)
                live = (in_block < reach) | (position == own)
                bias[pl.ds(row, 1), :] = jnp.where(live, 0.0, masked_score)
                return carry

            lax.fori_loop(0, bias.shape[0], mask, 0)
            for copy in tails:
                copy.wait()

        def step(chunk, carry):
            @pl.when(chunk < chunks)
            def _():
                load(request, chunk).wait()

            split(request, chunk)
            return carry

        lax.fori_loop(0, chunks + 1, step, 0)
        for chunk in range(chunks + 1):
            store(request, chunk).wait()


def unpack(meta, prefix_kv, pool, new_kv, row_total):
    requests, length = prefix_kv.shape[:2]
    blocks, block_len = pool.shape[:2]
    tokens = blocks * block_len
    chunks = length // tokens
    size = 2 * KVH * tokens
    whole = (KVH, length + tokens, HD)
    hbm, vmem = pl.BlockSpec(memory_space=pltpu.HBM), pl.BlockSpec(memory_space=pltpu.VMEM)
    arrays = tuple(map(tiles, (prefix_kv, pool, new_kv)))
    return pl.pallas_call(
        functools.partial(unpack_kernel, new_kv.shape[0], block_len),
        name="unpack",
        in_specs=[hbm] * 6,
        out_specs=[vmem, hbm, vmem],
        out_shape=[
            jax.ShapeDtypeStruct((requests,) + whole, bf16),
            pltpu.HBM((requests,) + whole, bf16),
            jax.ShapeDtypeStruct((row_total, tokens), f32),
        ],
        scratch_shapes=[
            pltpu.VMEM((chunks + 1, size, HD), bf16),
            pltpu.VMEM((2, size, HD), f32),
            pltpu.VMEM(whole, bf16),
            pltpu.SemaphoreType.DMA((chunks,)),
            pltpu.SemaphoreType.DMA((3,)),
            pltpu.SemaphoreType.DMA((chunks + 1,)),
        ]
        + meta_scratch(meta),
        compiler_params=pltpu.CompilerParams(vmem_limit_bytes=VMEM_LIMIT),
        cost_estimate=pl.CostEstimate(
            flops=0, bytes_accessed=3 * prefix_kv.size, transcendentals=0
        ),
    )(*map(in_hbm, meta + arrays))


def attend_kernel(query, keys, values, bias, out, wide, stacks, value_buffer, sem):
    groups = HQ // KVH
    requests = keys.shape[0]
    targets = out.shape[0] // KVH
    beams = query.shape[0] // requests
    count = groups * beams
    share = count // targets
    tokens = bias.shape[1]
    length = keys.shape[2] - tokens
    factor = HD ** (-0.5) * math.log2(math.e)
    contract = (((1,), (1,)), ((), ()))
    lane = lax.broadcasted_iota(jnp.int32, (count, HD), 1)

    def load(request, head):
        return pltpu.make_async_copy(values.at[request, head], value_buffer.at[head], sem.at[head])

    for request in range(requests):
        for head in range(KVH):
            load(request, head).start()
        span = pl.ds(request * beams, beams)
        wide[...] = query[span].astype(f32).reshape(beams * HQ, HD)
        for head in range(HQ):
            stacks[head * beams : (head + 1) * beams, :] = wide[
                pl.ds(head, beams, stride=HQ), :
            ].astype(bf16)

        def one(head):
            stacked = stacks[pl.ds(pl.multiple_of(head * count, count), count), :]
            score = lax.dot_general(
                stacked, keys[request, head], contract, preferred_element_type=f32
            )
            tail = score[:, length:] + jnp.concatenate([bias[span, :]] * groups, axis=0)
            score = jnp.concatenate([score[:, :length], tail], axis=1)
            top = jnp.max(score, axis=1, keepdims=True)
            weight = jnp.exp2((score - top) * factor)
            total = jnp.sum(weight, axis=1, keepdims=True)
            result = jnp.dot(weight.astype(bf16), value_buffer[head], preferred_element_type=f32)
            packed = jnp.zeros((count, HD), f32)
            for at, term in enumerate(pieces(top) + pieces(total)):
                packed = jnp.where(lane == at, term, packed)
            if count < HD:
                packed = jnp.concatenate([packed, jnp.zeros((HD - count, HD), f32)], axis=0)
            stats = packed.T
            for t in range(targets):
                at = head * targets + t
                out[at, request, :share, :] = result[t * share : (t + 1) * share].astype(bf16)
                mine = stats if t == 0 else pltpu.roll(stats, HD - t * share, 1)
                out[at, request, share : share + STAT_ROWS, :] = mine[:STAT_ROWS].astype(bf16)

        def some(step, carry):
            heads = [step * AT_ONCE + i for i in range(AT_ONCE)]
            for head in heads:
                load(request, head).wait()
            for head in heads:
                one(head)
            return carry

        lax.fori_loop(0, KVH // AT_ONCE, some, 0)


def attend(everyone, keys, values, bias, devices):
    requests, _, length, _ = keys.shape
    beams = everyone.shape[0] // requests
    groups = HQ // KVH
    targets = devices // KVH
    rows = groups // targets * beams + STAT_ROWS
    hbm, vmem = pl.BlockSpec(memory_space=pltpu.HBM), pl.BlockSpec(memory_space=pltpu.VMEM)
    return pl.pallas_call(
        attend_kernel,
        name="attend",
        in_specs=[vmem, vmem, hbm, vmem],
        out_specs=vmem,
        out_shape=jax.ShapeDtypeStruct((devices, requests, rows, HD), bf16),
        scratch_shapes=[
            pltpu.VMEM((beams * HQ, HD), f32),
            pltpu.VMEM((beams * HQ, HD), bf16),
            pltpu.VMEM((KVH, length, HD), bf16),
            pltpu.SemaphoreType.DMA((KVH,)),
        ],
        compiler_params=pltpu.CompilerParams(vmem_limit_bytes=VMEM_LIMIT),
        cost_estimate=pl.CostEstimate(
            flops=4 * everyone.size * length,
            bytes_accessed=4 * keys.size,
            transcendentals=everyone.size * length // HD,
        ),
    )(everyone, keys, in_hbm(values), bias)


def project_kernel(partial, weight, out, attended, scratch, buffer, sem):
    devices, requests, rows, _ = partial.shape
    share = rows - STAT_ROWS
    row_total = out.shape[0]
    beams = row_total // requests
    own = share // beams
    chunks = out.shape[1]
    parts = sem.shape[0]
    step = weight.shape[1] // parts
    factor = HD ** (-0.5) * math.log2(math.e)

    def load(part):
        lanes = pl.ds(part * step, step)
        return pltpu.make_async_copy(weight.at[:, lanes], buffer.at[part], sem.at[part])

    for part in range(parts):
        load(part).start()

    for r in range(requests):
        stats = [partial[p, r, share:rows, :].astype(f32) for p in range(devices)]
        tops = jnp.concatenate([s[0:1] + s[1:2] + s[2:3] for s in stats], axis=0)
        sums = jnp.concatenate([s[3:4] + s[4:5] + s[5:6] for s in stats], axis=0)
        scale = jnp.exp2((tops - jnp.max(tops, axis=0, keepdims=True)) * factor)
        scale = scale / jnp.sum(scale * sums, axis=0, keepdims=True)
        if devices < HD:
            scale = jnp.concatenate([scale, jnp.zeros((HD - devices, HD), f32)], axis=0)
        scale = scale.T
        total = jnp.zeros((share, HD), f32)
        for p in range(devices):
            total = total + partial[p, r, :share, :].astype(f32) * scale[:share, p : p + 1]
        for h in range(own):
            attended[r * beams : (r + 1) * beams, h * HD : (h + 1) * HD] = total[
                h * beams : (h + 1) * beams
            ].astype(bf16)

    for part in range(parts):
        load(part).wait()
        product = jnp.dot(attended[...], buffer[part], preferred_element_type=f32)
        for c in range(step // HD):
            scratch[pl.ds(part * (step // HD) + c, row_total, stride=chunks), :] = product[
                :, c * HD : (c + 1) * HD
            ]
    for row in range(row_total):
        out[row] = scratch[row * chunks : (row + 1) * chunks, :].astype(bf16)


def project(partial, weight, row_total):
    depth, width = weight.shape
    parts = max(1, width // 1024)
    return pl.pallas_call(
        project_kernel,
        name="project",
        in_specs=[
            pl.BlockSpec(memory_space=pltpu.VMEM),
            pl.BlockSpec(memory_space=pltpu.HBM),
        ],
        out_specs=pl.BlockSpec(memory_space=pltpu.VMEM),
        out_shape=jax.ShapeDtypeStruct((row_total, width // HD, HD), bf16),
        scratch_shapes=[
            pltpu.VMEM((row_total, depth), bf16),
            pltpu.VMEM((row_total * (width // HD), HD), f32),
            pltpu.VMEM((parts, depth, width // parts), bf16),
            pltpu.SemaphoreType.DMA((parts,)),
        ],
        compiler_params=pltpu.CompilerParams(vmem_limit_bytes=VMEM_LIMIT),
        cost_estimate=pl.CostEstimate(
            flops=2 * row_total * depth * width, bytes_accessed=2 * weight.size, transcendentals=0
        ),
    )(partial, in_hbm(weight))


def exchange(array):
    return lax.all_to_all(array, "ctx", split_axis=0, concat_axis=0, tiled=True)


def local(
    queries, new_kv, prefix_kv, pool, out_weight, parents, tail_table, fresh_slots, tail_lengths
):
    devices = lax.axis_size("ctx")
    rows = queries.shape[0]
    row_total = rows * devices
    width = out_weight.shape[1]
    rounds = rounds_of(devices)
    meta = (parents, tail_table.T, tail_lengths)

    def move(index, blocks):
        first, _ = rounds[index]
        return [
            lax.ppermute(block, "ctx", [(i, i ^ ((at + 1) << first)) for i in range(devices)])
            for at, block in enumerate(blocks)
        ]

    wide = ask(queries, devices)
    everyone = exchange(wide).reshape(row_total, HQ, HD)
    tokens = unpack(meta, prefix_kv, pool, new_kv, row_total)
    arrived = []
    for index in range(len(rounds)):
        blocks = pick(rounds[:index], rounds[index], devices, rows, meta, pool, arrived)
        arrived = arrived + move(index, blocks)
    partial = attend(everyone, *tokens, devices)
    partial = exchange(partial)
    products = project(partial, out_weight, row_total)
    products = exchange(products.reshape(devices, rows * (width // HD), HD))
    result = jnp.sum(products.astype(f32), axis=0).reshape(rows, width)
    new_pool = place(rounds, rows, meta + (fresh_slots,), new_kv, pool, arrived)
    return (result, new_pool)


def solution(mesh):
    in_specs = (
        P(("req", "ctx"), None),
        P(("req", "ctx"), None, None),
        P("req", "ctx", None, None),
        P(("req", "ctx"), None, None, None),
        P("ctx", None),
        P("req"),
        P("req", None),
        P("req"),
        P("req"),
    )
    out_specs = (P(("req", "ctx"), None), P(("req", "ctx"), None, None, None))
    return jax.shard_map(local, mesh=mesh, in_specs=in_specs, out_specs=out_specs, check_vma=False)
```

```python
import functools
import math

import jax
import jax.numpy as jnp
from jax import lax
from jax.experimental import pallas as pl
from jax.experimental.pallas import tpu as pltpu
from jax.sharding import PartitionSpec as P


HQ = 64
KVH = 8
HD = 128
CAP = 2

STAT_ROWS = 8
AT_ONCE = 2
VMEM_LIMIT = 20 << 20
masked_score = -1e30
bf16 = jnp.bfloat16
f32 = jnp.float32


def in_hbm(array):
    return pltpu.with_memory_space_constraint(array, pltpu.HBM)


def rounds_of(devices):
    total = devices.bit_length() - 1
    return [(0, 2)] + [(bit, 1) for bit in range(2, total)]


def channels_of(rounds):
    return [(first, mask) for first, bits in rounds for mask in range(1, 1 << bits)]


def load_meta(sources, targets, sem):
    copies = [pltpu.make_async_copy(s, t, sem.at[i]) for i, (s, t) in enumerate(zip(sources, targets))]
    for copy in copies:
        copy.start()
    return copies


def meta_scratch(meta):
    return [pltpu.SMEM(m.shape, jnp.int32) for m in meta] + [pltpu.SemaphoreType.DMA((len(meta),))]


def source_of(row, parents, table, lengths, block_len):
    parent = parents[row]
    length = lengths[parent]
    return length, table[length // block_len, parent]


def fetch_block(rounds, me, source, dest, part, rows, pool, arrived, target, sem):
    pool_dev = pool.shape[0]
    done = sum(bits for _, bits in rounds)
    moved = (source // pool_dev ^ me) & ((1 << done) - 1)

    @pl.when(moved == 0)
    def _():
        pltpu.make_async_copy(pool.at[source % pool_dev], target, sem).start()

    for (first, mask), ref in zip(channels_of(rounds), arrived):
        bits = dict(rounds)[first]

        @pl.when((moved >> first) == mask)
        def _():
            at = (dest >> (first + bits)) * rows + part
            pltpu.make_async_copy(ref.at[at], target, sem).start()


def begin_picks(rounds, now, rows, me, meta, pool, arrived, outs, sem):
    first, bits = now
    for mask in range(1, 1 << bits):
        out = outs[mask - 1]
        low = (me & ((1 << (first + bits)) - 1)) ^ (mask << first)

        def begin(at, carry):
            dest = (at // rows << (first + bits)) | low
            part = at % rows
            _, source = source_of(dest * rows + part, *meta, pool.shape[1])
            fetch_block(
                rounds, me, source, dest, part, rows, pool, arrived, out.at[at], sem.at[mask - 1, at]
            )
            return carry

        lax.fori_loop(0, out.shape[0], begin, 0)


def end_picks(pool, outs, sem):
    for index, out in enumerate(outs):

        def finish(at, carry):
            pltpu.make_async_copy(pool.at[0], out.at[at], sem.at[index, at]).wait()
            return carry

        lax.fori_loop(0, out.shape[0], finish, 0)


def ask_kernel(query, out, wide):
    devices, rows = out.shape[:2]
    heads = query.shape[1] // HD
    for row in range(rows):
        for head in range(heads):
            wide[head : head + 1, :] = query[row : row + 1, head * HD : (head + 1) * HD].astype(f32)
        value = wide[...].astype(bf16)
        for device in range(devices):
            out[device, row] = value


def ask(queries, devices):
    rows, width = queries.shape
    heads = width // HD
    vmem = pl.BlockSpec(memory_space=pltpu.VMEM)
    return pl.pallas_call(
        ask_kernel,
        name="ask",
        in_specs=[vmem],
        out_specs=vmem,
        out_shape=jax.ShapeDtypeStruct((devices, rows, heads, HD), bf16),
        scratch_shapes=[pltpu.VMEM((heads, HD), f32)],
        compiler_params=pltpu.CompilerParams(vmem_limit_bytes=VMEM_LIMIT),
    )(queries)


def pick_shapes(now, devices, rows, pool):
    first, bits = now
    count = (devices >> (first + bits)) * rows
    partners = (1 << bits) - 1
    return [jax.ShapeDtypeStruct((count,) + pool.shape[1:], bf16)] * partners, (partners, count)


def pick_kernel(rounds, now, rows, channels, parents_in, table_in, lengths_in, pool, *refs):
    partners = (1 << now[1]) - 1
    arrived, refs = refs[:channels], refs[channels:]
    outs, (parents, table, lengths, meta_sem, sem) = refs[:partners], refs[partners:]
    meta = (parents, table, lengths)
    for copy in load_meta((parents_in, table_in, lengths_in), meta, meta_sem):
        copy.wait()
    begin_picks(rounds, now, rows, lax.axis_index("ctx"), meta, pool, arrived, outs, sem)
    end_picks(pool, outs, sem)


def pick(rounds, now, devices, rows, meta, pool, arrived):
    shapes, semaphores = pick_shapes(now, devices, rows, pool)
    vmem, hbm = pl.BlockSpec(memory_space=pltpu.VMEM), pl.BlockSpec(memory_space=pltpu.HBM)
    return pl.pallas_call(
        functools.partial(pick_kernel, rounds, now, rows, len(arrived)),
        name="pick",
        in_specs=[hbm] * 4 + [pl.BlockSpec(memory_space=pl.ANY)] * len(arrived),
        out_specs=[vmem] * len(shapes),
        out_shape=shapes,
        scratch_shapes=meta_scratch(meta) + [pltpu.SemaphoreType.DMA(semaphores)],
        compiler_params=pltpu.CompilerParams(vmem_limit_bytes=VMEM_LIMIT),
        cost_estimate=pl.CostEstimate(flops=0, bytes_accessed=1 << 22, transcendentals=0),
    )(*map(in_hbm, meta), in_hbm(pool), *arrived)


def place_kernel(rounds, rows, parents_in, table_in, lengths_in, fresh_in, new_kv, pool, *refs):
    channels = len(channels_of(rounds))
    arrived, (out, parents, table, lengths, fresh, meta_sem, sem) = refs[:channels], refs[channels:]
    me = lax.axis_index("ctx")
    pool_dev, block_len = pool.shape[:2]
    whole = pltpu.make_async_copy(pool, out, sem)
    whole.start()
    sources = (parents_in, table_in, lengths_in, fresh_in)
    for copy in load_meta(sources, (parents, table, lengths, fresh), meta_sem):
        copy.wait()
    whole.wait()
    for part in range(rows):
        row = me * rows + part
        length, source = source_of(row, parents, table, lengths, block_len)
        slot = fresh[row] - me * pool_dev
        fetch_block(rounds, me, source, me, part, rows, pool, arrived, out.at[slot], sem)
        pltpu.make_async_copy(pool.at[0], out.at[slot], sem).wait()
        offset = length % block_len

        def token(at, carry):
            @pl.when(at == offset)
            def _():
                out[slot, at] = new_kv[part]

            @pl.when(at > offset)
            def _():
                out[slot, at] = jnp.zeros(out.shape[2:], bf16)

            return carry

        lax.fori_loop(0, block_len, token, 0)


def place(rounds, rows, meta, new_kv, pool, arrived):
    vmem, hbm = pl.BlockSpec(memory_space=pltpu.VMEM), pl.BlockSpec(memory_space=pltpu.HBM)
    return pl.pallas_call(
        functools.partial(place_kernel, rounds, rows),
        name="place",
        in_specs=[hbm] * 4 + [vmem, hbm] + [pl.BlockSpec(memory_space=pl.ANY)] * len(arrived),
        out_specs=vmem,
        out_shape=jax.ShapeDtypeStruct(pool.shape, bf16),
        scratch_shapes=meta_scratch(meta) + [pltpu.SemaphoreType.DMA],
        compiler_params=pltpu.CompilerParams(vmem_limit_bytes=VMEM_LIMIT),
        cost_estimate=pl.CostEstimate(flops=0, bytes_accessed=4 * pool.size, transcendentals=0),
    )(*map(in_hbm, meta), new_kv, in_hbm(pool), *arrived)


def pieces(value):
    high = value.astype(bf16)
    rest = value - high.astype(f32)
    middle = rest.astype(bf16)
    low = (rest - middle.astype(f32)).astype(bf16)
    return high.astype(f32), middle.astype(f32), low.astype(f32)


def tiles(array):
    width = array.shape[-1]
    split = array.reshape(-1, 2, width // HD, HD).transpose(0, 2, 1, 3)
    return split.reshape(-1, HD)


def unpack_kernel(
    now,
    rows,
    block_len,
    parents_in,
    table_in,
    lengths_in,
    prefix,
    pool,
    new_kv,
    blocked,
    keys,
    values,
    bias,
    *refs,
):
    partners = (1 << now[1]) - 1
    chosen, refs = refs[:partners], refs[partners:]
    raw, wide, value_buffer, in_sem, tail_sem, out_sem, pick_sem, *refs = refs
    parents, table, lengths, meta_sem = refs
    requests = keys.shape[0]
    per = 2 * KVH
    size = raw.shape[1]
    tokens = size // per
    chunks = raw.shape[0] - 1
    old = tokens - CAP * block_len
    blocks = tokens // block_len
    me = lax.axis_index("ctx")
    metas = load_meta((parents_in, table_in, lengths_in), (parents, table, lengths), meta_sem)

    first, last = old * per, (old + rows) * per
    spans = [
        (pool.at[pl.ds(0, first)], 0, first),
        (new_kv, first, last - first),
        (pool.at[pl.ds(last, size - last)], last, size - last),
    ]
    tails = [
        pltpu.make_async_copy(source, raw.at[chunks, pl.ds(at, count)], tail_sem.at[index])
        for index, (source, at, count) in enumerate(spans)
    ]

    def load(request, chunk):
        at = pl.multiple_of((request * chunks + chunk) * size, size)
        return pltpu.make_async_copy(prefix.at[pl.ds(at, size)], raw.at[chunk], in_sem.at[chunk])

    def store(request, chunk):
        span = pl.ds(pl.multiple_of(chunk * tokens, tokens), tokens)
        return pltpu.make_async_copy(
            value_buffer.at[:, span], values.at[request, :, span], out_sem.at[chunk]
        )

    def split(request, chunk):
        slot = chunk % 2
        wide[slot] = raw[chunk].astype(f32)
        span = pl.ds(pl.multiple_of(chunk * tokens, tokens), tokens)
        for head in range(KVH):
            keys[request, head, span, :] = wide[
                slot, pl.ds(2 * head, tokens, stride=per), :
            ].astype(bf16)
            value_buffer[head, span, :] = wide[
                slot, pl.ds(2 * head + 1, tokens, stride=per), :
            ].astype(bf16)
        store(request, chunk).start()

    for copy in tails:
        copy.start()
    for request in range(requests):
        for chunk in range(chunks):
            load(request, chunk).start()
        if request == 0:
            for copy in metas:
                copy.wait()
            meta = (parents, table, lengths)
            begin_picks([], now, rows, me, meta, blocked, [], chosen, pick_sem)
            position = lax.broadcasted_iota(jnp.int32, (1, tokens), 1)
            in_block, at_block = position % block_len, position // block_len

            def mask(row, carry):
                parent = parents[row]
                tail = lengths[parent]
                reach = jnp.zeros((1, tokens), jnp.int32)
                for depth in range(table.shape[0]):
                    block = table[depth, parent] - me * blocks
                    reach = jnp.where(at_block == block, tail - depth * block_len, reach)
                own = row - me * rows
                own = jnp.where((own >= 0) & (own < rows), own + old, -1)
                live = (in_block < reach) | (position == own)
                bias[pl.ds(row, 1), :] = jnp.where(live, 0.0, masked_score)
                return carry

            lax.fori_loop(0, bias.shape[0], mask, 0)
            for copy in tails:
                copy.wait()

        def step(chunk, carry):
            @pl.when(chunk < chunks)
            def _():
                load(request, chunk).wait()

            split(request, chunk)
            return carry

        lax.fori_loop(0, chunks + 1, step, 0)
        for chunk in range(chunks + 1):
            store(request, chunk).wait()
    end_picks(blocked, chosen, pick_sem)


def unpack(now, devices, meta, prefix_kv, pool, new_kv):
    rows = new_kv.shape[0]
    row_total = rows * devices
    requests, length = prefix_kv.shape[:2]
    blocks, block_len = pool.shape[:2]
    tokens = blocks * block_len
    chunks = length // tokens
    size = 2 * KVH * tokens
    whole = (KVH, length + tokens, HD)
    hbm, vmem = pl.BlockSpec(memory_space=pltpu.HBM), pl.BlockSpec(memory_space=pltpu.VMEM)
    arrays = tuple(map(tiles, (prefix_kv, pool, new_kv))) + (pool,)
    shapes, semaphores = pick_shapes(now, devices, rows, pool)
    return pl.pallas_call(
        functools.partial(unpack_kernel, now, rows, block_len),
        name="unpack",
        in_specs=[hbm] * 7,
        out_specs=[vmem, hbm] + [vmem] * (1 + len(shapes)),
        out_shape=[
            jax.ShapeDtypeStruct((requests,) + whole, bf16),
            pltpu.HBM((requests,) + whole, bf16),
            jax.ShapeDtypeStruct((row_total, tokens), f32),
        ]
        + shapes,
        scratch_shapes=[
            pltpu.VMEM((chunks + 1, size, HD), bf16),
            pltpu.VMEM((2, size, HD), f32),
            pltpu.VMEM(whole, bf16),
            pltpu.SemaphoreType.DMA((chunks,)),
            pltpu.SemaphoreType.DMA((3,)),
            pltpu.SemaphoreType.DMA((chunks + 1,)),
            pltpu.SemaphoreType.DMA(semaphores),
        ]
        + meta_scratch(meta),
        compiler_params=pltpu.CompilerParams(vmem_limit_bytes=VMEM_LIMIT),
        cost_estimate=pl.CostEstimate(
            flops=0, bytes_accessed=3 * prefix_kv.size, transcendentals=0
        ),
    )(*map(in_hbm, meta + arrays))


def attend_kernel(query, keys, values, bias, out, wide, stacks, value_buffer, sem):
    groups = HQ // KVH
    requests = keys.shape[0]
    targets = out.shape[0] // KVH
    beams = query.shape[0] // requests
    count = groups * beams
    share = count // targets
    tokens = bias.shape[1]
    length = keys.shape[2] - tokens
    factor = HD ** (-0.5) * math.log2(math.e)
    contract = (((1,), (1,)), ((), ()))
    lane = lax.broadcasted_iota(jnp.int32, (count, HD), 1)

    def load(request, head):
        return pltpu.make_async_copy(values.at[request, head], value_buffer.at[head], sem.at[head])

    for request in range(requests):
        for head in range(KVH):
            load(request, head).start()
        span = pl.ds(request * beams, beams)
        wide[...] = query[span].astype(f32).reshape(beams * HQ, HD)
        for head in range(HQ):
            stacks[head * beams : (head + 1) * beams, :] = wide[
                pl.ds(head, beams, stride=HQ), :
            ].astype(bf16)

        def one(head):
            stacked = stacks[pl.ds(pl.multiple_of(head * count, count), count), :]
            score = lax.dot_general(
                stacked, keys[request, head], contract, preferred_element_type=f32
            )
            tail = score[:, length:] + jnp.concatenate([bias[span, :]] * groups, axis=0)
            score = jnp.concatenate([score[:, :length], tail], axis=1)
            top = jnp.max(score, axis=1, keepdims=True)
            weight = jnp.exp2((score - top) * factor)
            total = jnp.sum(weight, axis=1, keepdims=True)
            result = jnp.dot(weight.astype(bf16), value_buffer[head], preferred_element_type=f32)
            packed = jnp.zeros((count, HD), f32)
            for at, term in enumerate(pieces(top) + pieces(total)):
                packed = jnp.where(lane == at, term, packed)
            if count < HD:
                packed = jnp.concatenate([packed, jnp.zeros((HD - count, HD), f32)], axis=0)
            stats = packed.T
            for t in range(targets):
                at = head * targets + t
                out[at, request, :share, :] = result[t * share : (t + 1) * share].astype(bf16)
                mine = stats if t == 0 else pltpu.roll(stats, HD - t * share, 1)
                out[at, request, share : share + STAT_ROWS, :] = mine[:STAT_ROWS].astype(bf16)

        def some(step, carry):
            heads = [step * AT_ONCE + i for i in range(AT_ONCE)]
            for head in heads:
                load(request, head).wait()
            for head in heads:
                one(head)
            return carry

        lax.fori_loop(0, KVH // AT_ONCE, some, 0)


def attend(everyone, keys, values, bias, devices):
    requests, _, length, _ = keys.shape
    beams = everyone.shape[0] // requests
    groups = HQ // KVH
    targets = devices // KVH
    rows = groups // targets * beams + STAT_ROWS
    hbm, vmem = pl.BlockSpec(memory_space=pltpu.HBM), pl.BlockSpec(memory_space=pltpu.VMEM)
    return pl.pallas_call(
        attend_kernel,
        name="attend",
        in_specs=[vmem, vmem, hbm, vmem],
        out_specs=vmem,
        out_shape=jax.ShapeDtypeStruct((devices, requests, rows, HD), bf16),
        scratch_shapes=[
            pltpu.VMEM((beams * HQ, HD), f32),
            pltpu.VMEM((beams * HQ, HD), bf16),
            pltpu.VMEM((KVH, length, HD), bf16),
            pltpu.SemaphoreType.DMA((KVH,)),
        ],
        compiler_params=pltpu.CompilerParams(vmem_limit_bytes=VMEM_LIMIT),
        cost_estimate=pl.CostEstimate(
            flops=4 * everyone.size * length,
            bytes_accessed=4 * keys.size,
            transcendentals=everyone.size * length // HD,
        ),
    )(everyone, keys, in_hbm(values), bias)


def project_kernel(partial, weight, out, attended, scratch, buffer, sem):
    devices, requests, rows, _ = partial.shape
    share = rows - STAT_ROWS
    row_total = out.shape[0]
    beams = row_total // requests
    own = share // beams
    chunks = out.shape[1]
    parts = sem.shape[0]
    step = weight.shape[1] // parts
    factor = HD ** (-0.5) * math.log2(math.e)

    def load(part):
        lanes = pl.ds(part * step, step)
        return pltpu.make_async_copy(weight.at[:, lanes], buffer.at[part], sem.at[part])

    for part in range(parts):
        load(part).start()

    for r in range(requests):
        stats = [partial[p, r, share:rows, :].astype(f32) for p in range(devices)]
        tops = jnp.concatenate([s[0:1] + s[1:2] + s[2:3] for s in stats], axis=0)
        sums = jnp.concatenate([s[3:4] + s[4:5] + s[5:6] for s in stats], axis=0)
        scale = jnp.exp2((tops - jnp.max(tops, axis=0, keepdims=True)) * factor)
        scale = scale / jnp.sum(scale * sums, axis=0, keepdims=True)
        if devices < HD:
            scale = jnp.concatenate([scale, jnp.zeros((HD - devices, HD), f32)], axis=0)
        scale = scale.T
        total = jnp.zeros((share, HD), f32)
        for p in range(devices):
            total = total + partial[p, r, :share, :].astype(f32) * scale[:share, p : p + 1]
        for h in range(own):
            attended[r * beams : (r + 1) * beams, h * HD : (h + 1) * HD] = total[
                h * beams : (h + 1) * beams
            ].astype(bf16)

    for part in range(parts):
        load(part).wait()
        product = jnp.dot(attended[...], buffer[part], preferred_element_type=f32)
        for c in range(step // HD):
            scratch[pl.ds(part * (step // HD) + c, row_total, stride=chunks), :] = product[
                :, c * HD : (c + 1) * HD
            ]
    for row in range(row_total):
        out[row] = scratch[row * chunks : (row + 1) * chunks, :].astype(bf16)


def project(partial, weight, row_total):
    depth, width = weight.shape
    parts = max(1, width // 1024)
    return pl.pallas_call(
        project_kernel,
        name="project",
        in_specs=[
            pl.BlockSpec(memory_space=pltpu.VMEM),
            pl.BlockSpec(memory_space=pltpu.HBM),
        ],
        out_specs=pl.BlockSpec(memory_space=pltpu.VMEM),
        out_shape=jax.ShapeDtypeStruct((row_total, width // HD, HD), bf16),
        scratch_shapes=[
            pltpu.VMEM((row_total, depth), bf16),
            pltpu.VMEM((row_total * (width // HD), HD), f32),
            pltpu.VMEM((parts, depth, width // parts), bf16),
            pltpu.SemaphoreType.DMA((parts,)),
        ],
        compiler_params=pltpu.CompilerParams(vmem_limit_bytes=VMEM_LIMIT),
        cost_estimate=pl.CostEstimate(
            flops=2 * row_total * depth * width, bytes_accessed=2 * weight.size, transcendentals=0
        ),
    )(partial, in_hbm(weight))


def exchange(array):
    return lax.all_to_all(array, "ctx", split_axis=0, concat_axis=0, tiled=True)


def local(
    queries, new_kv, prefix_kv, pool, out_weight, parents, tail_table, fresh_slots, tail_lengths
):
    devices = lax.axis_size("ctx")
    rows = queries.shape[0]
    row_total = rows * devices
    width = out_weight.shape[1]
    rounds = rounds_of(devices)
    meta = (parents, tail_table.T, tail_lengths)

    def move(index, blocks):
        first, _ = rounds[index]
        return [
            lax.ppermute(block, "ctx", [(i, i ^ ((at + 1) << first)) for i in range(devices)])
            for at, block in enumerate(blocks)
        ]

    wide = ask(queries, devices)
    everyone = exchange(wide).reshape(row_total, HQ, HD)
    keys, values, bias, *blocks = unpack(
        rounds[0], devices, meta, prefix_kv, pool, new_kv
    )
    arrived = move(0, blocks)
    for index in range(1, len(rounds)):
        blocks = pick(rounds[:index], rounds[index], devices, rows, meta, pool, arrived)
        arrived = arrived + move(index, blocks)
    partial = attend(everyone, keys, values, bias, devices)
    partial = exchange(partial)
    products = project(partial, out_weight, row_total)
    products = exchange(products.reshape(devices, rows * (width // HD), HD))
    result = jnp.sum(products.astype(f32), axis=0).reshape(rows, width)
    new_pool = place(rounds, rows, meta + (fresh_slots,), new_kv, pool, arrived)
    return (result, new_pool)


def solution(mesh):
    in_specs = (
        P(("req", "ctx"), None),
        P(("req", "ctx"), None, None),
        P("req", "ctx", None, None),
        P(("req", "ctx"), None, None, None),
        P("ctx", None),
        P("req"),
        P("req", None),
        P("req"),
        P("req"),
    )
    out_specs = (P(("req", "ctx"), None), P(("req", "ctx"), None, None, None))
    return jax.shard_map(local, mesh=mesh, in_specs=in_specs, out_specs=out_specs, check_vma=False)
```

```python
import functools
import math

import jax
import jax.numpy as jnp
from jax import lax
from jax.experimental import pallas as pl
from jax.experimental.pallas import tpu as pltpu
from jax.sharding import PartitionSpec as P


HQ = 64
KVH = 8
HD = 128
CAP = 2

STAT_ROWS = 8
AT_ONCE = 8
VMEM_LIMIT = 20 << 20
masked_score = -1e30
bf16 = jnp.bfloat16
f32 = jnp.float32


def in_hbm(array):
    return pltpu.with_memory_space_constraint(array, pltpu.HBM)


def rounds_of(devices):
    total = devices.bit_length() - 1
    return [(0, 2)] + [(bit, 1) for bit in range(2, total)]


def channels_of(rounds):
    return [(first, mask) for first, bits in rounds for mask in range(1, 1 << bits)]


def load_meta(sources, targets, sem):
    copies = [pltpu.make_async_copy(s, t, sem.at[i]) for i, (s, t) in enumerate(zip(sources, targets))]
    for copy in copies:
        copy.start()
    return copies


def meta_scratch(meta):
    return [pltpu.SMEM(m.shape, jnp.int32) for m in meta] + [pltpu.SemaphoreType.DMA((len(meta),))]


def source_of(row, parents, table, lengths, block_len):
    parent = parents[row]
    length = lengths[parent]
    return length, table[length // block_len, parent]


def fetch_block(rounds, me, source, dest, part, rows, pool, arrived, target, sem):
    pool_dev = pool.shape[0]
    done = sum(bits for _, bits in rounds)
    moved = (source // pool_dev ^ me) & ((1 << done) - 1)

    @pl.when(moved == 0)
    def _():
        pltpu.make_async_copy(pool.at[source % pool_dev], target, sem).start()

    for (first, mask), ref in zip(channels_of(rounds), arrived):
        bits = dict(rounds)[first]

        @pl.when((moved >> first) == mask)
        def _():
            at = (dest >> (first + bits)) * rows + part
            pltpu.make_async_copy(ref.at[at], target, sem).start()


def begin_picks(rounds, now, rows, me, meta, pool, arrived, outs, sem):
    first, bits = now
    for mask in range(1, 1 << bits):
        out = outs[mask - 1]
        low = (me & ((1 << (first + bits)) - 1)) ^ (mask << first)

        def begin(at, carry):
            dest = (at // rows << (first + bits)) | low
            part = at % rows
            _, source = source_of(dest * rows + part, *meta, pool.shape[1])
            fetch_block(
                rounds, me, source, dest, part, rows, pool, arrived, out.at[at], sem.at[mask - 1, at]
            )
            return carry

        lax.fori_loop(0, out.shape[0], begin, 0)


def end_picks(pool, outs, sem):
    for index, out in enumerate(outs):

        def finish(at, carry):
            pltpu.make_async_copy(pool.at[0], out.at[at], sem.at[index, at]).wait()
            return carry

        lax.fori_loop(0, out.shape[0], finish, 0)


def ask_kernel(query, out, wide):
    devices, rows = out.shape[:2]
    heads = query.shape[1] // HD
    for row in range(rows):
        for head in range(heads):
            wide[head : head + 1, :] = query[row : row + 1, head * HD : (head + 1) * HD].astype(f32)
        value = wide[...].astype(bf16)
        for device in range(devices):
            out[device, row] = value


def ask(queries, devices):
    rows, width = queries.shape
    heads = width // HD
    vmem = pl.BlockSpec(memory_space=pltpu.VMEM)
    return pl.pallas_call(
        ask_kernel,
        name="ask",
        in_specs=[vmem],
        out_specs=vmem,
        out_shape=jax.ShapeDtypeStruct((devices, rows, heads, HD), bf16),
        scratch_shapes=[pltpu.VMEM((heads, HD), f32)],
        compiler_params=pltpu.CompilerParams(vmem_limit_bytes=VMEM_LIMIT),
    )(queries)


def pick_shapes(now, devices, rows, pool):
    first, bits = now
    count = (devices >> (first + bits)) * rows
    partners = (1 << bits) - 1
    return [jax.ShapeDtypeStruct((count,) + pool.shape[1:], bf16)] * partners, (partners, count)


def pick_kernel(rounds, now, rows, channels, parents_in, table_in, lengths_in, pool, *refs):
    partners = (1 << now[1]) - 1
    arrived, refs = refs[:channels], refs[channels:]
    outs, (parents, table, lengths, meta_sem, sem) = refs[:partners], refs[partners:]
    meta = (parents, table, lengths)
    for copy in load_meta((parents_in, table_in, lengths_in), meta, meta_sem):
        copy.wait()
    begin_picks(rounds, now, rows, lax.axis_index("ctx"), meta, pool, arrived, outs, sem)
    end_picks(pool, outs, sem)


def pick(rounds, now, devices, rows, meta, pool, arrived):
    shapes, semaphores = pick_shapes(now, devices, rows, pool)
    vmem, hbm = pl.BlockSpec(memory_space=pltpu.VMEM), pl.BlockSpec(memory_space=pltpu.HBM)
    return pl.pallas_call(
        functools.partial(pick_kernel, rounds, now, rows, len(arrived)),
        name="pick",
        in_specs=[hbm] * 4 + [pl.BlockSpec(memory_space=pl.ANY)] * len(arrived),
        out_specs=[vmem] * len(shapes),
        out_shape=shapes,
        scratch_shapes=meta_scratch(meta) + [pltpu.SemaphoreType.DMA(semaphores)],
        compiler_params=pltpu.CompilerParams(vmem_limit_bytes=VMEM_LIMIT),
        cost_estimate=pl.CostEstimate(flops=0, bytes_accessed=1 << 22, transcendentals=0),
    )(*map(in_hbm, meta), in_hbm(pool), *arrived)


def place_kernel(rounds, rows, parents_in, table_in, lengths_in, fresh_in, new_kv, pool, *refs):
    channels = len(channels_of(rounds))
    arrived, (out, parents, table, lengths, fresh, meta_sem, sem) = refs[:channels], refs[channels:]
    me = lax.axis_index("ctx")
    pool_dev, block_len = pool.shape[:2]
    whole = pltpu.make_async_copy(pool, out, sem)
    whole.start()
    sources = (parents_in, table_in, lengths_in, fresh_in)
    for copy in load_meta(sources, (parents, table, lengths, fresh), meta_sem):
        copy.wait()
    whole.wait()
    for part in range(rows):
        row = me * rows + part
        length, source = source_of(row, parents, table, lengths, block_len)
        slot = fresh[row] - me * pool_dev
        fetch_block(rounds, me, source, me, part, rows, pool, arrived, out.at[slot], sem)
        pltpu.make_async_copy(pool.at[0], out.at[slot], sem).wait()
        offset = length % block_len

        def token(at, carry):
            @pl.when(at == offset)
            def _():
                out[slot, at] = new_kv[part]

            @pl.when(at > offset)
            def _():
                out[slot, at] = jnp.zeros(out.shape[2:], bf16)

            return carry

        lax.fori_loop(0, block_len, token, 0)


def place(rounds, rows, meta, new_kv, pool, arrived):
    vmem, hbm = pl.BlockSpec(memory_space=pltpu.VMEM), pl.BlockSpec(memory_space=pltpu.HBM)
    return pl.pallas_call(
        functools.partial(place_kernel, rounds, rows),
        name="place",
        in_specs=[hbm] * 4 + [vmem, hbm] + [pl.BlockSpec(memory_space=pl.ANY)] * len(arrived),
        out_specs=vmem,
        out_shape=jax.ShapeDtypeStruct(pool.shape, bf16),
        scratch_shapes=meta_scratch(meta) + [pltpu.SemaphoreType.DMA],
        compiler_params=pltpu.CompilerParams(vmem_limit_bytes=VMEM_LIMIT),
        cost_estimate=pl.CostEstimate(flops=0, bytes_accessed=4 * pool.size, transcendentals=0),
    )(*map(in_hbm, meta), new_kv, in_hbm(pool), *arrived)


def pieces(value):
    high = value.astype(bf16)
    rest = value - high.astype(f32)
    middle = rest.astype(bf16)
    low = (rest - middle.astype(f32)).astype(bf16)
    return high.astype(f32), middle.astype(f32), low.astype(f32)


def tiles(array):
    width = array.shape[-1]
    split = array.reshape(-1, 2, width // HD, HD).transpose(0, 2, 1, 3)
    return split.reshape(-1, HD)


def unpack_kernel(
    now,
    rows,
    block_len,
    parents_in,
    table_in,
    lengths_in,
    prefix,
    pool,
    new_kv,
    blocked,
    keys,
    values,
    bias,
    *refs,
):
    partners = (1 << now[1]) - 1
    chosen, refs = refs[:partners], refs[partners:]
    raw, wide, value_buffer, in_sem, tail_sem, out_sem, *refs = refs
    buffers, refs = refs[:partners], refs[partners:]
    pick_sem, sent_sem, parents, table, lengths, meta_sem = refs
    requests = keys.shape[0]
    per = 2 * KVH
    size = raw.shape[1]
    tokens = size // per
    chunks = raw.shape[0] - 1
    old = tokens - CAP * block_len
    blocks = tokens // block_len
    me = lax.axis_index("ctx")
    metas = load_meta((parents_in, table_in, lengths_in), (parents, table, lengths), meta_sem)

    first, last = old * per, (old + rows) * per
    spans = [
        (pool.at[pl.ds(0, first)], 0, first),
        (new_kv, first, last - first),
        (pool.at[pl.ds(last, size - last)], last, size - last),
    ]
    tails = [
        pltpu.make_async_copy(source, raw.at[chunks, pl.ds(at, count)], tail_sem.at[index])
        for index, (source, at, count) in enumerate(spans)
    ]

    def load(request, chunk):
        at = pl.multiple_of((request * chunks + chunk) * size, size)
        return pltpu.make_async_copy(prefix.at[pl.ds(at, size)], raw.at[chunk], in_sem.at[chunk])

    def store(request, chunk):
        span = pl.ds(pl.multiple_of(chunk * tokens, tokens), tokens)
        return pltpu.make_async_copy(
            value_buffer.at[:, span], values.at[request, :, span], out_sem.at[chunk]
        )

    def split(request, chunk):
        slot = chunk % 2
        wide[slot] = raw[chunk].astype(f32)
        span = pl.ds(pl.multiple_of(chunk * tokens, tokens), tokens)
        for head in range(KVH):
            keys[request, head, span, :] = wide[
                slot, pl.ds(2 * head, tokens, stride=per), :
            ].astype(bf16)
            value_buffer[head, span, :] = wide[
                slot, pl.ds(2 * head + 1, tokens, stride=per), :
            ].astype(bf16)
        store(request, chunk).start()

    def mask(row, carry):
        parent = parents[row]
        tail = lengths[parent]
        reach = jnp.zeros((1, tokens), jnp.int32)
        for depth in range(table.shape[0]):
            block = table[depth, parent] - me * blocks
            reach = jnp.where(at_block == block, tail - depth * block_len, reach)
        own = row - me * rows
        own = jnp.where((own >= 0) & (own < rows), own + old, -1)
        live = (in_block < reach) | (position == own)
        bias[pl.ds(row, 1), :] = jnp.where(live, 0.0, masked_score)
        return carry

    position = lax.broadcasted_iota(jnp.int32, (1, tokens), 1)
    in_block, at_block = position % block_len, position // block_len
    for request in range(requests):
        for chunk in range(chunks):
            load(request, chunk).start()
        if request == 0:
            for copy in tails:
                copy.start()
            for copy in metas:
                copy.wait()
            meta = (parents, table, lengths)
            begin_picks([], now, rows, me, meta, blocked, [], buffers, pick_sem)

        def step(chunk, carry):
            load(request, chunk).wait()
            split(request, chunk)
            return carry

        lax.fori_loop(0, chunks, step, 0)
        if request == 0:
            for copy in tails:
                copy.wait()
        split(request, chunks)
        if request == 0:
            end_picks(blocked, buffers, pick_sem)
            sends = [
                pltpu.make_async_copy(source, target, sent_sem.at[index])
                for index, (source, target) in enumerate(zip(buffers, chosen))
            ]
            for copy in sends:
                copy.start()
            lax.fori_loop(0, bias.shape[0], mask, 0)
        for chunk in range(chunks + 1):
            store(request, chunk).wait()
    for copy in sends:
        copy.wait()


def unpack(now, devices, meta, prefix_kv, pool, new_kv):
    rows = new_kv.shape[0]
    row_total = rows * devices
    requests, length = prefix_kv.shape[:2]
    blocks, block_len = pool.shape[:2]
    tokens = blocks * block_len
    chunks = length // tokens
    size = 2 * KVH * tokens
    whole = (KVH, length + tokens, HD)
    hbm, vmem = pl.BlockSpec(memory_space=pltpu.HBM), pl.BlockSpec(memory_space=pltpu.VMEM)
    arrays = tuple(map(tiles, (prefix_kv, pool, new_kv))) + (pool,)
    shapes, semaphores = pick_shapes(now, devices, rows, pool)
    return pl.pallas_call(
        functools.partial(unpack_kernel, now, rows, block_len),
        name="unpack",
        in_specs=[hbm] * 7,
        out_specs=[vmem, hbm, vmem] + [hbm] * len(shapes),
        out_shape=[
            jax.ShapeDtypeStruct((requests,) + whole, bf16),
            pltpu.HBM((requests,) + whole, bf16),
            jax.ShapeDtypeStruct((row_total, tokens), f32),
        ]
        + [pltpu.HBM(shape.shape, shape.dtype) for shape in shapes],
        scratch_shapes=[
            pltpu.VMEM((chunks + 1, size, HD), bf16),
            pltpu.VMEM((2, size, HD), f32),
            pltpu.VMEM(whole, bf16),
            pltpu.SemaphoreType.DMA((chunks,)),
            pltpu.SemaphoreType.DMA((3,)),
            pltpu.SemaphoreType.DMA((chunks + 1,)),
        ]
        + [pltpu.VMEM(shape.shape, shape.dtype) for shape in shapes]
        + [pltpu.SemaphoreType.DMA(semaphores), pltpu.SemaphoreType.DMA((len(shapes),))]
        + meta_scratch(meta),
        compiler_params=pltpu.CompilerParams(vmem_limit_bytes=VMEM_LIMIT),
        cost_estimate=pl.CostEstimate(
            flops=0, bytes_accessed=3 * prefix_kv.size, transcendentals=0
        ),
    )(*map(in_hbm, meta + arrays))


def attend_kernel(query, keys, values, bias, out, wide, stacks, value_buffer, sem):
    groups = HQ // KVH
    requests = keys.shape[0]
    targets = out.shape[0] // KVH
    beams = query.shape[0] // requests
    count = groups * beams
    share = count // targets
    tokens = bias.shape[1]
    length = keys.shape[2] - tokens
    factor = HD ** (-0.5) * math.log2(math.e)
    contract = (((1,), (1,)), ((), ()))
    lane = lax.broadcasted_iota(jnp.int32, (count, HD), 1)
    stat_row = lax.broadcasted_iota(jnp.int32, (STAT_ROWS, HD), 0)

    def load(request, head):
        return pltpu.make_async_copy(values.at[request, head], value_buffer.at[head], sem.at[head])

    for request in range(requests):
        for head in range(KVH):
            load(request, head).start()
        span = pl.ds(request * beams, beams)
        stacks[...] = pltpu.einshape("bhd->hbd", query[span]).reshape(HQ * beams, HD)

        def scores(head):
            stacked = stacks[pl.ds(pl.multiple_of(head * count, count), count), :]
            score = lax.dot_general(
                stacked, keys[request, head], contract, preferred_element_type=f32
            )
            tail = score[:, length:] + jnp.concatenate([bias[span, :]] * groups, axis=0)
            return jnp.concatenate([score[:, :length], tail], axis=1)

        def softmax(score):
            top = jnp.max(score, axis=1, keepdims=True)
            weight = jnp.exp2((score - top) * factor)
            return weight.astype(bf16), top, jnp.sum(weight, axis=1, keepdims=True)

        def finish(head, weight, top, total):
            result = jnp.dot(weight, value_buffer[head], preferred_element_type=f32)
            packed = jnp.where(lane == 0, top, total)
            if count < HD:
                packed = jnp.concatenate([packed, jnp.zeros((HD - count, HD), f32)], axis=0)
            flat = packed.T
            stats = jnp.zeros((STAT_ROWS, HD), f32)
            for at, term in enumerate(pieces(flat[0:1]) + pieces(flat[1:2])):
                stats = jnp.where(stat_row == at, term, stats)
            for t in range(targets):
                at = head * targets + t
                out[at, request, :share, :] = result[t * share : (t + 1) * share].astype(bf16)
                mine = stats if t == 0 else pltpu.roll(stats, HD - t * share, 1)
                out[at, request, share : share + STAT_ROWS, :] = mine.astype(bf16)

        def some(step, carry):
            heads = [step * AT_ONCE + i for i in range(AT_ONCE)]
            ready = softmax(scores(heads[0]))
            for head in heads:
                load(request, head).wait()
            for index, head in enumerate(heads):
                ahead = scores(heads[index + 1]) if index + 1 < AT_ONCE else None
                finish(head, *ready)
                ready = ahead if ahead is None else softmax(ahead)
            return carry

        lax.fori_loop(0, KVH // AT_ONCE, some, 0)


def attend(everyone, keys, values, bias, devices):
    requests, _, length, _ = keys.shape
    beams = everyone.shape[0] // requests
    groups = HQ // KVH
    targets = devices // KVH
    rows = groups // targets * beams + STAT_ROWS
    hbm, vmem = pl.BlockSpec(memory_space=pltpu.HBM), pl.BlockSpec(memory_space=pltpu.VMEM)
    return pl.pallas_call(
        attend_kernel,
        name="attend",
        in_specs=[vmem, vmem, hbm, vmem],
        out_specs=vmem,
        out_shape=jax.ShapeDtypeStruct((devices, requests, rows, HD), bf16),
        scratch_shapes=[
            pltpu.VMEM((beams * HQ, HD), f32),
            pltpu.VMEM((beams * HQ, HD), bf16),
            pltpu.VMEM((KVH, length, HD), bf16),
            pltpu.SemaphoreType.DMA((KVH,)),
        ],
        compiler_params=pltpu.CompilerParams(vmem_limit_bytes=VMEM_LIMIT),
        cost_estimate=pl.CostEstimate(
            flops=4 * everyone.size * length,
            bytes_accessed=4 * keys.size,
            transcendentals=everyone.size * length // HD,
        ),
    )(everyone, keys, in_hbm(values), bias)


def project_kernel(partial, weight, out, attended, scratch, buffer, sem):
    devices, requests, rows, _ = partial.shape
    share = rows - STAT_ROWS
    row_total = out.shape[0]
    beams = row_total // requests
    own = share // beams
    chunks = out.shape[1]
    parts = sem.shape[0]
    step = weight.shape[1] // parts
    factor = HD ** (-0.5) * math.log2(math.e)

    def load(part):
        lanes = pl.ds(part * step, step)
        return pltpu.make_async_copy(weight.at[:, lanes], buffer.at[part], sem.at[part])

    for part in range(parts):
        load(part).start()

    for r in range(requests):
        stats = [partial[p, r, share:rows, :].astype(f32) for p in range(devices)]
        tops = jnp.concatenate([s[0:1] + s[1:2] + s[2:3] for s in stats], axis=0)
        sums = jnp.concatenate([s[3:4] + s[4:5] + s[5:6] for s in stats], axis=0)
        scale = jnp.exp2((tops - jnp.max(tops, axis=0, keepdims=True)) * factor)
        scale = scale / jnp.sum(scale * sums, axis=0, keepdims=True)
        if devices < HD:
            scale = jnp.concatenate([scale, jnp.zeros((HD - devices, HD), f32)], axis=0)
        scale = scale.T
        total = jnp.zeros((share, HD), f32)
        for p in range(devices):
            total = total + partial[p, r, :share, :].astype(f32) * scale[:share, p : p + 1]
        for h in range(own):
            attended[r * beams : (r + 1) * beams, h * HD : (h + 1) * HD] = total[
                h * beams : (h + 1) * beams
            ].astype(bf16)

    for part in range(parts):
        load(part).wait()
        product = jnp.dot(attended[...], buffer[part], preferred_element_type=f32)
        for c in range(step // HD):
            scratch[pl.ds(part * (step // HD) + c, row_total, stride=chunks), :] = product[
                :, c * HD : (c + 1) * HD
            ]
    for row in range(row_total):
        out[row] = scratch[row * chunks : (row + 1) * chunks, :].astype(bf16)


def project(partial, weight, row_total):
    depth, width = weight.shape
    parts = max(1, width // 1024)
    return pl.pallas_call(
        project_kernel,
        name="project",
        in_specs=[
            pl.BlockSpec(memory_space=pltpu.VMEM),
            pl.BlockSpec(memory_space=pltpu.HBM),
        ],
        out_specs=pl.BlockSpec(memory_space=pltpu.VMEM),
        out_shape=jax.ShapeDtypeStruct((row_total, width // HD, HD), bf16),
        scratch_shapes=[
            pltpu.VMEM((row_total, depth), bf16),
            pltpu.VMEM((row_total * (width // HD), HD), f32),
            pltpu.VMEM((parts, depth, width // parts), bf16),
            pltpu.SemaphoreType.DMA((parts,)),
        ],
        compiler_params=pltpu.CompilerParams(vmem_limit_bytes=VMEM_LIMIT),
        cost_estimate=pl.CostEstimate(
            flops=2 * row_total * depth * width, bytes_accessed=2 * weight.size, transcendentals=0
        ),
    )(partial, in_hbm(weight))


def exchange(array):
    return lax.all_to_all(array, "ctx", split_axis=0, concat_axis=0, tiled=True)


def local(
    queries, new_kv, prefix_kv, pool, out_weight, parents, tail_table, fresh_slots, tail_lengths
):
    devices = lax.axis_size("ctx")
    rows = queries.shape[0]
    row_total = rows * devices
    width = out_weight.shape[1]
    rounds = rounds_of(devices)
    meta = (parents, tail_table.T, tail_lengths)

    def move(index, blocks):
        first, _ = rounds[index]
        return [
            lax.ppermute(block, "ctx", [(i, i ^ ((at + 1) << first)) for i in range(devices)])
            for at, block in enumerate(blocks)
        ]

    wide = ask(queries, devices)
    everyone = exchange(wide).reshape(row_total, HQ, HD)
    keys, values, bias, *blocks = unpack(
        rounds[0], devices, meta, prefix_kv, pool, new_kv
    )
    arrived = move(0, blocks)
    for index in range(1, len(rounds)):
        blocks = pick(rounds[:index], rounds[index], devices, rows, meta, pool, arrived)
        arrived = arrived + move(index, blocks)
    partial = attend(everyone, keys, values, bias, devices)
    partial = exchange(partial)
    products = project(partial, out_weight, row_total)
    products = exchange(products.reshape(devices, rows * (width // HD), HD))
    result = jnp.sum(products.astype(f32), axis=0).reshape(rows, width)
    new_pool = place(rounds, rows, meta + (fresh_slots,), new_kv, pool, arrived)
    return (result, new_pool)


def solution(mesh):
    in_specs = (
        P(("req", "ctx"), None),
        P(("req", "ctx"), None, None),
        P("req", "ctx", None, None),
        P(("req", "ctx"), None, None, None),
        P("ctx", None),
        P("req"),
        P("req", None),
        P("req"),
        P("req"),
    )
    out_specs = (P(("req", "ctx"), None), P(("req", "ctx"), None, None, None))
    return jax.shard_map(local, mesh=mesh, in_specs=in_specs, out_specs=out_specs, check_vma=False)
```

```python
import functools
import math

import jax
import jax.numpy as jnp
from jax import lax
from jax.experimental import pallas as pl
from jax.experimental.pallas import tpu as pltpu
from jax.sharding import PartitionSpec as P


HQ = 64
KVH = 8
HD = 128
CAP = 2

STAT_ROWS = 8
PARTS = 8
WARM = 2
AT_ONCE = 8
VMEM_LIMIT = 20 << 20
masked_score = -1e30
bf16 = jnp.bfloat16
f32 = jnp.float32


def in_hbm(array):
    return pltpu.with_memory_space_constraint(array, pltpu.HBM)


def rounds_of(devices):
    total = devices.bit_length() - 1
    return [(0, 2)] + [(bit, 1) for bit in range(2, total)]


def channels_of(rounds):
    return [(first, mask) for first, bits in rounds for mask in range(1, 1 << bits)]


def load_meta(sources, targets, sem):
    copies = [pltpu.make_async_copy(s, t, sem.at[i]) for i, (s, t) in enumerate(zip(sources, targets))]
    for copy in copies:
        copy.start()
    return copies


def meta_scratch(meta):
    return [pltpu.SMEM(m.shape, jnp.int32) for m in meta] + [pltpu.SemaphoreType.DMA((len(meta),))]


def source_of(row, parents, table, lengths, block_len):
    parent = parents[row]
    length = lengths[parent]
    return length, table[length // block_len, parent]


def fetch_block(rounds, me, source, dest, part, rows, pool, arrived, target, sem):
    pool_dev = pool.shape[0]
    done = sum(bits for _, bits in rounds)
    moved = (source // pool_dev ^ me) & ((1 << done) - 1)

    @pl.when(moved == 0)
    def _():
        pltpu.make_async_copy(pool.at[source % pool_dev], target, sem).start()

    for (first, mask), ref in zip(channels_of(rounds), arrived):
        bits = dict(rounds)[first]

        @pl.when((moved >> first) == mask)
        def _():
            at = (dest >> (first + bits)) * rows + part
            pltpu.make_async_copy(ref.at[at], target, sem).start()


def begin_picks(rounds, now, rows, me, meta, pool, arrived, outs, sem):
    first, bits = now
    for mask in range(1, 1 << bits):
        out = outs[mask - 1]
        low = (me & ((1 << (first + bits)) - 1)) ^ (mask << first)

        def begin(at, carry):
            dest = (at // rows << (first + bits)) | low
            part = at % rows
            _, source = source_of(dest * rows + part, *meta, pool.shape[1])
            fetch_block(
                rounds, me, source, dest, part, rows, pool, arrived, out.at[at], sem.at[mask - 1, at]
            )
            return carry

        lax.fori_loop(0, out.shape[0], begin, 0)


def end_picks(pool, outs, sem):
    for index, out in enumerate(outs):

        def finish(at, carry):
            pltpu.make_async_copy(pool.at[0], out.at[at], sem.at[index, at]).wait()
            return carry

        lax.fori_loop(0, out.shape[0], finish, 0)


def ask_kernel(query, out, wide):
    devices, rows = out.shape[:2]
    heads = query.shape[1] // HD
    for row in range(rows):
        for head in range(heads):
            wide[head : head + 1, :] = query[row : row + 1, head * HD : (head + 1) * HD].astype(f32)
        value = wide[...].astype(bf16)
        for device in range(devices):
            out[device, row] = value


def ask(queries, devices):
    rows, width = queries.shape
    heads = width // HD
    vmem = pl.BlockSpec(memory_space=pltpu.VMEM)
    return pl.pallas_call(
        ask_kernel,
        name="ask",
        in_specs=[vmem],
        out_specs=vmem,
        out_shape=jax.ShapeDtypeStruct((devices, rows, heads, HD), bf16),
        scratch_shapes=[pltpu.VMEM((heads, HD), f32)],
        compiler_params=pltpu.CompilerParams(vmem_limit_bytes=VMEM_LIMIT),
    )(queries)


def pick_shapes(now, devices, rows, pool):
    first, bits = now
    count = (devices >> (first + bits)) * rows
    partners = (1 << bits) - 1
    return [jax.ShapeDtypeStruct((count,) + pool.shape[1:], bf16)] * partners, (partners, count)


def pick_kernel(rounds, now, rows, channels, parents_in, table_in, lengths_in, pool, *refs):
    partners = (1 << now[1]) - 1
    arrived, refs = refs[:channels], refs[channels:]
    outs, (parents, table, lengths, meta_sem, sem) = refs[:partners], refs[partners:]
    meta = (parents, table, lengths)
    for copy in load_meta((parents_in, table_in, lengths_in), meta, meta_sem):
        copy.wait()
    begin_picks(rounds, now, rows, lax.axis_index("ctx"), meta, pool, arrived, outs, sem)
    end_picks(pool, outs, sem)


def pick(rounds, now, devices, rows, meta, pool, arrived):
    shapes, semaphores = pick_shapes(now, devices, rows, pool)
    vmem, hbm = pl.BlockSpec(memory_space=pltpu.VMEM), pl.BlockSpec(memory_space=pltpu.HBM)
    return pl.pallas_call(
        functools.partial(pick_kernel, rounds, now, rows, len(arrived)),
        name="pick",
        in_specs=[hbm] * 4 + [pl.BlockSpec(memory_space=pl.ANY)] * len(arrived),
        out_specs=[vmem] * len(shapes),
        out_shape=shapes,
        scratch_shapes=meta_scratch(meta) + [pltpu.SemaphoreType.DMA(semaphores)],
        compiler_params=pltpu.CompilerParams(vmem_limit_bytes=VMEM_LIMIT),
        cost_estimate=pl.CostEstimate(flops=0, bytes_accessed=1 << 22, transcendentals=0),
    )(*map(in_hbm, meta), in_hbm(pool), *arrived)


def base_kernel(
    rounds, rows, parents_in, table_in, lengths_in, fresh_in, new_in, pool, *refs
):
    channels = len(channels_of(rounds)) - 1
    arrived, (whole, tail, mask, *refs) = refs[:channels], refs[channels:]
    old_blocks, new_kv, parents, table, lengths, fresh, meta_sem, sems = refs
    me = lax.axis_index("ctx")
    pool_dev, block_len = pool.shape[:2]
    old = pool_dev - CAP
    zero = jnp.zeros(mask.shape[3:], bf16)
    one = jnp.ones(mask.shape[3:], bf16)
    first = pltpu.make_async_copy(pool.at[pl.ds(0, old)], old_blocks, sems.at[0])
    last = pltpu.make_async_copy(pool.at[pl.ds(old, CAP)], tail, sems.at[1])
    token_copy = pltpu.make_async_copy(new_in, new_kv, sems.at[2])
    sources = (parents_in, table_in, lengths_in, fresh_in)
    metas = load_meta(sources, (parents, table, lengths, fresh), meta_sem)
    for copy in (first, last, token_copy):
        copy.start()
    mask[...] = jnp.zeros(mask.shape, bf16)
    for copy in metas:
        copy.wait()
    token_copy.wait()
    last.wait()
    first.wait()
    send = pltpu.make_async_copy(old_blocks, whole.at[pl.ds(0, old)], sems.at[0])
    send.start()
    bit = rounds[-1][0]
    for part in range(rows):
        row = me * rows + part
        length, source = source_of(row, parents, table, lengths, block_len)
        slot = fresh[row] - me * pool_dev - old
        fetch_block(
            rounds[:-1], me, source, me, part, rows, pool, arrived, tail.at[slot], sems.at[1]
        )
        pltpu.make_async_copy(pool.at[0], tail.at[slot], sems.at[1]).wait()
        offset = length % block_len
        awaited = (((source // pool_dev) ^ me) >> bit) & 1

        def token(at, carry):
            @pl.when((at < offset) & (awaited == 1))
            def _():
                mask[part, slot, at] = one

            @pl.when(at == offset)
            def _():
                tail[slot, at] = new_kv[part]

            @pl.when(at > offset)
            def _():
                tail[slot, at] = zero

            return carry

        lax.fori_loop(0, block_len, token, 0)
    send.wait()


def base(rounds, rows, meta, new_kv, pool, arrived):
    vmem, hbm = pl.BlockSpec(memory_space=pltpu.VMEM), pl.BlockSpec(memory_space=pltpu.HBM)
    block = pool.shape[1:]
    return pl.pallas_call(
        functools.partial(base_kernel, rounds, rows),
        name="base",
        in_specs=[hbm] * 6 + [pl.BlockSpec(memory_space=pl.ANY)] * len(arrived),
        out_specs=[hbm, vmem, vmem],
        out_shape=[
            pltpu.HBM(pool.shape, bf16),
            jax.ShapeDtypeStruct((CAP,) + block, bf16),
            jax.ShapeDtypeStruct((rows, CAP) + block, bf16),
        ],
        scratch_shapes=[
            pltpu.VMEM((pool.shape[0] - CAP,) + block, bf16),
            pltpu.VMEM(new_kv.shape, bf16),
        ]
        + meta_scratch(meta)
        + [pltpu.SemaphoreType.DMA((3,))],
        compiler_params=pltpu.CompilerParams(vmem_limit_bytes=VMEM_LIMIT),
        cost_estimate=pl.CostEstimate(flops=0, bytes_accessed=4 * pool.size, transcendentals=0),
    )(*map(in_hbm, meta + (new_kv, pool)), *arrived)


def place_kernel(whole, tail, mask, last, out, merged, sem):
    old = out.shape[0] - CAP
    block = tail[...]
    for part in range(mask.shape[0]):
        block = jnp.where(mask[part] != 0, last[part][None], block)
    merged[...] = block
    copy = pltpu.make_async_copy(merged, out.at[pl.ds(old, CAP)], sem)
    copy.start()
    copy.wait()


def place(whole, tail, mask, last):
    vmem, hbm = pl.BlockSpec(memory_space=pltpu.VMEM), pl.BlockSpec(memory_space=pltpu.HBM)
    return pl.pallas_call(
        place_kernel,
        name="place",
        in_specs=[hbm, vmem, vmem, vmem],
        out_specs=hbm,
        out_shape=pltpu.HBM(whole.shape, bf16),
        input_output_aliases={0: 0},
        scratch_shapes=[pltpu.VMEM(tail.shape, bf16), pltpu.SemaphoreType.DMA],
        compiler_params=pltpu.CompilerParams(vmem_limit_bytes=VMEM_LIMIT),
        cost_estimate=pl.CostEstimate(flops=0, bytes_accessed=4 * tail.size, transcendentals=0),
    )(whole, tail, mask, last)


def pieces(value):
    high = value.astype(bf16)
    rest = value - high.astype(f32)
    middle = rest.astype(bf16)
    low = (rest - middle.astype(f32)).astype(bf16)
    return high.astype(f32), middle.astype(f32), low.astype(f32)


def tiles(array):
    width = array.shape[-1]
    split = array.reshape(-1, 2, width // HD, HD).transpose(0, 2, 1, 3)
    return split.reshape(-1, HD)


def unpack_kernel(
    now,
    rows,
    block_len,
    parents_in,
    table_in,
    lengths_in,
    prefix,
    pool,
    new_kv,
    blocked,
    keys,
    values,
    bias,
    *refs,
):
    partners = (1 << now[1]) - 1
    chosen, refs = refs[:partners], refs[partners:]
    raw, wide, value_buffer, in_sem, tail_sem, out_sem, *refs = refs
    buffers, refs = refs[:partners], refs[partners:]
    pick_sem, sent_sem, parents, table, lengths, meta_sem = refs
    requests = keys.shape[0]
    per = 2 * KVH
    size = raw.shape[1]
    tokens = size // per
    chunks = raw.shape[0] - 1
    old = tokens - CAP * block_len
    blocks = tokens // block_len
    me = lax.axis_index("ctx")
    metas = load_meta((parents_in, table_in, lengths_in), (parents, table, lengths), meta_sem)

    first, last = old * per, (old + rows) * per
    spans = [
        (pool.at[pl.ds(0, first)], 0, first),
        (new_kv, first, last - first),
        (pool.at[pl.ds(last, size - last)], last, size - last),
    ]
    tails = [
        pltpu.make_async_copy(source, raw.at[chunks, pl.ds(at, count)], tail_sem.at[index])
        for index, (source, at, count) in enumerate(spans)
    ]

    def load(request, chunk):
        at = pl.multiple_of((request * chunks + chunk) * size, size)
        return pltpu.make_async_copy(prefix.at[pl.ds(at, size)], raw.at[chunk], in_sem.at[chunk])

    def store(request, chunk):
        span = pl.ds(pl.multiple_of(chunk * tokens, tokens), tokens)
        return pltpu.make_async_copy(
            value_buffer.at[:, span], values.at[request, :, span], out_sem.at[chunk]
        )

    def split(request, chunk):
        slot = chunk % 2
        wide[slot] = raw[chunk].astype(f32)
        span = pl.ds(pl.multiple_of(chunk * tokens, tokens), tokens)
        for head in range(KVH):
            keys[request, head, span, :] = wide[
                slot, pl.ds(2 * head, tokens, stride=per), :
            ].astype(bf16)
            value_buffer[head, span, :] = wide[
                slot, pl.ds(2 * head + 1, tokens, stride=per), :
            ].astype(bf16)
        store(request, chunk).start()

    def mask(row, carry):
        parent = parents[row]
        tail = lengths[parent]
        reach = jnp.zeros((1, tokens), jnp.int32)
        for depth in range(table.shape[0]):
            block = table[depth, parent] - me * blocks
            reach = jnp.where(at_block == block, tail - depth * block_len, reach)
        own = row - me * rows
        own = jnp.where((own >= 0) & (own < rows), own + old, -1)
        live = (in_block < reach) | (position == own)
        bias[pl.ds(row, 1), :] = jnp.where(live, 0.0, masked_score)
        return carry

    position = lax.broadcasted_iota(jnp.int32, (1, tokens), 1)
    in_block, at_block = position % block_len, position // block_len
    for request in range(requests):
        for chunk in range(chunks):
            load(request, chunk).start()
        if request == 0:
            for copy in tails:
                copy.start()
            for copy in metas:
                copy.wait()
            meta = (parents, table, lengths)
            begin_picks([], now, rows, me, meta, blocked, [], buffers, pick_sem)

        def step(chunk, carry):
            load(request, chunk).wait()
            split(request, chunk)
            return carry

        lax.fori_loop(0, chunks, step, 0)
        if request == 0:
            for copy in tails:
                copy.wait()
        split(request, chunks)
        if request == 0:
            end_picks(blocked, buffers, pick_sem)
            sends = [
                pltpu.make_async_copy(source, target, sent_sem.at[index])
                for index, (source, target) in enumerate(zip(buffers, chosen))
            ]
            for copy in sends:
                copy.start()
            lax.fori_loop(0, bias.shape[0], mask, 0)
        for chunk in range(chunks + 1):
            store(request, chunk).wait()
    for copy in sends:
        copy.wait()


def unpack(now, devices, meta, prefix_kv, pool, new_kv):
    rows = new_kv.shape[0]
    row_total = rows * devices
    requests, length = prefix_kv.shape[:2]
    blocks, block_len = pool.shape[:2]
    tokens = blocks * block_len
    chunks = length // tokens
    size = 2 * KVH * tokens
    whole = (KVH, length + tokens, HD)
    hbm, vmem = pl.BlockSpec(memory_space=pltpu.HBM), pl.BlockSpec(memory_space=pltpu.VMEM)
    arrays = tuple(map(tiles, (prefix_kv, pool, new_kv))) + (pool,)
    shapes, semaphores = pick_shapes(now, devices, rows, pool)
    return pl.pallas_call(
        functools.partial(unpack_kernel, now, rows, block_len),
        name="unpack",
        in_specs=[hbm] * 7,
        out_specs=[vmem, hbm, vmem] + [hbm] * len(shapes),
        out_shape=[
            jax.ShapeDtypeStruct((requests,) + whole, bf16),
            pltpu.HBM((requests,) + whole, bf16),
            jax.ShapeDtypeStruct((row_total, tokens), f32),
        ]
        + [pltpu.HBM(shape.shape, shape.dtype) for shape in shapes],
        scratch_shapes=[
            pltpu.VMEM((chunks + 1, size, HD), bf16),
            pltpu.VMEM((2, size, HD), f32),
            pltpu.VMEM(whole, bf16),
            pltpu.SemaphoreType.DMA((chunks,)),
            pltpu.SemaphoreType.DMA((3,)),
            pltpu.SemaphoreType.DMA((chunks + 1,)),
        ]
        + [pltpu.VMEM(shape.shape, shape.dtype) for shape in shapes]
        + [pltpu.SemaphoreType.DMA(semaphores), pltpu.SemaphoreType.DMA((len(shapes),))]
        + meta_scratch(meta),
        compiler_params=pltpu.CompilerParams(vmem_limit_bytes=VMEM_LIMIT),
        cost_estimate=pl.CostEstimate(
            flops=0, bytes_accessed=3 * prefix_kv.size, transcendentals=0
        ),
    )(*map(in_hbm, meta + arrays))


def attend_kernel(query, keys, values, bias, out, wide, stacks, value_buffer, sem):
    groups = HQ // KVH
    requests = keys.shape[0]
    targets = out.shape[0] // KVH
    beams = query.shape[0] // requests
    count = groups * beams
    share = count // targets
    tokens = bias.shape[1]
    length = keys.shape[2] - tokens
    factor = HD ** (-0.5) * math.log2(math.e)
    contract = (((1,), (1,)), ((), ()))
    lane = lax.broadcasted_iota(jnp.int32, (count, HD), 1)
    stat_row = lax.broadcasted_iota(jnp.int32, (STAT_ROWS, HD), 0)

    def load(request, head):
        return pltpu.make_async_copy(values.at[request, head], value_buffer.at[head], sem.at[head])

    for request in range(requests):
        for head in range(KVH):
            load(request, head).start()
        span = pl.ds(request * beams, beams)
        stacks[...] = pltpu.einshape("bhd->hbd", query[span]).reshape(HQ * beams, HD)

        def scores(head):
            stacked = stacks[pl.ds(pl.multiple_of(head * count, count), count), :]
            score = lax.dot_general(
                stacked, keys[request, head], contract, preferred_element_type=f32
            )
            tail = score[:, length:] + jnp.concatenate([bias[span, :]] * groups, axis=0)
            return jnp.concatenate([score[:, :length], tail], axis=1)

        def softmax(score):
            top = jnp.max(score, axis=1, keepdims=True)
            weight = jnp.exp2((score - top) * factor)
            return weight.astype(bf16), top, jnp.sum(weight, axis=1, keepdims=True)

        def finish(head, weight, top, total):
            result = jnp.dot(weight, value_buffer[head], preferred_element_type=f32)
            packed = jnp.where(lane == 0, top, total)
            if count < HD:
                packed = jnp.concatenate([packed, jnp.zeros((HD - count, HD), f32)], axis=0)
            flat = packed.T
            stats = jnp.zeros((STAT_ROWS, HD), f32)
            for at, term in enumerate(pieces(flat[0:1]) + pieces(flat[1:2])):
                stats = jnp.where(stat_row == at, term, stats)
            for t in range(targets):
                at = head * targets + t
                out[at, request, :share, :] = result[t * share : (t + 1) * share].astype(bf16)
                mine = stats if t == 0 else pltpu.roll(stats, HD - t * share, 1)
                out[at, request, share : share + STAT_ROWS, :] = mine.astype(bf16)

        def some(step, carry):
            heads = [step * AT_ONCE + i for i in range(AT_ONCE)]
            ready = softmax(scores(heads[0]))
            for head in heads:
                load(request, head).wait()
            for index, head in enumerate(heads):
                ahead = scores(heads[index + 1]) if index + 1 < AT_ONCE else None
                finish(head, *ready)
                ready = ahead if ahead is None else softmax(ahead)
            return carry

        lax.fori_loop(0, KVH // AT_ONCE, some, 0)


def attend(everyone, keys, values, bias, devices):
    requests, _, length, _ = keys.shape
    beams = everyone.shape[0] // requests
    groups = HQ // KVH
    targets = devices // KVH
    rows = groups // targets * beams + STAT_ROWS
    hbm, vmem = pl.BlockSpec(memory_space=pltpu.HBM), pl.BlockSpec(memory_space=pltpu.VMEM)
    return pl.pallas_call(
        attend_kernel,
        name="attend",
        in_specs=[vmem, vmem, hbm, vmem],
        out_specs=vmem,
        out_shape=jax.ShapeDtypeStruct((devices, requests, rows, HD), bf16),
        scratch_shapes=[
            pltpu.VMEM((beams * HQ, HD), f32),
            pltpu.VMEM((beams * HQ, HD), bf16),
            pltpu.VMEM((KVH, length, HD), bf16),
            pltpu.SemaphoreType.DMA((KVH,)),
        ],
        compiler_params=pltpu.CompilerParams(vmem_limit_bytes=VMEM_LIMIT),
        cost_estimate=pl.CostEstimate(
            flops=4 * everyone.size * length,
            bytes_accessed=4 * keys.size,
            transcendentals=everyone.size * length // HD,
        ),
    )(everyone, keys, in_hbm(values), bias)


def project_kernel(partial, warmed, weight, out, attended, scratch, buffer, sem):
    devices, requests, rows, _ = partial.shape
    share = rows - STAT_ROWS
    row_total = out.shape[0]
    beams = row_total // requests
    own = share // beams
    chunks = out.shape[1]
    ready = warmed.shape[0]
    step = warmed.shape[2]
    parts = ready + sem.shape[0]
    factor = HD ** (-0.5) * math.log2(math.e)

    def load(part):
        lanes = pl.ds(part * step, step)
        at = part - ready
        return pltpu.make_async_copy(weight.at[:, lanes], buffer.at[at], sem.at[at])

    for part in range(ready, parts):
        load(part).start()

    for r in range(requests):
        stats = [partial[p, r, share:rows, :].astype(f32) for p in range(devices)]
        tops = jnp.concatenate([s[0:1] + s[1:2] + s[2:3] for s in stats], axis=0)
        sums = jnp.concatenate([s[3:4] + s[4:5] + s[5:6] for s in stats], axis=0)
        scale = jnp.exp2((tops - jnp.max(tops, axis=0, keepdims=True)) * factor)
        scale = scale / jnp.sum(scale * sums, axis=0, keepdims=True)
        if devices < HD:
            scale = jnp.concatenate([scale, jnp.zeros((HD - devices, HD), f32)], axis=0)
        scale = scale.T
        total = jnp.zeros((share, HD), f32)
        for p in range(devices):
            total = total + partial[p, r, :share, :].astype(f32) * scale[:share, p : p + 1]
        for h in range(own):
            attended[r * beams : (r + 1) * beams, h * HD : (h + 1) * HD] = total[
                h * beams : (h + 1) * beams
            ].astype(bf16)

    for part in range(parts):
        if part >= ready:
            load(part).wait()
        block = warmed[part] if part < ready else buffer[part - ready]
        product = jnp.dot(attended[...], block, preferred_element_type=f32)
        for c in range(step // HD):
            scratch[pl.ds(part * (step // HD) + c, row_total, stride=chunks), :] = product[
                :, c * HD : (c + 1) * HD
            ]
    for row in range(row_total):
        out[row] = scratch[row * chunks : (row + 1) * chunks, :].astype(bf16)


def warm_kernel(weight, out, sem):
    parts, _, step = out.shape
    copies = [
        pltpu.make_async_copy(weight.at[:, pl.ds(i * step, step)], out.at[i], sem.at[i])
        for i in range(parts)
    ]
    for copy in copies:
        copy.start()
    for copy in copies:
        copy.wait()


def warm(weight):
    depth, width = weight.shape
    step = width // PARTS
    return pl.pallas_call(
        warm_kernel,
        name="warm",
        in_specs=[pl.BlockSpec(memory_space=pltpu.HBM)],
        out_specs=pl.BlockSpec(memory_space=pltpu.VMEM),
        out_shape=jax.ShapeDtypeStruct((WARM, depth, step), bf16),
        scratch_shapes=[pltpu.SemaphoreType.DMA((WARM,))],
        compiler_params=pltpu.CompilerParams(vmem_limit_bytes=VMEM_LIMIT),
        cost_estimate=pl.CostEstimate(
            flops=0, bytes_accessed=4 * WARM * depth * step, transcendentals=0
        ),
    )(in_hbm(weight))


def project(partial, warmed, weight, row_total):
    depth, width = weight.shape
    cold = PARTS - WARM
    vmem, hbm = pl.BlockSpec(memory_space=pltpu.VMEM), pl.BlockSpec(memory_space=pltpu.HBM)
    return pl.pallas_call(
        project_kernel,
        name="project",
        in_specs=[vmem, vmem, hbm],
        out_specs=vmem,
        out_shape=jax.ShapeDtypeStruct((row_total, width // HD, HD), bf16),
        scratch_shapes=[
            pltpu.VMEM((row_total, depth), bf16),
            pltpu.VMEM((row_total * (width // HD), HD), f32),
            pltpu.VMEM((cold, depth, width // PARTS), bf16),
            pltpu.SemaphoreType.DMA((cold,)),
        ],
        compiler_params=pltpu.CompilerParams(vmem_limit_bytes=VMEM_LIMIT),
        cost_estimate=pl.CostEstimate(
            flops=2 * row_total * depth * width, bytes_accessed=2 * weight.size, transcendentals=0
        ),
    )(partial, warmed, in_hbm(weight))


def exchange(array):
    return lax.all_to_all(array, "ctx", split_axis=0, concat_axis=0, tiled=True)


def local(
    queries, new_kv, prefix_kv, pool, out_weight, parents, tail_table, fresh_slots, tail_lengths
):
    devices = lax.axis_size("ctx")
    rows = queries.shape[0]
    row_total = rows * devices
    width = out_weight.shape[1]
    rounds = rounds_of(devices)
    meta = (parents, tail_table.T, tail_lengths)

    def move(index, blocks):
        first, _ = rounds[index]
        return [
            lax.ppermute(block, "ctx", [(i, i ^ ((at + 1) << first)) for i in range(devices)])
            for at, block in enumerate(blocks)
        ]

    wide = ask(queries, devices)
    everyone = exchange(wide).reshape(row_total, HQ, HD)
    keys, values, bias, *blocks = unpack(
        rounds[0], devices, meta, prefix_kv, pool, new_kv
    )
    arrived = move(0, blocks)
    for index in range(1, len(rounds)):
        blocks = pick(rounds[:index], rounds[index], devices, rows, meta, pool, arrived)
        arrived = arrived + move(index, blocks)
    partial = attend(everyone, keys, values, bias, devices)
    partial = exchange(partial)
    warmed = warm(out_weight)
    products = project(partial, warmed, out_weight, row_total)
    products = exchange(products.reshape(devices, rows * (width // HD), HD))
    result = jnp.sum(products.astype(f32), axis=0).reshape(rows, width)
    parts = base(rounds, rows, meta + (fresh_slots,), new_kv, pool, arrived[:-1])
    new_pool = place(*parts, arrived[-1])
    return (result, new_pool)


def solution(mesh):
    in_specs = (
        P(("req", "ctx"), None),
        P(("req", "ctx"), None, None),
        P("req", "ctx", None, None),
        P(("req", "ctx"), None, None, None),
        P("ctx", None),
        P("req"),
        P("req", None),
        P("req"),
        P("req"),
    )
    out_specs = (P(("req", "ctx"), None), P(("req", "ctx"), None, None, None))
    return jax.shard_map(local, mesh=mesh, in_specs=in_specs, out_specs=out_specs, check_vma=False)
```

```python
import functools
import math

import jax
import jax.numpy as jnp
from jax import lax
from jax.experimental import pallas as pl
from jax.experimental.pallas import tpu as pltpu
from jax.sharding import PartitionSpec as P


HQ = 64
KVH = 8
HD = 128
CAP = 2

STAT_ROWS = 8
PARTS = 8
WARM = 2
AT_ONCE = 8
VMEM_LIMIT = 20 << 20
masked_score = -1e30
bf16 = jnp.bfloat16
f32 = jnp.float32


def in_hbm(array):
    return pltpu.with_memory_space_constraint(array, pltpu.HBM)


def div(value, size):
    return value >> (size.bit_length() - 1) if size & (size - 1) == 0 else lax.div(value, size)


def rem(value, size):
    return value & (size - 1) if size & (size - 1) == 0 else lax.rem(value, size)


def each(count, body):
    if count <= 4:
        for at in range(count):
            body(at, 0)
    else:
        lax.fori_loop(0, count, body, 0)


def rounds_of(devices):
    total = devices.bit_length() - 1
    return [(0, 2)] + [(bit, 1) for bit in range(2, total)]


def channels_of(rounds):
    return [(first, mask) for first, bits in rounds for mask in range(1, 1 << bits)]


def load_meta(sources, targets, sem):
    copies = [pltpu.make_async_copy(s, t, sem.at[i]) for i, (s, t) in enumerate(zip(sources, targets))]
    for copy in copies:
        copy.start()
    return copies


def meta_scratch(meta):
    return [pltpu.SMEM(m.shape, jnp.int32) for m in meta] + [pltpu.SemaphoreType.DMA((len(meta),))]


def source_of(row, parents, table, lengths, block_len):
    parent = parents[row]
    length = lengths[parent]
    return length, table[div(length, block_len), parent]


def fetch_block(rounds, me, source, dest, part, rows, pool, arrived, target, sem):
    pool_dev = pool.shape[0]
    done = sum(bits for _, bits in rounds)
    moved = (div(source, pool_dev) ^ me) & ((1 << done) - 1)

    if not rounds:
        pltpu.make_async_copy(pool.at[rem(source, pool_dev)], target, sem).start()
        return

    @pl.when(moved == 0)
    def _():
        pltpu.make_async_copy(pool.at[rem(source, pool_dev)], target, sem).start()

    for (first, mask), ref in zip(channels_of(rounds), arrived):
        bits = dict(rounds)[first]

        @pl.when((moved >> first) == mask)
        def _():
            at = (dest >> (first + bits)) * rows + part
            pltpu.make_async_copy(ref.at[at], target, sem).start()


def begin_picks(rounds, now, rows, me, meta, pool, arrived, outs, sem):
    first, bits = now
    for mask in range(1, 1 << bits):
        out = outs[mask - 1]
        low = (me & ((1 << (first + bits)) - 1)) ^ (mask << first)

        def begin(at, carry):
            dest = (at << (first + bits)) | low if rows == 1 else (at // rows << (first + bits)) | low
            part = 0 if rows == 1 else at % rows
            _, source = source_of(dest * rows + part, *meta, pool.shape[1])
            fetch_block(
                rounds, me, source, dest, part, rows, pool, arrived, out.at[at], sem.at[mask - 1, at]
            )
            return carry

        each(out.shape[0], begin)


def end_picks(pool, outs, sem):
    for index, out in enumerate(outs):

        def finish(at, carry):
            pltpu.make_async_copy(pool.at[0], out.at[at], sem.at[index, at]).wait()
            return carry

        each(out.shape[0], finish)


def ask_kernel(query, out, wide):
    devices, rows = out.shape[:2]
    heads = query.shape[1] // HD
    for row in range(rows):
        for head in range(heads):
            wide[head : head + 1, :] = query[row : row + 1, head * HD : (head + 1) * HD].astype(f32)
        value = wide[...].astype(bf16)
        for device in range(devices):
            out[device, row] = value


def ask(queries, devices):
    rows, width = queries.shape
    heads = width // HD
    vmem = pl.BlockSpec(memory_space=pltpu.VMEM)
    return pl.pallas_call(
        ask_kernel,
        name="ask",
        in_specs=[vmem],
        out_specs=vmem,
        out_shape=jax.ShapeDtypeStruct((devices, rows, heads, HD), bf16),
        scratch_shapes=[pltpu.VMEM((heads, HD), f32)],
        compiler_params=pltpu.CompilerParams(vmem_limit_bytes=VMEM_LIMIT),
    )(queries)


def pick_shapes(now, devices, rows, pool):
    first, bits = now
    count = (devices >> (first + bits)) * rows
    partners = (1 << bits) - 1
    return [jax.ShapeDtypeStruct((count,) + pool.shape[1:], bf16)] * partners, (partners, count)


def pick_kernel(rounds, now, rows, channels, parents_in, table_in, lengths_in, pool, *refs):
    partners = (1 << now[1]) - 1
    arrived, refs = refs[:channels], refs[channels:]
    outs, (parents, table, lengths, meta_sem, sem) = refs[:partners], refs[partners:]
    meta = (parents, table, lengths)
    for copy in load_meta((parents_in, table_in, lengths_in), meta, meta_sem):
        copy.wait()
    begin_picks(rounds, now, rows, lax.axis_index("ctx"), meta, pool, arrived, outs, sem)
    end_picks(pool, outs, sem)


def pick(rounds, now, devices, rows, meta, pool, arrived):
    shapes, semaphores = pick_shapes(now, devices, rows, pool)
    vmem, hbm = pl.BlockSpec(memory_space=pltpu.VMEM), pl.BlockSpec(memory_space=pltpu.HBM)
    return pl.pallas_call(
        functools.partial(pick_kernel, rounds, now, rows, len(arrived)),
        name="pick",
        in_specs=[hbm] * 4 + [pl.BlockSpec(memory_space=pl.ANY)] * len(arrived),
        out_specs=[vmem] * len(shapes),
        out_shape=shapes,
        scratch_shapes=meta_scratch(meta) + [pltpu.SemaphoreType.DMA(semaphores)],
        compiler_params=pltpu.CompilerParams(vmem_limit_bytes=VMEM_LIMIT),
        cost_estimate=pl.CostEstimate(flops=0, bytes_accessed=1 << 22, transcendentals=0),
    )(*map(in_hbm, meta), in_hbm(pool), *arrived)


def base_kernel(
    rounds, rows, parents_in, table_in, lengths_in, fresh_in, new_in, pool, *refs
):
    channels = len(channels_of(rounds)) - 1
    arrived, (whole, tail, mask, *refs) = refs[:channels], refs[channels:]
    old_blocks, new_kv, parents, table, lengths, fresh, meta_sem, sems = refs
    me = lax.axis_index("ctx")
    pool_dev, block_len = pool.shape[:2]
    old = pool_dev - CAP
    zero = jnp.zeros(mask.shape[3:], bf16)
    one = jnp.ones(mask.shape[3:], bf16)
    first = pltpu.make_async_copy(pool.at[pl.ds(0, old)], old_blocks, sems.at[0])
    last = pltpu.make_async_copy(pool.at[pl.ds(old, CAP)], tail, sems.at[1])
    token_copy = pltpu.make_async_copy(new_in, new_kv, sems.at[2])
    sources = (parents_in, table_in, lengths_in, fresh_in)
    metas = load_meta(sources, (parents, table, lengths, fresh), meta_sem)
    for copy in (first, last, token_copy):
        copy.start()
    mask[...] = jnp.zeros(mask.shape, bf16)
    for copy in metas:
        copy.wait()
    token_copy.wait()
    last.wait()
    first.wait()
    send = pltpu.make_async_copy(old_blocks, whole.at[pl.ds(0, old)], sems.at[0])
    send.start()
    bit = rounds[-1][0]
    for part in range(rows):
        row = me * rows + part
        length, source = source_of(row, parents, table, lengths, block_len)
        slot = fresh[row] - me * pool_dev - old
        fetch_block(
            rounds[:-1], me, source, me, part, rows, pool, arrived, tail.at[slot], sems.at[1]
        )
        pltpu.make_async_copy(pool.at[0], tail.at[slot], sems.at[1]).wait()
        offset = rem(length, block_len)
        awaited = ((div(source, pool_dev) ^ me) >> bit) & 1

        def token(at, carry):
            @pl.when((at < offset) & (awaited == 1))
            def _():
                mask[part, slot, at] = one

            @pl.when(at == offset)
            def _():
                tail[slot, at] = new_kv[part]

            @pl.when(at > offset)
            def _():
                tail[slot, at] = zero

            return carry

        lax.fori_loop(0, block_len, token, 0)
    send.wait()


def base(rounds, rows, meta, new_kv, pool, arrived):
    vmem, hbm = pl.BlockSpec(memory_space=pltpu.VMEM), pl.BlockSpec(memory_space=pltpu.HBM)
    block = pool.shape[1:]
    return pl.pallas_call(
        functools.partial(base_kernel, rounds, rows),
        name="base",
        in_specs=[hbm] * 6 + [pl.BlockSpec(memory_space=pl.ANY)] * len(arrived),
        out_specs=[hbm, vmem, vmem],
        out_shape=[
            pltpu.HBM(pool.shape, bf16),
            jax.ShapeDtypeStruct((CAP,) + block, bf16),
            jax.ShapeDtypeStruct((rows, CAP) + block, bf16),
        ],
        scratch_shapes=[
            pltpu.VMEM((pool.shape[0] - CAP,) + block, bf16),
            pltpu.VMEM(new_kv.shape, bf16),
        ]
        + meta_scratch(meta)
        + [pltpu.SemaphoreType.DMA((3,))],
        compiler_params=pltpu.CompilerParams(vmem_limit_bytes=VMEM_LIMIT),
        cost_estimate=pl.CostEstimate(flops=0, bytes_accessed=4 * pool.size, transcendentals=0),
    )(*map(in_hbm, meta + (new_kv, pool)), *arrived)


def place_kernel(whole, tail, mask, last, products, out, result, merged, sem):
    old = out.shape[0] - CAP
    block = tail[...]
    for part in range(mask.shape[0]):
        block = jnp.where(mask[part] != 0, last[part][None], block)
    merged[...] = block
    copy = pltpu.make_async_copy(merged, out.at[pl.ds(old, CAP)], sem)
    copy.start()
    total = products[0].astype(f32)
    for device in range(1, products.shape[0]):
        total = total + products[device].astype(f32)
    result[...] = total
    copy.wait()


def place(whole, tail, mask, last, products):
    vmem, hbm = pl.BlockSpec(memory_space=pltpu.VMEM), pl.BlockSpec(memory_space=pltpu.HBM)
    return pl.pallas_call(
        place_kernel,
        name="place",
        in_specs=[hbm, vmem, vmem, vmem, vmem],
        out_specs=[hbm, vmem],
        out_shape=[
            pltpu.HBM(whole.shape, bf16),
            jax.ShapeDtypeStruct(products.shape[1:], f32),
        ],
        input_output_aliases={0: 0},
        scratch_shapes=[pltpu.VMEM(tail.shape, bf16), pltpu.SemaphoreType.DMA],
        compiler_params=pltpu.CompilerParams(vmem_limit_bytes=VMEM_LIMIT),
        cost_estimate=pl.CostEstimate(flops=0, bytes_accessed=4 * tail.size, transcendentals=0),
    )(whole, tail, mask, last, products)


def pieces(value):
    high = value.astype(bf16)
    rest = value - high.astype(f32)
    middle = rest.astype(bf16)
    low = (rest - middle.astype(f32)).astype(bf16)
    return high.astype(f32), middle.astype(f32), low.astype(f32)


def tiles(array):
    width = array.shape[-1]
    split = array.reshape(-1, 2, width // HD, HD).transpose(0, 2, 1, 3)
    return split.reshape(-1, HD)


def unpack_kernel(
    now,
    rows,
    block_len,
    parents_in,
    table_in,
    lengths_in,
    prefix,
    pool,
    new_kv,
    blocked,
    keys,
    values,
    bias,
    *refs,
):
    partners = (1 << now[1]) - 1
    chosen, refs = refs[:partners], refs[partners:]
    raw, wide, value_buffer, in_sem, tail_sem, out_sem, *refs = refs
    buffers, refs = refs[:partners], refs[partners:]
    pick_sem, sent_sem, parents, table, lengths, meta_sem = refs
    requests = keys.shape[0]
    per = 2 * KVH
    size = raw.shape[1]
    tokens = size // per
    chunks = raw.shape[0] - 1
    old = tokens - CAP * block_len
    blocks = tokens // block_len
    me = lax.axis_index("ctx")
    metas = load_meta((parents_in, table_in, lengths_in), (parents, table, lengths), meta_sem)

    first, last = old * per, (old + rows) * per
    spans = [
        (pool.at[pl.ds(0, first)], 0, first),
        (new_kv, first, last - first),
        (pool.at[pl.ds(last, size - last)], last, size - last),
    ]
    tails = [
        pltpu.make_async_copy(source, raw.at[chunks, pl.ds(at, count)], tail_sem.at[index])
        for index, (source, at, count) in enumerate(spans)
    ]

    def load(request, chunk):
        at = pl.multiple_of((request * chunks + chunk) * size, size)
        return pltpu.make_async_copy(prefix.at[pl.ds(at, size)], raw.at[chunk], in_sem.at[chunk])

    def store(request, chunk):
        span = pl.ds(pl.multiple_of(chunk * tokens, tokens), tokens)
        return pltpu.make_async_copy(
            value_buffer.at[:, span], values.at[request, :, span], out_sem.at[chunk]
        )

    def split(request, chunk):
        slot = chunk % 2
        wide[slot] = raw[chunk].astype(f32)
        span = pl.ds(pl.multiple_of(chunk * tokens, tokens), tokens)
        for head in range(KVH):
            keys[request, head, span, :] = wide[
                slot, pl.ds(2 * head, tokens, stride=per), :
            ].astype(bf16)
            value_buffer[head, span, :] = wide[
                slot, pl.ds(2 * head + 1, tokens, stride=per), :
            ].astype(bf16)
        store(request, chunk).start()

    def mask(row, carry):
        parent = parents[row]
        tail = lengths[parent]
        reach = jnp.zeros((1, tokens), jnp.int32)
        for depth in range(table.shape[0]):
            block = table[depth, parent] - me * blocks
            reach = jnp.where(at_block == block, tail - depth * block_len, reach)
        own = row - me * rows
        own = jnp.where((own >= 0) & (own < rows), own + old, -1)
        live = (in_block < reach) | (position == own)
        bias[pl.ds(row, 1), :] = jnp.where(live, 0.0, masked_score)
        return carry

    position = lax.broadcasted_iota(jnp.int32, (1, tokens), 1)
    in_block, at_block = rem(position, block_len), div(position, block_len)
    for request in range(requests):
        for chunk in range(chunks):
            load(request, chunk).start()
        if request == 0:
            for copy in tails:
                copy.start()
            for copy in metas:
                copy.wait()
            meta = (parents, table, lengths)
            begin_picks([], now, rows, me, meta, blocked, [], buffers, pick_sem)

        def step(chunk, carry):
            load(request, chunk).wait()
            split(request, chunk)
            return carry

        lax.fori_loop(0, chunks, step, 0)
        if request == 0:
            for copy in tails:
                copy.wait()
        split(request, chunks)
        if request == 0:
            end_picks(blocked, buffers, pick_sem)
            sends = [
                pltpu.make_async_copy(source, target, sent_sem.at[index])
                for index, (source, target) in enumerate(zip(buffers, chosen))
            ]
            for copy in sends:
                copy.start()
            lax.fori_loop(0, bias.shape[0], mask, 0)
        for chunk in range(chunks + 1):
            store(request, chunk).wait()
    for copy in sends:
        copy.wait()


def unpack(now, devices, meta, prefix_kv, pool, new_kv):
    rows = new_kv.shape[0]
    row_total = rows * devices
    requests, length = prefix_kv.shape[:2]
    blocks, block_len = pool.shape[:2]
    tokens = blocks * block_len
    chunks = length // tokens
    size = 2 * KVH * tokens
    whole = (KVH, length + tokens, HD)
    hbm, vmem = pl.BlockSpec(memory_space=pltpu.HBM), pl.BlockSpec(memory_space=pltpu.VMEM)
    arrays = tuple(map(tiles, (prefix_kv, pool, new_kv))) + (pool,)
    shapes, semaphores = pick_shapes(now, devices, rows, pool)
    return pl.pallas_call(
        functools.partial(unpack_kernel, now, rows, block_len),
        name="unpack",
        in_specs=[hbm] * 7,
        out_specs=[vmem, hbm, vmem] + [hbm] * len(shapes),
        out_shape=[
            jax.ShapeDtypeStruct((requests,) + whole, bf16),
            pltpu.HBM((requests,) + whole, bf16),
            jax.ShapeDtypeStruct((row_total, tokens), f32),
        ]
        + [pltpu.HBM(shape.shape, shape.dtype) for shape in shapes],
        scratch_shapes=[
            pltpu.VMEM((chunks + 1, size, HD), bf16),
            pltpu.VMEM((2, size, HD), f32),
            pltpu.VMEM(whole, bf16),
            pltpu.SemaphoreType.DMA((chunks,)),
            pltpu.SemaphoreType.DMA((3,)),
            pltpu.SemaphoreType.DMA((chunks + 1,)),
        ]
        + [pltpu.VMEM(shape.shape, shape.dtype) for shape in shapes]
        + [pltpu.SemaphoreType.DMA(semaphores), pltpu.SemaphoreType.DMA((len(shapes),))]
        + meta_scratch(meta),
        compiler_params=pltpu.CompilerParams(vmem_limit_bytes=VMEM_LIMIT),
        cost_estimate=pl.CostEstimate(
            flops=0, bytes_accessed=3 * prefix_kv.size, transcendentals=0
        ),
    )(*map(in_hbm, meta + arrays))


def attend_kernel(query, keys, values, bias, out, wide, stacks, value_buffer, sem):
    groups = HQ // KVH
    requests = keys.shape[0]
    targets = out.shape[0] // KVH
    beams = query.shape[0] // requests
    count = groups * beams
    share = count // targets
    tokens = bias.shape[1]
    length = keys.shape[2] - tokens
    factor = HD ** (-0.5) * math.log2(math.e)
    contract = (((1,), (1,)), ((), ()))
    lane = lax.broadcasted_iota(jnp.int32, (count, HD), 1)
    stat_row = lax.broadcasted_iota(jnp.int32, (STAT_ROWS, HD), 0)

    def load(request, head):
        return pltpu.make_async_copy(values.at[request, head], value_buffer.at[head], sem.at[head])

    for request in range(requests):
        for head in range(KVH):
            load(request, head).start()
        span = pl.ds(request * beams, beams)
        stacks[...] = pltpu.einshape("bhd->hbd", query[span]).reshape(HQ * beams, HD)

        def scores(head):
            stacked = stacks[pl.ds(pl.multiple_of(head * count, count), count), :]
            score = lax.dot_general(
                stacked, keys[request, head], contract, preferred_element_type=f32
            )
            tail = score[:, length:] + jnp.concatenate([bias[span, :]] * groups, axis=0)
            return jnp.concatenate([score[:, :length], tail], axis=1)

        def softmax(score):
            top = jnp.max(score, axis=1, keepdims=True)
            weight = jnp.exp2((score - top) * factor)
            return weight.astype(bf16), top, jnp.sum(weight, axis=1, keepdims=True)

        def finish(head, weight, top, total):
            result = jnp.dot(weight, value_buffer[head], preferred_element_type=f32)
            packed = jnp.where(lane == 0, top, total)
            if count < HD:
                packed = jnp.concatenate([packed, jnp.zeros((HD - count, HD), f32)], axis=0)
            flat = packed.T
            stats = jnp.zeros((STAT_ROWS, HD), f32)
            for at, term in enumerate(pieces(flat[0:1]) + pieces(flat[1:2])):
                stats = jnp.where(stat_row == at, term, stats)
            for t in range(targets):
                at = head * targets + t
                out[at, request, :share, :] = result[t * share : (t + 1) * share].astype(bf16)
                mine = stats if t == 0 else pltpu.roll(stats, HD - t * share, 1)
                out[at, request, share : share + STAT_ROWS, :] = mine.astype(bf16)

        def some(step, carry):
            heads = [step * AT_ONCE + i for i in range(AT_ONCE)]
            ready = softmax(scores(heads[0]))
            for head in heads:
                load(request, head).wait()
            for index, head in enumerate(heads):
                ahead = scores(heads[index + 1]) if index + 1 < AT_ONCE else None
                finish(head, *ready)
                ready = ahead if ahead is None else softmax(ahead)
            return carry

        lax.fori_loop(0, KVH // AT_ONCE, some, 0)


def attend(everyone, keys, values, bias, devices):
    requests, _, length, _ = keys.shape
    beams = everyone.shape[0] // requests
    groups = HQ // KVH
    targets = devices // KVH
    rows = groups // targets * beams + STAT_ROWS
    hbm, vmem = pl.BlockSpec(memory_space=pltpu.HBM), pl.BlockSpec(memory_space=pltpu.VMEM)
    return pl.pallas_call(
        attend_kernel,
        name="attend",
        in_specs=[vmem, vmem, hbm, vmem],
        out_specs=vmem,
        out_shape=jax.ShapeDtypeStruct((devices, requests, rows, HD), bf16),
        scratch_shapes=[
            pltpu.VMEM((beams * HQ, HD), f32),
            pltpu.VMEM((beams * HQ, HD), bf16),
            pltpu.VMEM((KVH, length, HD), bf16),
            pltpu.SemaphoreType.DMA((KVH,)),
        ],
        compiler_params=pltpu.CompilerParams(vmem_limit_bytes=VMEM_LIMIT),
        cost_estimate=pl.CostEstimate(
            flops=4 * everyone.size * length,
            bytes_accessed=4 * keys.size,
            transcendentals=everyone.size * length // HD,
        ),
    )(everyone, keys, in_hbm(values), bias)


def project_kernel(partial, warmed, weight, out, attended, scratch, buffer, sem):
    devices, requests, rows, _ = partial.shape
    share = rows - STAT_ROWS
    row_total = out.shape[0]
    beams = row_total // requests
    own = share // beams
    chunks = out.shape[1]
    ready = warmed.shape[0]
    step = warmed.shape[2]
    parts = ready + sem.shape[0]
    factor = HD ** (-0.5) * math.log2(math.e)

    def load(part):
        lanes = pl.ds(part * step, step)
        at = part - ready
        return pltpu.make_async_copy(weight.at[:, lanes], buffer.at[at], sem.at[at])

    for part in range(ready, parts):
        load(part).start()

    for r in range(requests):
        stats = [partial[p, r, share:rows, :].astype(f32) for p in range(devices)]
        tops = jnp.concatenate([s[0:1] + s[1:2] + s[2:3] for s in stats], axis=0)
        sums = jnp.concatenate([s[3:4] + s[4:5] + s[5:6] for s in stats], axis=0)
        scale = jnp.exp2((tops - jnp.max(tops, axis=0, keepdims=True)) * factor)
        scale = scale / jnp.sum(scale * sums, axis=0, keepdims=True)
        if devices < HD:
            scale = jnp.concatenate([scale, jnp.zeros((HD - devices, HD), f32)], axis=0)
        scale = scale.T
        total = jnp.zeros((share, HD), f32)
        for p in range(devices):
            total = total + partial[p, r, :share, :].astype(f32) * scale[:share, p : p + 1]
        for h in range(own):
            attended[r * beams : (r + 1) * beams, h * HD : (h + 1) * HD] = total[
                h * beams : (h + 1) * beams
            ].astype(bf16)

    for part in range(parts):
        if part >= ready:
            load(part).wait()
        block = warmed[part] if part < ready else buffer[part - ready]
        product = jnp.dot(attended[...], block, preferred_element_type=f32)
        for c in range(step // HD):
            scratch[pl.ds(part * (step // HD) + c, row_total, stride=chunks), :] = product[
                :, c * HD : (c + 1) * HD
            ]
    for row in range(row_total):
        out[row] = scratch[row * chunks : (row + 1) * chunks, :].astype(bf16)


def warm_kernel(weight, out, sem):
    parts, _, step = out.shape
    copies = [
        pltpu.make_async_copy(weight.at[:, pl.ds(i * step, step)], out.at[i], sem.at[i])
        for i in range(parts)
    ]
    for copy in copies:
        copy.start()
    for copy in copies:
        copy.wait()


def warm(weight):
    depth, width = weight.shape
    step = width // PARTS
    return pl.pallas_call(
        warm_kernel,
        name="warm",
        in_specs=[pl.BlockSpec(memory_space=pltpu.HBM)],
        out_specs=pl.BlockSpec(memory_space=pltpu.VMEM),
        out_shape=jax.ShapeDtypeStruct((WARM, depth, step), bf16),
        scratch_shapes=[pltpu.SemaphoreType.DMA((WARM,))],
        compiler_params=pltpu.CompilerParams(vmem_limit_bytes=VMEM_LIMIT),
        cost_estimate=pl.CostEstimate(
            flops=0, bytes_accessed=4 * WARM * depth * step, transcendentals=0
        ),
    )(in_hbm(weight))


def project(partial, warmed, weight, row_total):
    depth, width = weight.shape
    cold = PARTS - WARM
    vmem, hbm = pl.BlockSpec(memory_space=pltpu.VMEM), pl.BlockSpec(memory_space=pltpu.HBM)
    return pl.pallas_call(
        project_kernel,
        name="project",
        in_specs=[vmem, vmem, hbm],
        out_specs=vmem,
        out_shape=jax.ShapeDtypeStruct((row_total, width // HD, HD), bf16),
        scratch_shapes=[
            pltpu.VMEM((row_total, depth), bf16),
            pltpu.VMEM((row_total * (width // HD), HD), f32),
            pltpu.VMEM((cold, depth, width // PARTS), bf16),
            pltpu.SemaphoreType.DMA((cold,)),
        ],
        compiler_params=pltpu.CompilerParams(vmem_limit_bytes=VMEM_LIMIT),
        cost_estimate=pl.CostEstimate(
            flops=2 * row_total * depth * width, bytes_accessed=2 * weight.size, transcendentals=0
        ),
    )(partial, warmed, in_hbm(weight))


def exchange(array):
    return lax.all_to_all(array, "ctx", split_axis=0, concat_axis=0, tiled=True)


def local(
    queries, new_kv, prefix_kv, pool, out_weight, parents, tail_table, fresh_slots, tail_lengths
):
    devices = lax.axis_size("ctx")
    rows = queries.shape[0]
    row_total = rows * devices
    width = out_weight.shape[1]
    rounds = rounds_of(devices)
    meta = (parents, tail_table.T, tail_lengths)

    def move(index, blocks):
        first, _ = rounds[index]
        return [
            lax.ppermute(block, "ctx", [(i, i ^ ((at + 1) << first)) for i in range(devices)])
            for at, block in enumerate(blocks)
        ]

    wide = ask(queries, devices)
    everyone = exchange(wide).reshape(row_total, HQ, HD)
    keys, values, bias, *blocks = unpack(
        rounds[0], devices, meta, prefix_kv, pool, new_kv
    )
    arrived = move(0, blocks)
    for index in range(1, len(rounds)):
        blocks = pick(rounds[:index], rounds[index], devices, rows, meta, pool, arrived)
        arrived = arrived + move(index, blocks)
    partial = attend(everyone, keys, values, bias, devices)
    partial = exchange(partial)
    warmed = warm(out_weight)
    products = project(partial, warmed, out_weight, row_total)
    products = exchange(products.reshape(devices, rows * (width // HD), HD))
    parts = base(rounds, rows, meta + (fresh_slots,), new_kv, pool, arrived[:-1])
    new_pool, result = place(*parts, arrived[-1], products)
    return (result.reshape(rows, width), new_pool)


def solution(mesh):
    in_specs = (
        P(("req", "ctx"), None),
        P(("req", "ctx"), None, None),
        P("req", "ctx", None, None),
        P(("req", "ctx"), None, None, None),
        P("ctx", None),
        P("req"),
        P("req", None),
        P("req"),
        P("req"),
    )
    out_specs = (P(("req", "ctx"), None), P(("req", "ctx"), None, None, None))
    return jax.shard_map(local, mesh=mesh, in_specs=in_specs, out_specs=out_specs, check_vma=False)
```
